32 devices in a mesh: fsdp: 8 (over y, x, core), dp: 4 (over z).
Axes of the slice: x: 2, y: 2, z: 4, core: 2. Of those that a mesh axis runs over, the one named last changes fastest.
Arguments:
- inputs: bfloat16 [2, 32, 512, 1024], P(None, ('fsdp', 'dp')), may hold values from -6 to 6
- block_ids: int32 [2, 32, 512], P(None, ('fsdp', 'dp')), may hold values from 0 to 3, never falling along the last dimension, each value on 1 to 256 neighbouring positions
- routes: int32 [2, 32, 512, 8], P(None, ('fsdp', 'dp')), may hold values from 0 to 31, all different within a row; in each aligned block of 512 rows (0 to 511, 512 to 1023, ..., all dimensions but the last counted through in order) at most 144 rows name the same one
- out_grad: bfloat16 [2, 32, 512, 1024], P(None, ('fsdp', 'dp')), may hold values from -6 to 6
- norm_gain: bfloat16 [1024], P(('fsdp', 'dp')), may hold values from 0.5 to 1.5
- w_query: bfloat16 [1024, 1024], P(('fsdp', 'dp')), may hold values from -0.75 to 0.75
- key_weight: bfloat16 [1024, 512], P(('fsdp', 'dp')), may hold values from -0.75 to 0.75
- value_weight: bfloat16 [1024, 512], P(('fsdp', 'dp')), may hold values from -0.1875 to 0.1875
- w_output: bfloat16 [1024, 1024], P(('fsdp', 'dp')), may hold values from -2 to 2
- moe_gain: bfloat16 [1024], P(('fsdp', 'dp')), may hold values from 0.5 to 1.5
- w_router: bfloat16 [1024, 32], P(('fsdp', 'dp')), may hold values from -0.09375 to 0.09375
- w_gate: bfloat16 [32, 1024, 512], P('fsdp', 'dp'), may hold values from -0.1875 to 0.1875
- w_up: bfloat16 [32, 1024, 512], P('fsdp', 'dp'), may hold values from -0.1875 to 0.1875
- w_down: bfloat16 [32, 512, 1024], P('fsdp', 'dp'), may hold values from -4 to 4
Outputs:
- output: bfloat16 [2, 32, 512, 1024], P(None, ('fsdp', 'dp'))
- input_grad: float32 [2, 32, 512, 1024], P(None, ('fsdp', 'dp'))
- grad_norm_gain: float32 [1024], P(('fsdp', 'dp'))
- grad_w_query: float32 [1024, 1024], P(('fsdp', 'dp'))
- grad_w_key: float32 [1024, 512], P(('fsdp', 'dp'))
- grad_w_value: float32 [1024, 512], P(('fsdp', 'dp'))
- grad_w_output: float32 [1024, 1024], P(('fsdp', 'dp'))
- grad_moe_gain: float32 [1024], P(('fsdp', 'dp'))
- grad_w_router: float32 [1024, 32], P(('fsdp', 'dp'))
- grad_w_gate: float32 [32, 1024, 512], P('fsdp', 'dp')
- grad_w_up: float32 [32, 1024, 512], P('fsdp', 'dp')
- grad_w_down: float32 [32, 512, 1024], P('fsdp', 'dp')
The draws below stay inside these ranges and needn't reach their ends.
Inputs may be any that keep to these rules, and one draw needn't show every extreme that they name: `block_ids`: along each sequence the ids never fall; a run of equal ids holds 1 to 256 tokens. `routes`: each token names 8 different experts. Among the 512 tokens of one sequence no expert is named more than 144 times, and in every draw some expert is named exactly 144 times in some sequence.
All inputs are finite; a program needn't handle non-finite values.
Results may differ from the reference program's by a relative error of at most 0.017.
Values may be sent and summed in bfloat16 or wider, within the bound.
A program may use at most 320 MiB of HBM per device.

```python
import math
import jax
import jax.numpy as jnp
import numpy as np
from jax import lax

MODEL_WIDTH = 1024
QUERY_HEADS = 16
KEY_VALUE_HEADS = 8
HEAD_SIZE = 64
E = 32
F = 512
K = 8
BLOCK = 256
SEQ = 512
MB = 2
NSEQ = 32
CAP = 144


def block_scale(stream_key, shape, split, smallest, largest):
    factor_of = 1.0
    for position, parts in split:
        heights = jax.random.uniform(jax.random.fold_in(jax.random.fold_in(stream_key, 6), position), (parts,), jnp.float32, smallest / len(split), largest / len(split))
        factor_of = factor_of * jnp.repeat(jnp.exp(heights), shape[position] // parts).reshape((-1,) + (1,) * (len(shape) - 1 - position))
    return factor_of


def length_profile(number_of, total, bound, skew):
    loads = [(1 << 20) // math.isqrt(grade ** skew) + 1 for grade in range(2, number_of + 1)]
    rest, holding = total - bound - (number_of - 1), [1] * (number_of - 1)
    while rest > 0:
        free = [i for i in range(number_of - 1) if holding[i] < bound]
        whole, budget = sum([loads[i] for i in free]), rest
        for i in free:
            addition = min(bound - holding[i], max(1, budget * loads[i] // whole), rest)
            holding[i] = holding[i] + addition
            rest = rest - addition
    return np.array([bound] + holding)


def ragged_sizes(rng, number_of, total, most, skew):
    if number_of == 2:
        one = jax.random.randint(rng, (), max(1, total - most), min(most, total - 1) + 1)
        return jnp.stack([one, total - one])
    lengths = jnp.asarray(length_profile(number_of, total, most, skew), jnp.int32)
    couples = (number_of - 1) // 2
    source_of, taker = lengths[1:1 + 2 * couples:2], lengths[2:2 + 2 * couples:2]
    slack = jnp.minimum(source_of - 1, most - taker)
    moved = jax.random.randint(jax.random.fold_in(rng, 1), (couples,), 0, 1 << 20) % (slack + 1)
    lengths = lengths.at[1:1 + 2 * couples:2].set(source_of - moved).at[2:2 + 2 * couples:2].set(taker + moved)
    return lengths[jax.random.permutation(jax.random.fold_in(rng, 2), number_of)]


def assign_block(stream_key, own, number, rows, number_of, top, most, skew):
    sequence = jax.random.permutation(stream_key, number_of)
    crowded, common = shares(number_of, rows * top, most, skew, True), shares(number_of, rows * top, most, skew, False)
    places = jnp.arange(number_of)

    def named(lengths, turn):
        used = int((lengths > 0).sum())
        fixed = max(1, used // 4)
        moved = fixed + (places - fixed + turn * (used - fixed)) % max(1, number_of - fixed)
        return jnp.zeros((number_of,), jnp.int32).at[sequence[jnp.where(places < fixed, places, moved)]].set(jnp.asarray(lengths, jnp.int32))

    lengths = jnp.where(number % 4 == 0, named(crowded, number // 4), named(common, number - number // 4 - 1))
    mixed = jax.random.permutation(jax.random.fold_in(own, 3), number_of)
    source_of, receiver = mixed[0:number_of // 2 * 2:2], mixed[1:number_of // 2 * 2:2]
    margin = jnp.minimum(lengths[source_of] - 1, most - lengths[receiver]) // 2
    margin = jnp.where((source_of == sequence[0]) | (receiver == sequence[0]) | (lengths[receiver] == 0), 0, jnp.maximum(margin, 0))
    moved = jax.random.randint(jax.random.fold_in(own, 4), (number_of // 2,), 0, 1 << 20) % (margin + 1)
    lengths = lengths.at[source_of].add(-moved).at[receiver].add(moved)
    members = jnp.searchsorted(jnp.cumsum(lengths), jnp.arange(rows * top), side="right").astype(jnp.int32)
    listing = members.reshape(top, rows).T
    listing = listing[jax.random.permutation(jax.random.fold_in(own, 1), rows)]
    turn = jax.random.randint(jax.random.fold_in(own, 2), (rows, 1), 0, top)
    return jnp.take_along_axis(listing, (jnp.arange(top)[None, :] + turn) % top, axis=1)


def shares(amount, total, most, lean, full):
    portions = [(1 << 20) // math.isqrt(rank ** lean) + 1 for rank in range(1, amount + 1)]
    largest = most if full else min(most, max(-(-total // amount), total * portions[0] // sum(portions)))
    least = 1 if total - largest >= amount - 1 else 0
    holding, spare = [largest] + [least] * (amount - 1), total - largest - least * (amount - 1)
    while spare > 0:
        movable = [i for i in range(1, amount) if holding[i] < largest] or [i for i in range(1, amount) if holding[i] < most]
        mass, left = sum([portions[i] for i in movable]), spare
        for i in movable:
            more = min(most - holding[i], max(1, left * portions[i] // mass), spare)
            holding[i] = holding[i] + more
            spare = spare - more
    return np.array(holding)


def bell_draw(key, shape, deviation, limit, pieces=(), kind=jnp.bfloat16):
    entries = deviation * jax.random.normal(key, shape, jnp.float32)
    if pieces:
        entries = entries * block_scale(key, shape, pieces, -0.22, 0.18)
    return jnp.clip(entries, -limit, limit).astype(kind)


def setup_inputs(seed: int = 0) -> dict:
    arg_keys = jax.random.split(jax.random.key(seed), 15)
    inputs = bell_draw(arg_keys[0], (MB, NSEQ, SEQ, MODEL_WIDTH), 1.0, 6.0, ((1, 32),))
    block_ids = jax.vmap(lambda own: jnp.searchsorted(jnp.cumsum(ragged_sizes(own, 2 * SEQ // BLOCK, SEQ, BLOCK, 0)), jnp.arange(SEQ), side="right"))(jax.random.split(arg_keys[1], MB * NSEQ)).reshape((MB, NSEQ, SEQ)).astype(jnp.int32)
    routes_keys = jax.random.split(jax.random.fold_in(arg_keys[2], 1), MB * NSEQ * SEQ // SEQ)
    routes_turns = jax.random.permutation(jax.random.fold_in(arg_keys[2], 3), MB * NSEQ * SEQ // SEQ)
    routes = jax.vmap(lambda own, number: assign_block(jax.random.fold_in(arg_keys[2], 2), own, number, SEQ, E, K, CAP, 0))(routes_keys, routes_turns).reshape((MB, NSEQ, SEQ, K))
    out_grad = bell_draw(arg_keys[3], (MB, NSEQ, SEQ, MODEL_WIDTH), 1.0, 6.0, ((1, 32),))
    norm_gain = jnp.clip(1.0 + 0.1 * jax.random.normal(arg_keys[4], (MODEL_WIDTH,), jnp.float32), 0.5, 1.5).astype(jnp.bfloat16)
    w_query = bell_draw(arg_keys[5], (MODEL_WIDTH, QUERY_HEADS * HEAD_SIZE), (MODEL_WIDTH // 16) ** -0.5, 0.75, ((0, 32),))
    key_weight = bell_draw(arg_keys[6], (MODEL_WIDTH, KEY_VALUE_HEADS * HEAD_SIZE), (MODEL_WIDTH // 16) ** -0.5, 0.75, ((0, 32),))
    value_weight = bell_draw(arg_keys[7], (MODEL_WIDTH, KEY_VALUE_HEADS * HEAD_SIZE), MODEL_WIDTH ** -0.5, 0.1875, ((0, 32),))
    w_output = bell_draw(arg_keys[8], (QUERY_HEADS * HEAD_SIZE, MODEL_WIDTH), (QUERY_HEADS * HEAD_SIZE // 128) ** -0.5, 2.0, ((0, 32),))
    moe_gain = jnp.clip(1.0 + 0.1 * jax.random.normal(arg_keys[9], (MODEL_WIDTH,), jnp.float32), 0.5, 1.5).astype(jnp.bfloat16)
    w_router = bell_draw(arg_keys[10], (MODEL_WIDTH, E), (4 * MODEL_WIDTH) ** -0.5, 0.09375, ((0, 32),))
    w_gate = bell_draw(arg_keys[11], (E, MODEL_WIDTH, F), MODEL_WIDTH ** -0.5, 0.1875, ((0, 8), (1, 4)))
    w_up = bell_draw(arg_keys[12], (E, MODEL_WIDTH, F), MODEL_WIDTH ** -0.5, 0.1875, ((0, 8), (1, 4)))
    w_down = bell_draw(arg_keys[13], (E, F, MODEL_WIDTH), (max(1, F // 256)) ** -0.5, 4.0, ((0, 8), (1, 4)))
    return dict(inputs=inputs, block_ids=block_ids, routes=routes, out_grad=out_grad, norm_gain=norm_gain, w_query=w_query, key_weight=key_weight, value_weight=value_weight, w_output=w_output, moe_gain=moe_gain, w_router=w_router, w_gate=w_gate, w_up=w_up, w_down=w_down)


EPS = 1e-06
RESIDUAL_SCALE = 0.22
SCORE_SCALE = 0.015625
THETA = 10000.0
NEG_FILL = -1e+30
HIGH = lax.Precision.HIGHEST

@jax.custom_vjp
def lower_bound(v):
    return lax.optimization_barrier(v.astype(jnp.bfloat16)).astype(jnp.float32)

@jax.custom_vjp
def low_back(v):
    return v

def low_keep(v):
    return (lower_bound(v), None)

def low_pass(kept, grad):
    return (grad,)

def back_keep(v):
    return (v, None)

def back_low(kept, grad):
    return (lower_bound(grad),)
lower_bound.defvjp(low_keep, low_pass)
low_back.defvjp(back_keep, back_low)

def rope_tables(sequence_length, head_dim):
    half_dim = head_dim // 2
    inverse_freq = THETA ** (-(jnp.arange(half_dim, dtype=jnp.float32) * 2.0) / head_dim)
    angles = jnp.arange(sequence_length, dtype=jnp.float32)[:, None] * inverse_freq[None, :]
    cosine_table = jnp.concatenate([jnp.cos(angles), jnp.cos(angles)], axis=1)
    sine_table = jnp.concatenate([jnp.sin(angles), jnp.sin(angles)], axis=1)
    return (cosine_table[:, None, :], sine_table[:, None, :])

def apply_rotary(stack, cosine_table, sine_table):
    half_dim = stack.shape[-1] // 2
    turned = jnp.concatenate([-stack[..., half_dim:], stack[..., :half_dim]], axis=-1)
    return stack * cosine_table + turned * sine_table

def rms_scale(rows, gain):
    return rows * lax.rsqrt(lax.optimization_barrier(jnp.mean(rows * rows, axis=-1, keepdims=True)) + EPS) * gain

def route_gates(logits, picks):
    chosen = jnp.take_along_axis(logits, picks, axis=1)
    lifted = jnp.exp(chosen - lax.optimization_barrier(jnp.max(chosen, axis=1, keepdims=True)))
    return lifted / lax.optimization_barrier(jnp.sum(lifted, axis=1, keepdims=True))

def slot_layout(picks, experts, capacity):
    flat = picks.reshape(-1).astype(jnp.int32)
    onehot = (flat[:, None] == jnp.arange(experts, dtype=jnp.int32)[None, :]).astype(jnp.int32)
    before = jnp.cumsum(onehot, axis=0) - onehot
    rank = lax.optimization_barrier(jnp.sum(before * onehot, axis=1))
    slot = flat * capacity + rank
    route_of = jnp.zeros((experts * capacity,), jnp.int32).at[slot].set(jnp.arange(flat.shape[0], dtype=jnp.int32))
    filled = jnp.zeros((experts * capacity,), jnp.int32).at[slot].set(jnp.ones_like(slot))
    return (slot, route_of, filled)

def sequence_layer(rows, ids, picks, gain_one, w_query, key_weight, value_weight, w_output, gain_two, w_router, w_gate, w_up, w_down):
    sequence_length = rows.shape[0]
    cosine_table, sine_table = rope_tables(sequence_length, HEAD_SIZE)
    normed = lower_bound(rms_scale(rows, gain_one))
    query = low_back(jnp.dot(normed, w_query, precision=HIGH))
    key_rows = low_back(jnp.dot(normed, key_weight, precision=HIGH))
    value_rows = lower_bound(low_back(jnp.dot(normed, value_weight, precision=HIGH)))
    rotated_queries = lower_bound(apply_rotary(query.reshape(sequence_length, QUERY_HEADS, HEAD_SIZE), cosine_table, sine_table))
    rotated_keys = lower_bound(apply_rotary(key_rows.reshape(sequence_length, KEY_VALUE_HEADS, HEAD_SIZE), cosine_table, sine_table))
    visible = ids[None, :] <= ids[:, None]
    group_size = QUERY_HEADS // KEY_VALUE_HEADS
    grouped_queries = rotated_queries.reshape(sequence_length, KEY_VALUE_HEADS, group_size, HEAD_SIZE).transpose(1, 0, 2, 3)
    key_groups = rotated_keys.transpose(1, 0, 2)
    grouped_values = value_rows.reshape(sequence_length, KEY_VALUE_HEADS, HEAD_SIZE).transpose(1, 0, 2)

    def attend(operands):
        query_group, key_group, value_group = operands
        scores = low_back(SCORE_SCALE * jnp.einsum('sgd,td->gst', query_group, key_group, precision=HIGH))
        scores = jnp.where(visible[None], scores, NEG_FILL)
        lifted = jnp.exp(scores - lax.optimization_barrier(jnp.max(scores, axis=2, keepdims=True)))
        weights = lifted / lax.optimization_barrier(jnp.sum(lifted, axis=2, keepdims=True))
        return jnp.einsum('gst,td->sgd', lower_bound(weights), value_group, precision=HIGH)
    mixed = lax.map(jax.checkpoint(attend), (grouped_queries, key_groups, grouped_values))
    attended = lower_bound(low_back(mixed.transpose(1, 0, 2, 3).reshape(sequence_length, QUERY_HEADS * HEAD_SIZE)))
    branch = low_back(jnp.dot(attended, w_output, precision=HIGH))
    residual = rows + RESIDUAL_SCALE * branch
    moe_in = lower_bound(rms_scale(residual, gain_two))
    logits = low_back(jnp.dot(moe_in, w_router, precision=HIGH))
    gates = route_gates(logits, picks)
    slot, route_of, filled = slot_layout(picks, E, CAP)
    dispatch = low_back(jnp.where(filled[:, None] > 0, moe_in[route_of // K], 0.0)).reshape(E, CAP, MODEL_WIDTH)
    pre_gate = low_back(jnp.einsum('ecd,edf->ecf', dispatch, w_gate, precision=HIGH))
    pre_up = low_back(jnp.einsum('ecd,edf->ecf', dispatch, w_up, precision=HIGH))
    activation = lower_bound(jax.nn.silu(pre_gate) * pre_up)
    produced = lower_bound(low_back(jnp.einsum('ecf,efd->ecd', activation, w_down, precision=HIGH)))
    gathered = produced.reshape(E * CAP, MODEL_WIDTH)[slot].reshape(sequence_length, K, MODEL_WIDTH)
    moe_sum = lax.optimization_barrier(jnp.sum(gates[:, :, None] * gathered, axis=1))
    return residual + RESIDUAL_SCALE * moe_sum

def reference(inputs, block_ids, routes, out_grad, norm_gain, w_query, key_weight, value_weight, w_output, moe_gain, w_router, w_gate, w_up, w_down):
    count = MB * NSEQ
    per_group = math.gcd(count, max(1, 4096 // SEQ))
    groups = count // per_group
    rows_all = inputs.astype(jnp.float32).reshape(groups, per_group, SEQ, MODEL_WIDTH)
    ids_all = block_ids.reshape(groups, per_group, SEQ)
    picks_all = routes.reshape(groups, per_group, SEQ, K)
    grads_all = out_grad.astype(jnp.float32).reshape(groups, per_group, SEQ, MODEL_WIDTH)
    weights = tuple((weight.astype(jnp.float32) for weight in (norm_gain, w_query, key_weight, value_weight, w_output, moe_gain, w_router, w_gate, w_up, w_down)))

    def group_step(carry, operands):
        rows, ids, picks, cotangent = operands

        def forward(group_rows, group_weights):

            def one_sequence(seq_rows, seq_ids, seq_picks):
                return sequence_layer(seq_rows, seq_ids, seq_picks, *group_weights)
            return jax.vmap(jax.checkpoint(one_sequence))(group_rows, ids, picks)
        result, pullback = jax.vjp(forward, rows, weights)
        rows_grad, weight_grads = pullback(cotangent)
        carry = jax.tree.map(lambda running, term: running + term, carry, weight_grads)
        return (carry, (result.astype(jnp.bfloat16), rows_grad))
    start_sums = jax.tree.map(jnp.zeros_like, weights)
    totals, (results, row_grads) = lax.scan(group_step, start_sums, (rows_all, ids_all, picks_all, grads_all))
    return (results.reshape(MB, NSEQ, SEQ, MODEL_WIDTH), row_grads.reshape(MB, NSEQ, SEQ, MODEL_WIDTH), totals[0], totals[1], totals[2], totals[3], totals[4], totals[5], totals[6], totals[7], totals[8], totals[9])
```

```python
import functools

import jax
import jax.numpy as jnp
import numpy as np
from jax import lax
from jax.experimental import pallas as pl
from jax.experimental.pallas import tpu as pltpu
from jax.sharding import PartitionSpec as P

QUERY_HEADS = 16
KEY_VALUE_HEADS = 8
HEAD_SIZE = 64
CAP = 144
EPS = 1e-06
RESIDUAL_SCALE = 0.22
SCORE_SCALE = 0.015625
THETA = 10000.0
NEG_FILL = -1e30
LANES = 128

BF = jnp.bfloat16
F32 = jnp.float32
VMEM_LIMIT = 64 * 1024 * 1024 - 128 * 1024


def mm(a, b):
    return jnp.dot(a, b, preferred_element_type=F32)


def mm_nt(a, b):
    return lax.dot_general(a, b, (((1,), (1,)), ((), ())), preferred_element_type=F32)


def mm_tn(a, b):
    return lax.dot_general(a, b, (((0,), (0,)), ((), ())), preferred_element_type=F32)


def rope_tables(sequence_length):
    half = HEAD_SIZE // 2
    inverse = np.float32(THETA) ** (-(np.arange(half, dtype=np.float32) * 2.0) / HEAD_SIZE)
    angles = np.arange(sequence_length, dtype=np.float32)[:, None] * inverse.astype(np.float32)[None, :]
    cosine, sine = np.cos(angles), np.sin(angles)
    copies = LANES // HEAD_SIZE
    cosine = np.tile(np.concatenate([cosine, cosine], 1), (1, copies))
    sine = np.tile(np.concatenate([-sine, sine], 1), (1, copies))
    return cosine.astype(np.float32), sine.astype(np.float32)


def lane_iota(shape):
    return lax.broadcasted_iota(jnp.int32, shape, len(shape) - 1)


def turn(block, cosine, sine):
    half = HEAD_SIZE // 2
    lower = (lane_iota(block.shape) % HEAD_SIZE) < half
    partner = jnp.where(
        lower, pltpu.roll(block, LANES - half, 1), pltpu.roll(block, half, 1)
    )
    return block * cosine + partner * sine


def tile_ds(index, width):
    return pl.ds(pl.multiple_of(index * width, width), width)


def head_pair(block, place):
    lower = lane_iota(block.shape) < HEAD_SIZE
    moved = pltpu.roll(block, HEAD_SIZE, 1)
    zero = jnp.zeros_like(block)
    low, high = (block, moved) if place == 0 else (moved, block)
    return jnp.where(lower, low, zero), jnp.where(lower, zero, high)


def attention_forward_kernel(
    x_ref, w_ref, gain_one_ref, gain_two_ref, id_row_ref, id_col_ref, cos_ref, sin_ref, picks_ref,
    q_ref, k_ref, v_ref, att_ref, lse_ref, res_ref, pay_ref, gate_ref,
    normed_ref, bias_ref,
    *, q_width, kv_width, experts,
):
    rows, width = x_ref.shape
    x = x_ref[...].astype(F32)
    scale = lax.rsqrt(jnp.mean(x * x, axis=1, keepdims=True) + EPS)
    normed_ref[...] = (x * scale * gain_one_ref[...]).astype(BF)
    bias_ref[...] = jnp.where(id_col_ref[...] <= id_row_ref[...], 0.0, NEG_FILL)
    step = 256

    def project(out_ref, start, count, rotate):
        def body(j, carry):
            cols = pl.ds(pl.multiple_of(start + j * step, step), step)
            part = mm(normed_ref[...], w_ref[:, cols])
            if rotate:
                part = jnp.concatenate(
                    [
                        turn(part[:, i * LANES : (i + 1) * LANES], cos_ref[...], sin_ref[...])
                        for i in range(step // LANES)
                    ],
                    axis=1,
                )
            out_ref[:, tile_ds(j, step)] = part.astype(BF)
            return carry

        lax.fori_loop(0, count // step, body, 0)

    project(q_ref, 0, q_width, True)
    project(k_ref, q_width, kv_width, True)
    project(v_ref, q_width + kv_width, kv_width, False)

    def pair_body(j, carry):
        k_block = k_ref[:, tile_ds(j, LANES)].astype(F32)
        v_block = v_ref[:, tile_ds(j, LANES)].astype(F32)
        for place in range(2):
            keys = head_pair(k_block, place)
            vals = head_pair(v_block, place)
            group = 2 * j + place
            q_block = q_ref[:, tile_ds(group, LANES)]
            out = None
            for side in range(2):
                scores = mm_nt(keys[side].astype(BF), q_block) * SCORE_SCALE + bias_ref[...]
                highest = jnp.max(scores, axis=0, keepdims=True)
                lifted = jnp.exp(scores - highest)
                total = jnp.sum(lifted, axis=0, keepdims=True)
                low = (lifted * (1.0 / total)).astype(BF)
                lse_ref[pl.ds(2 * group + side, 1), :] = highest + jnp.log(total)
                part = mm_tn(vals[side].astype(BF), low)
                out = part if out is None else out + part
            att_ref[:, tile_ds(group, LANES)] = out.T.astype(BF)
        return carry

    lax.fori_loop(0, KEY_VALUE_HEADS // 2, pair_body, 0)

    start = q_width + 2 * kv_width

    def out_body(j, total):
        cols = pl.ds(pl.multiple_of(start + j * step, step), step)
        here = tile_ds(j, step)
        value = x_ref[:, here].astype(F32) + RESIDUAL_SCALE * mm(att_ref[...], w_ref[:, cols])
        res_ref[:, here] = value
        return total + jnp.sum(value * value, axis=1, keepdims=True)

    square = lax.fori_loop(0, width // step, out_body, jnp.zeros((rows, 1), F32))
    scale = lax.rsqrt(square * (1.0 / width) + EPS)
    pay_ref[:rows, :] = (res_ref[...] * scale * gain_two_ref[...]).astype(BF)
    logits = mm(pay_ref[:rows, :], w_ref[:, start + width :])
    lanes = lane_iota(logits.shape)
    chosen = lanes < 0
    for k in range(picks_ref.shape[1]):
        chosen = chosen | (picks_ref[:, k : k + 1] == lanes)
    masked = jnp.where(chosen, logits, NEG_FILL)
    lifted = jnp.where(chosen, jnp.exp(masked - jnp.max(masked, axis=1, keepdims=True)), 0.0)
    gates = lifted / jnp.sum(lifted, axis=1, keepdims=True)
    across = gates.T[:experts, :]
    gate_ref[...] = across
    high = across.astype(BF)
    pay_ref[rows:, :rows] = high
    pay_ref[rows:, rows:] = (across - high.astype(F32)).astype(BF)


def attention_forward(x, pack, gain_one, gain_two, ids, picks, tables, q_width, kv_width, experts):
    rows, width = x.shape
    out_shape = (
        jax.ShapeDtypeStruct((rows, q_width), BF),
        jax.ShapeDtypeStruct((rows, kv_width), BF),
        jax.ShapeDtypeStruct((rows, kv_width), BF),
        jax.ShapeDtypeStruct((rows, q_width), BF),
        jax.ShapeDtypeStruct((QUERY_HEADS, rows), F32),
        jax.ShapeDtypeStruct((rows, width), F32),
        jax.ShapeDtypeStruct((rows + experts, width), BF),
        jax.ShapeDtypeStruct((experts, rows), F32),
    )
    flops = 2 * rows * width * (q_width + 2 * kv_width + width) + 8 * QUERY_HEADS * rows * rows * 128
    return pl.pallas_call(
        functools.partial(
            attention_forward_kernel, q_width=q_width, kv_width=kv_width, experts=experts
        ),
        out_shape=out_shape,
        scratch_shapes=[pltpu.VMEM((rows, width), BF), pltpu.VMEM((rows, rows), F32)],
        compiler_params=pltpu.CompilerParams(vmem_limit_bytes=VMEM_LIMIT),
        cost_estimate=pl.CostEstimate(
            flops=flops, transcendentals=QUERY_HEADS * rows * rows, bytes_accessed=16 << 20
        ),
        name="attention_forward",
    )(x, pack, gain_one, gain_two, ids[None, :], ids[:, None], *tables, picks)


def slot_marks(sel_ref, gate_rows, upper_ref, local):
    picked = mm(sel_ref[...], gate_rows)
    rows = picked.shape[1] // 2
    gates = picked[:, :rows] + picked[:, rows:]
    used = gates != 0.0
    rank = mm(used.astype(F32).astype(BF), upper_ref[...])
    slots = jnp.where(used, rank, -1.0)
    places = lax.broadcasted_iota(jnp.int32, (CAP, rows), 0).astype(F32)
    hits = [places == slots[e : e + 1, :] for e in range(local)]
    return gates, hits


def fill_upper(upper_ref):
    rows = upper_ref.shape[0]
    upper = lax.broadcasted_iota(jnp.int32, (rows, rows), 0) < lane_iota((rows, rows))
    upper_ref[...] = jnp.where(upper, 1.0, 0.0).astype(BF)


def dispatch_kernel(sel_ref, pay_ref, grad_ref, *refs, local):
    rows_ref, slot_ref, upper_ref = refs[-3:]

    @pl.when(pl.program_id(0) == 0)
    def _():
        fill_upper(upper_ref)

    rows = grad_ref.shape[1]
    gates, hits = slot_marks(sel_ref, pay_ref[0, rows:, :], upper_ref, local)
    marks = jnp.concatenate([jnp.where(h, 1.0, 0.0).astype(BF) for h in hits], axis=0)
    column = jnp.concatenate(
        [
            jnp.sum(jnp.where(h, gates[e : e + 1, :], 0.0), axis=1, keepdims=True)
            for e, h in enumerate(hits)
        ],
        axis=0,
    )
    moved = mm(marks, pay_ref[0, :rows, :]).astype(BF)
    grads = (column * (RESIDUAL_SCALE * mm(marks, grad_ref[0]))).astype(BF)
    for e in range(local):
        rows_ref[e, 0, 0] = moved[e * CAP : (e + 1) * CAP]
        slot_ref[e, 0, 0] = grads[e * CAP : (e + 1) * CAP]


def dispatch(sel, pays, grads, place, places, local, carried):
    count, rows, width = grads.shape
    shape = jax.ShapeDtypeStruct((local, places, count, CAP, width), BF)
    out_spec = pl.BlockSpec((local, 1, 1, CAP, width), lambda s: (0, place, s, 0, 0))
    in_specs = [
        pl.BlockSpec(sel.shape, lambda s: (0, 0)),
        pl.BlockSpec((1,) + pays.shape[1:], lambda s: (s, 0, 0)),
        pl.BlockSpec((1, rows, width), lambda s: (s, 0, 0)),
    ]
    operands = [sel, pays, grads]
    aliases = {}
    if carried is not None:
        operands += list(carried)
        in_specs += [pl.BlockSpec(memory_space=pl.ANY)] * 2
        aliases = {3: 0, 4: 1}
    return pl.pallas_call(
        functools.partial(dispatch_kernel, local=local),
        out_shape=(shape, shape),
        grid=(count,),
        in_specs=in_specs,
        out_specs=(out_spec, out_spec),
        scratch_shapes=[pltpu.VMEM((rows, rows), BF)],
        input_output_aliases=aliases,
        compiler_params=pltpu.CompilerParams(vmem_limit_bytes=VMEM_LIMIT),
        cost_estimate=pl.CostEstimate(
            flops=4 * count * local * CAP * rows * width, transcendentals=0, bytes_accessed=20 << 20
        ),
        name="dispatch",
    )(*operands)


def expert_kernel(
    x_ref, s_ref, wg_ref, wu_ref, wd_ref,
    pr_ref, dg_ref, dot_ref, grad_ref,
    act_ref, both_ref, acc_in_ref, acc_down_ref,
    *, chunk, tile, last,
):
    rows, width = x_ref.shape[-2:]
    hidden = wg_ref.shape[-1]
    owners = grad_ref.shape[0]
    in_rows, down_rows = width // owners, hidden // owners
    step = pl.program_id(0)

    def chunk_body(c, carry):
        here = tile_ds(c, chunk)
        x = x_ref[0, 0, here, :]
        s = s_ref[0, 0, here, :]
        pre_gate = mm(x, wg_ref[0])
        pre_up = mm(x, wu_ref[0])
        act_grad = mm_nt(s, wd_ref[0])
        logistic = jax.nn.sigmoid(pre_gate)
        swish = pre_gate * logistic
        act = (swish * pre_up).astype(BF)
        gate_in = (
            act_grad * pre_up * logistic * (1.0 + pre_gate * (1.0 - logistic))
        ).astype(BF)
        up_in = (act_grad * swish).astype(BF)
        dot_ref[0, here, :] = jnp.sum(act.astype(F32) * act_grad, axis=1, keepdims=True)
        act_ref[here, :] = act
        both_ref[here, :hidden] = gate_in
        both_ref[here, hidden:] = up_in
        pr_ref[0, here, :] = mm(act, wd_ref[0]).astype(BF)
        dg_ref[0, here, :] = (mm_nt(gate_in, wg_ref[0]) + mm_nt(up_in, wu_ref[0])).astype(BF)
        return carry

    lax.fori_loop(0, rows // chunk, chunk_body, 0)

    def in_body(t, carry):
        here = tile_ds(t, tile)
        part = mm_tn(x_ref[0, 0, :, here], both_ref[...])

        @pl.when(step == 0)
        def _():
            acc_in_ref[here, :] = part

        if last > 1:

            @pl.when((step > 0) & (step < last))
            def _():
                acc_in_ref[here, :] = acc_in_ref[here, :] + part

        @pl.when(step == last)
        def _():
            total = (acc_in_ref[here, :] + part).astype(BF)
            for i in range(tile // in_rows):
                piece = total[i * in_rows : (i + 1) * in_rows]
                owner = t * (tile // in_rows) + i
                grad_ref[owner, :in_rows, :] = piece[:, :hidden]
                grad_ref[owner, in_rows : 2 * in_rows, :] = piece[:, hidden:]

        return carry

    lax.fori_loop(0, width // tile, in_body, 0)

    def down_body(t, carry):
        here = tile_ds(t, tile)
        part = mm_tn(act_ref[:, here], s_ref[0, 0])

        @pl.when(step == 0)
        def _():
            acc_down_ref[here, :] = part

        if last > 1:

            @pl.when((step > 0) & (step < last))
            def _():
                acc_down_ref[here, :] = acc_down_ref[here, :] + part

        @pl.when(step == last)
        def _():
            total = (acc_down_ref[here, :] + part).astype(BF)
            for i in range(tile // down_rows):
                piece = total[i * down_rows : (i + 1) * down_rows]
                owner = t * (tile // down_rows) + i
                for c in range(width // hidden):
                    first = 2 * in_rows + c * down_rows
                    grad_ref[owner, first : first + down_rows, :] = piece[
                        :, c * hidden : (c + 1) * hidden
                    ]

        return carry

    lax.fori_loop(0, hidden // tile, down_body, 0)


def expert(which, owners, rows_in, slot_grad, gate_w, up_w, down_w):
    local, micro, rows, width = rows_in.shape
    hidden = gate_w.shape[2]
    out_shape = (
        jax.ShapeDtypeStruct((micro, rows, width), BF),
        jax.ShapeDtypeStruct((micro, rows, width), BF),
        jax.ShapeDtypeStruct((micro, rows, 1), F32),
        jax.ShapeDtypeStruct((owners, 3 * width // owners, hidden), BF),
    )
    in_spec = pl.BlockSpec((1, 1, rows, width), lambda m: (which, m, 0, 0))
    weight = lambda shape: pl.BlockSpec((1,) + shape, lambda m: (which, 0, 0))
    row_spec = lambda last: pl.BlockSpec((1, rows, last), lambda m: (m, 0, 0))
    return pl.pallas_call(
        functools.partial(expert_kernel, chunk=rows // 3, tile=256, last=micro - 1),
        out_shape=out_shape,
        grid=(micro,),
        in_specs=[in_spec, in_spec, weight((width, hidden)), weight((width, hidden)), weight((hidden, width))],
        out_specs=(
            row_spec(width), row_spec(width), row_spec(1),
            pl.BlockSpec((owners, 3 * width // owners, hidden), lambda m: (0, 0, 0)),
        ),
        scratch_shapes=[
            pltpu.VMEM((rows, hidden), BF),
            pltpu.VMEM((rows, 2 * hidden), BF),
            pltpu.VMEM((width, 2 * hidden), F32),
            pltpu.VMEM((hidden, width), F32),
        ],
        compiler_params=pltpu.CompilerParams(vmem_limit_bytes=VMEM_LIMIT),
        cost_estimate=pl.CostEstimate(
            flops=18 * micro * rows * width * hidden, transcendentals=micro * rows * hidden,
            bytes_accessed=30 << 20,
        ),
        name="expert",
    )(rows_in, slot_grad, gate_w, up_w, down_w)


def combine_kernel(sel_ref, pay_ref, *refs, local, received):
    produced = refs[:local]
    returned = refs[local : 2 * local]
    dots = refs[2 * local : 3 * local]
    rest = refs[3 * local :]
    if received:
        other_ref, rest = rest[0], rest[1:]
    out_refs, upper_ref = rest[:-1], rest[-1]

    @pl.when(pl.program_id(0) == 0)
    def _():
        fill_upper(upper_ref)

    rows = upper_ref.shape[0]
    gates, hits = slot_marks(sel_ref, pay_ref[0], upper_ref, local)
    weighted = jnp.concatenate(
        [jnp.where(h, gates[e : e + 1, :], 0.0).astype(BF) for e, h in enumerate(hits)], axis=0
    )
    plain = jnp.concatenate([jnp.where(h, 1.0, 0.0).astype(BF) for h in hits], axis=0)
    made = jnp.concatenate([r[0, 0] for r in produced], axis=0)
    back = jnp.concatenate([r[0, 0] for r in returned], axis=0)
    out = mm_tn(weighted, made)
    grads = mm_tn(plain, back)
    pad = jnp.zeros((8 - local, rows), F32)
    dot_rows = jnp.concatenate(
        [
            jnp.sum(jnp.where(h, dots[e][0, 0], 0.0), axis=0, keepdims=True)
            for e, h in enumerate(hits)
        ]
        + ([pad] if local < 8 else []),
        axis=0,
    )
    high = dot_rows.astype(BF)
    low = (dot_rows - high.astype(F32)).astype(BF)
    tail = jnp.concatenate([mm_tn(sel_ref[...], high), mm_tn(sel_ref[...], low)], axis=1)
    if received:
        out = out + other_ref[0, :rows, :].astype(F32)
        grads = grads + other_ref[0, rows : 2 * rows, :].astype(F32)
        tail = tail + other_ref[0, 2 * rows :, :].astype(F32)
    def put(ref, at):
        ref[at, :rows, :] = out.astype(BF)
        ref[at, rows : 2 * rows, :] = grads.astype(BF)
        ref[at, 2 * rows :, :] = tail.astype(BF)

    if len(out_refs) == 1:
        put(out_refs[0], 0)
    else:
        for index, ref in enumerate(out_refs):
            pl.when(pl.program_id(0) == index)(functools.partial(put, ref, 0))


def combine(sel, pays, produced, returned, dots, micro, side, other):
    count, total_rows, width = pays.shape
    local = len(produced)
    experts = sel.shape[1]
    rows = total_rows - experts
    pick = lambda last: pl.BlockSpec((1, 1, CAP, last), lambda s: (micro, side * count + s, 0, 0))
    in_specs = [
        pl.BlockSpec(sel.shape, lambda s: (0, 0)),
        pl.BlockSpec((1, experts, width), lambda s: (s, rows // experts, 0)),
    ]
    in_specs += [pick(width)] * (2 * local) + [pick(1)] * local
    operands = [sel, pays, *produced, *returned, *dots]
    out_spec = pl.BlockSpec((1, 2 * rows + experts, width), lambda s: (s, 0, 0))
    out_shape = (jax.ShapeDtypeStruct((count, 2 * rows + experts, width), BF),)
    out_specs = (out_spec,)
    if other is not None:
        operands.append(other)
        in_specs.append(out_spec)
        out_shape = (jax.ShapeDtypeStruct((1, 2 * rows + experts, width), BF),) * count
        out_specs = (pl.BlockSpec((1, 2 * rows + experts, width), lambda s: (0, 0, 0)),) * count
    return pl.pallas_call(
        functools.partial(combine_kernel, local=local, received=other is not None),
        out_shape=out_shape,
        grid=(count,),
        in_specs=in_specs,
        out_specs=out_specs,
        scratch_shapes=[pltpu.VMEM((rows, rows), BF)],
        compiler_params=pltpu.CompilerParams(vmem_limit_bytes=VMEM_LIMIT),
        cost_estimate=pl.CostEstimate(
            flops=4 * count * local * CAP * rows * width, transcendentals=0, bytes_accessed=20 << 20
        ),
        name="combine",
    )(*operands)


def attention_backward_kernel(
    *refs, terms, q_width, kv_width, experts, carried,
):
    (
        x_ref, w_ref, gain_one_ref, gain_two_ref, id_row_ref, id_col_ref, cos_ref, sin_ref,
        grad_ref, q_ref, k_ref, v_ref, att_ref, lse_ref, res_ref, pay_ref, gate_ref,
    ) = refs[:17]
    term_refs = refs[17 : 17 + terms]
    rest = refs[17 + terms :]
    if carried:
        prior_ref, rest = rest[0], rest[1:]
    out_ref, in_grad_ref, pack_ref, bias_ref, wide_ref, att_grad_ref, qkv_grad_ref, branch_ref, normed_ref = rest
    rows, width = x_ref.shape
    step = 256
    start = q_width + 2 * kv_width

    def put(row_slice, cols, value):
        if carried:
            value = value + prior_ref[row_slice, cols].astype(F32)
        pack_ref[row_slice, cols] = value.astype(BF)

    def gathered(low, high):
        total = term_refs[0][low:high, :].astype(F32)
        for ref in term_refs[1:]:
            total = total + ref[low:high, :].astype(F32)
        return total

    residual = res_ref[...]
    out_ref[...] = (residual + RESIDUAL_SCALE * gathered(0, rows)).astype(BF)
    tail = gathered(2 * rows, 2 * rows + experts)
    weighted = tail[:, :rows] + tail[:, rows:]
    chosen = weighted - gate_ref[...] * jnp.sum(weighted, axis=0, keepdims=True)
    chosen = jnp.concatenate([chosen, jnp.zeros((LANES - experts, rows), F32)], axis=0)
    logit_grad = chosen.T.astype(BF)
    moe_grad = gathered(rows, 2 * rows) + mm_nt(logit_grad, w_ref[:, start + width :])
    last = mm_tn(pay_ref[:rows, :], logit_grad)
    scale = lax.rsqrt(jnp.mean(residual * residual, axis=1, keepdims=True) + EPS)
    gain_two_grad = jnp.sum(moe_grad * residual * scale, axis=0, keepdims=True)
    u = moe_grad * gain_two_ref[...]
    inner = jnp.sum(u * residual, axis=1, keepdims=True) * (1.0 / width)
    res_grad = grad_ref[...].astype(F32) + scale * u - residual * (scale * scale * scale * inner)
    in_grad_ref[...] = res_grad
    branch_ref[...] = (RESIDUAL_SCALE * res_grad).astype(BF)
    bias_ref[...] = jnp.where(id_col_ref[...] <= id_row_ref[...], 0.0, NEG_FILL)

    def branch_body(j, carry):
        here = tile_ds(j, step)
        att_grad_ref[:, here] = mm_nt(
            branch_ref[...], w_ref[here, start : start + width]
        ).astype(BF)
        part = mm_tn(att_ref[:, here], branch_ref[...])
        put(here, slice(start, start + width), part)
        return carry

    lax.fori_loop(0, q_width // step, branch_body, 0)

    lower = lane_iota((rows, LANES)) < HEAD_SIZE

    def pair_body(j, carry):
        k_block = k_ref[:, tile_ds(j, LANES)].astype(F32)
        v_block = v_ref[:, tile_ds(j, LANES)].astype(F32)
        k_sums, v_sums = [], []
        for place in range(2):
            keys = [h.astype(BF) for h in head_pair(k_block, place)]
            vals = [h.astype(BF) for h in head_pair(v_block, place)]
            group = 2 * j + place
            here = tile_ds(group, LANES)
            q_block = q_ref[:, here]
            g_block = att_grad_ref[:, here]
            q_out = None
            k_parts, v_parts = [], []
            for side in range(2):
                scores = mm_nt(keys[side], q_block) * SCORE_SCALE + bias_ref[...]
                probs = jnp.exp(scores - lse_ref[pl.ds(2 * group + side, 1), :])
                weight_grad = mm_nt(vals[side], g_block)
                v_parts.append(mm(probs.astype(BF), g_block))
                dots = jnp.sum(probs * weight_grad, axis=0, keepdims=True)
                score_grad = (probs * (weight_grad - dots)).astype(BF)
                k_parts.append(mm(score_grad, q_block))
                part = mm_tn(keys[side], score_grad)
                q_out = part if q_out is None else q_out + part
            q_turned = turn(q_out.T * SCORE_SCALE, cos_ref[...], -sin_ref[...])
            qkv_grad_ref[:, here] = q_turned.astype(BF)
            for parts, sums in ((k_parts, k_sums), (v_parts, v_sums)):
                mixed = jnp.where(lower, parts[0], parts[1])
                sums.append(mixed + pltpu.roll(mixed, HEAD_SIZE, 1))
        k_total = jnp.where(lower, k_sums[0], k_sums[1]) * SCORE_SCALE
        v_total = jnp.where(lower, v_sums[0], v_sums[1])
        k_here = pl.ds(pl.multiple_of(q_width + j * LANES, LANES), LANES)
        v_here = pl.ds(pl.multiple_of(q_width + kv_width + j * LANES, LANES), LANES)
        qkv_grad_ref[:, k_here] = turn(k_total, cos_ref[...], -sin_ref[...]).astype(BF)
        qkv_grad_ref[:, v_here] = v_total.astype(BF)
        return carry

    lax.fori_loop(0, KEY_VALUE_HEADS // 2, pair_body, 0)

    x = x_ref[...].astype(F32)
    scale = lax.rsqrt(jnp.mean(x * x, axis=1, keepdims=True) + EPS)
    normed_ref[...] = (x * scale * gain_one_ref[...]).astype(BF)

    def norm_body(j, carry):
        here = tile_ds(j, step)
        grad = mm_nt(qkv_grad_ref[...], w_ref[here, :start])
        put(here, slice(0, start), mm_tn(normed_ref[:, here], qkv_grad_ref[...]))
        wide_ref[:, here] = grad
        return carry

    lax.fori_loop(0, width // step, norm_body, 0)
    normed_grad = wide_ref[...]
    gain_one_grad = jnp.sum(normed_grad * x * scale, axis=0, keepdims=True)
    u = normed_grad * gain_one_ref[...]
    inner = jnp.sum(u * x, axis=1, keepdims=True) * (1.0 / width)
    in_grad_ref[...] = in_grad_ref[...] + scale * u - x * (scale * scale * scale * inner)
    lanes = lane_iota((width, LANES))
    one = jnp.broadcast_to(gain_one_grad, (LANES, width)).T
    two = jnp.broadcast_to(gain_two_grad, (LANES, width)).T
    last = jnp.where(lanes == experts, one, last)
    last = jnp.where(lanes == experts + 1, two, last)
    put(slice(0, width), slice(start + width, start + width + LANES), last)


def attention_backward(
    x, pack, gain_one, gain_two, ids, tables, grad, saved, terms, prior, q_width, kv_width, experts
):
    rows, width = x.shape
    operands = [x, pack, gain_one, gain_two, ids[None, :], ids[:, None], *tables, grad, *saved, *terms]
    if prior is not None:
        operands.append(prior)
    flops = 4 * rows * width * (q_width + 2 * kv_width + width) + 20 * QUERY_HEADS * rows * rows * 128
    return pl.pallas_call(
        functools.partial(
            attention_backward_kernel, terms=len(terms), q_width=q_width, kv_width=kv_width,
            experts=experts, carried=prior is not None,
        ),
        out_shape=(
            jax.ShapeDtypeStruct((rows, width), BF),
            jax.ShapeDtypeStruct((rows, width), F32),
            jax.ShapeDtypeStruct(pack.shape, BF),
        ),
        scratch_shapes=[
            pltpu.VMEM((rows, rows), F32),
            pltpu.VMEM((rows, width), F32),
            pltpu.VMEM((rows, q_width), BF),
            pltpu.VMEM((rows, q_width + 2 * kv_width), BF),
            pltpu.VMEM((rows, width), BF),
            pltpu.VMEM((rows, width), BF),
        ],
        compiler_params=pltpu.CompilerParams(vmem_limit_bytes=VMEM_LIMIT),
        cost_estimate=pl.CostEstimate(
            flops=flops, transcendentals=QUERY_HEADS * rows * rows, bytes_accessed=40 << 20
        ),
        name="attention_backward",
    )(*operands)


def swap(value, distance, size):
    return lax.ppermute(value, "fsdp", [(i, i ^ distance) for i in range(size)])


def local(
    inputs, block_ids, routes, out_grad, norm_gain, w_query, key_weight, value_weight, w_output,
    moe_gain, w_router, w_gate, w_up, w_down,
):
    micro, _, rows, width = inputs.shape
    experts = w_router.shape[1]
    held = w_gate.shape[0]
    hidden = w_gate.shape[2]
    q_width, kv_width = w_query.shape[1], key_weight.shape[1]
    owners = lax.axis_size("fsdp")
    parts = lax.axis_size("dp")
    chips = owners // 2
    tables = tuple(jnp.asarray(t) for t in rope_tables(rows))
    start = q_width + 2 * kv_width + width

    def gather_peers(value):
        mine = jnp.stack([value] + [swap(value, 2 * r, owners) for r in range(1, chips)])
        return mine, swap(mine, 1, owners)

    pieces = [
        w_query, key_weight, value_weight, w_output, w_router, norm_gain[:, None], moe_gain[:, None]
    ]
    filled = sum(p.shape[1] for p in pieces)
    pieces.append(jnp.zeros((w_query.shape[0], start + LANES - filled), BF))
    pack = lax.all_gather(
        jnp.concatenate(pieces, axis=1), ("fsdp", "dp"), axis=0, tiled=True
    )
    gain_one = pack[:, start + experts].astype(F32)[None, :]
    gain_two = pack[:, start + experts + 1].astype(F32)[None, :]
    gate_w = lax.all_gather(w_gate, "dp", axis=1, tiled=True)
    up_w = lax.all_gather(w_up, "dp", axis=1, tiled=True)
    down_w = lax.all_gather(w_down, "dp", axis=1, tiled=True)
    grads = [gather_peers(out_grad[m, 0]) for m in range(micro)]
    first = lax.axis_index("fsdp") * held
    places = jnp.arange(8)[:, None]
    sel = ((jnp.arange(experts)[None, :] == first + places) & (places < held)).astype(BF)

    saved, pays = [], []
    for m in range(micro):
        x = inputs[m, 0]
        q, k, v, att, lse, res, pay, gates = attention_forward(
            x, pack, gain_one, gain_two, block_ids[m, 0], routes[m, 0], tables, q_width, kv_width, experts
        )
        saved.append((q, k, v, att, lse, res, pay, gates))
        pays.append(gather_peers(pay))
    carried = None
    for m in range(micro):
        for side in range(2):
            carried = dispatch(
                sel, pays[m][side], grads[m][side], m * 2 + side, micro * 2, held, carried
            )
    flat = (held, micro * chips // 4, 8 * CAP, width)
    rows_in, slot_grad = carried[0].reshape(flat), carried[1].reshape(flat)
    produced, returned, dots, weight_sums = [], [], [], []
    for e in range(held):
        pr, dg, dot, weight = expert(e, parts, rows_in, slot_grad, gate_w, up_w, down_w)
        split = (micro, 2 * chips, CAP)
        produced.append(pr.reshape(split + (width,)))
        returned.append(dg.reshape(split + (width,)))
        dots.append(dot.reshape(split + (1,)))
        weight_sums.append(
            lax.psum_scatter(weight, "dp", scatter_dimension=0, tiled=True)[0]
        )
    others = []
    for m in range(micro):
        (sent,) = combine(sel, pays[m][1], produced, returned, dots, m, 1, None)
        others.append(swap(sent, 1, owners))
    outputs, input_grads = [], []
    prior = None
    for m in range(micro):
        kept = combine(sel, pays[m][0], produced, returned, dots, m, 0, others[m])
        terms = [kept[0][0]] + [swap(kept[r][0], 2 * r, owners) for r in range(1, chips)]
        out, in_grad, prior = attention_backward(
            inputs[m, 0], pack, gain_one, gain_two, block_ids[m, 0], tables, out_grad[m, 0], saved[m],
            terms, prior, q_width, kv_width, experts,
        )
        outputs.append(out)
        input_grads.append(in_grad)
    layer = lax.psum_scatter(prior, ("fsdp", "dp"), scatter_dimension=0, tiled=True).astype(F32)
    marks = np.cumsum([0, q_width, kv_width, kv_width, width, experts, 1, 1])
    cut = [layer[:, a:b] for a, b in zip(marks[:-1], marks[1:])]
    in_rows, down_rows = width // parts, hidden // parts
    stacked = jnp.stack(weight_sums).astype(F32)
    grad_down = stacked[:, 2 * in_rows :].reshape(held, width // hidden, down_rows, hidden)
    grad_down = grad_down.transpose(0, 2, 1, 3).reshape(held, down_rows, width)
    return (
        jnp.stack(outputs)[:, None],
        jnp.stack(input_grads)[:, None],
        cut[5][:, 0], cut[0], cut[1], cut[2], cut[3], cut[6][:, 0], cut[4],
        stacked[:, :in_rows], stacked[:, in_rows : 2 * in_rows], grad_down,
    )


def solution(mesh):
    rows = ("fsdp", "dp")
    split = lambda rank: P(None, rows, *([None] * (rank - 2)))
    flat = P(rows, None)
    expert_spec = P("fsdp", "dp", None)
    in_specs = (
        split(4), split(3), split(4), split(4), P(rows), flat, flat, flat, flat, P(rows), flat,
        expert_spec, expert_spec, expert_spec,
    )
    out_specs = (
        split(4), split(4), P(rows), flat, flat, flat, flat, P(rows), flat,
        expert_spec, expert_spec, expert_spec,
    )
    return jax.shard_map(local, mesh=mesh, in_specs=in_specs, out_specs=out_specs, check_vma=False)
```

```python
import functools

import jax
import jax.numpy as jnp
import numpy as np
from jax import lax
from jax.experimental import pallas as pl
from jax.experimental.pallas import tpu as pltpu
from jax.sharding import PartitionSpec as P

QUERY_HEADS = 16
KEY_VALUE_HEADS = 8
HEAD_SIZE = 64
CAP = 144
EPS = 1e-06
RESIDUAL_SCALE = 0.22
SCORE_SCALE = 0.015625
THETA = 10000.0
NEG_FILL = -1e30
LANES = 128

BF = jnp.bfloat16
F32 = jnp.float32
VMEM_LIMIT = 64 * 1024 * 1024 - 128 * 1024


def mm(a, b):
    return jnp.dot(a, b, preferred_element_type=F32)


def mm_nt(a, b):
    return lax.dot_general(a, b, (((1,), (1,)), ((), ())), preferred_element_type=F32)


def mm_tn(a, b):
    return lax.dot_general(a, b, (((0,), (0,)), ((), ())), preferred_element_type=F32)


def rope_tables(sequence_length):
    half = HEAD_SIZE // 2
    inverse = np.float32(THETA) ** (-(np.arange(half, dtype=np.float32) * 2.0) / HEAD_SIZE)
    angles = np.arange(sequence_length, dtype=np.float32)[:, None] * inverse.astype(np.float32)[None, :]
    cosine, sine = np.cos(angles), np.sin(angles)
    copies = LANES // HEAD_SIZE
    cosine = np.tile(np.concatenate([cosine, cosine], 1), (1, copies))
    sine = np.tile(np.concatenate([-sine, sine], 1), (1, copies))
    return cosine.astype(np.float32), sine.astype(np.float32)


def lane_iota(shape):
    return lax.broadcasted_iota(jnp.int32, shape, len(shape) - 1)


def turn(block, cosine, sine):
    half = HEAD_SIZE // 2
    lower = (lane_iota(block.shape) % HEAD_SIZE) < half
    partner = jnp.where(
        lower, pltpu.roll(block, LANES - half, 1), pltpu.roll(block, half, 1)
    )
    return block * cosine + partner * sine


def tile_ds(index, width):
    return pl.ds(pl.multiple_of(index * width, width), width)


def head_pair(block, place):
    lower = lane_iota(block.shape) < HEAD_SIZE
    moved = pltpu.roll(block, HEAD_SIZE, 1)
    zero = jnp.zeros_like(block)
    low, high = (block, moved) if place == 0 else (moved, block)
    return jnp.where(lower, low, zero), jnp.where(lower, zero, high)


def attention_forward_kernel(
    x_ref, w_ref, gain_one_ref, gain_two_ref, id_row_ref, id_col_ref, cos_ref, sin_ref, picks_ref,
    q_ref, k_ref, v_ref, att_ref, lse_ref, res_ref, pay_ref, gate_ref,
    normed_ref, bias_ref,
    *, q_width, kv_width, experts,
):
    rows, width = x_ref.shape
    x = x_ref[...].astype(F32)
    scale = lax.rsqrt(jnp.mean(x * x, axis=1, keepdims=True) + EPS)
    normed_ref[...] = (x * scale * gain_one_ref[...]).astype(BF)
    bias_ref[...] = jnp.where(id_col_ref[...] <= id_row_ref[...], 0.0, NEG_FILL)
    step = 256

    def project(out_ref, start, count, rotate):
        def body(j, carry):
            cols = pl.ds(pl.multiple_of(start + j * step, step), step)
            part = mm(normed_ref[...], w_ref[:, cols])
            if rotate:
                part = jnp.concatenate(
                    [
                        turn(part[:, i * LANES : (i + 1) * LANES], cos_ref[...], sin_ref[...])
                        for i in range(step // LANES)
                    ],
                    axis=1,
                )
            out_ref[:, tile_ds(j, step)] = part.astype(BF)
            return carry

        lax.fori_loop(0, count // step, body, 0)

    project(q_ref, 0, q_width, True)
    project(k_ref, q_width, kv_width, True)
    project(v_ref, q_width + kv_width, kv_width, False)

    def pair_body(j, carry):
        k_block = k_ref[:, tile_ds(j, LANES)].astype(F32)
        v_block = v_ref[:, tile_ds(j, LANES)].astype(F32)
        for place in range(2):
            keys = head_pair(k_block, place)
            vals = head_pair(v_block, place)
            group = 2 * j + place
            q_block = q_ref[:, tile_ds(group, LANES)]
            out = None
            for side in range(2):
                scores = mm_nt(keys[side].astype(BF), q_block) * SCORE_SCALE + bias_ref[...]
                highest = jnp.max(scores, axis=0, keepdims=True)
                lifted = jnp.exp(scores - highest)
                total = jnp.sum(lifted, axis=0, keepdims=True)
                low = (lifted * (1.0 / total)).astype(BF)
                lse_ref[pl.ds(2 * group + side, 1), :] = highest + jnp.log(total)
                part = mm_tn(vals[side].astype(BF), low)
                out = part if out is None else out + part
            att_ref[:, tile_ds(group, LANES)] = out.T.astype(BF)
        return carry

    lax.fori_loop(0, KEY_VALUE_HEADS // 2, pair_body, 0)

    start = q_width + 2 * kv_width

    def out_body(j, total):
        cols = pl.ds(pl.multiple_of(start + j * step, step), step)
        here = tile_ds(j, step)
        value = x_ref[:, here].astype(F32) + RESIDUAL_SCALE * mm(att_ref[...], w_ref[:, cols])
        res_ref[:, here] = value
        return total + jnp.sum(value * value, axis=1, keepdims=True)

    square = lax.fori_loop(0, width // step, out_body, jnp.zeros((rows, 1), F32))
    scale = lax.rsqrt(square * (1.0 / width) + EPS)
    pay_ref[:rows, :] = (res_ref[...] * scale * gain_two_ref[...]).astype(BF)
    logits = mm(pay_ref[:rows, :], w_ref[:, start + width :])
    lanes = lane_iota(logits.shape)
    chosen = lanes < 0
    for k in range(picks_ref.shape[1]):
        chosen = chosen | (picks_ref[:, k : k + 1] == lanes)
    masked = jnp.where(chosen, logits, NEG_FILL)
    lifted = jnp.where(chosen, jnp.exp(masked - jnp.max(masked, axis=1, keepdims=True)), 0.0)
    gates = lifted / jnp.sum(lifted, axis=1, keepdims=True)
    across = gates.T[:experts, :]
    gate_ref[...] = across
    high = across.astype(BF)
    pay_ref[rows:, :rows] = high
    pay_ref[rows:, rows:] = (across - high.astype(F32)).astype(BF)


def attention_forward(x, pack, gain_one, gain_two, ids, picks, tables, q_width, kv_width, experts):
    rows, width = x.shape
    out_shape = (
        jax.ShapeDtypeStruct((rows, q_width), BF),
        jax.ShapeDtypeStruct((rows, kv_width), BF),
        jax.ShapeDtypeStruct((rows, kv_width), BF),
        jax.ShapeDtypeStruct((rows, q_width), BF),
        jax.ShapeDtypeStruct((QUERY_HEADS, rows), F32),
        jax.ShapeDtypeStruct((rows, width), F32),
        jax.ShapeDtypeStruct((rows + experts, width), BF),
        jax.ShapeDtypeStruct((experts, rows), F32),
    )
    flops = 2 * rows * width * (q_width + 2 * kv_width + width) + 8 * QUERY_HEADS * rows * rows * 128
    return pl.pallas_call(
        functools.partial(
            attention_forward_kernel, q_width=q_width, kv_width=kv_width, experts=experts
        ),
        out_shape=out_shape,
        scratch_shapes=[pltpu.VMEM((rows, width), BF), pltpu.VMEM((rows, rows), F32)],
        compiler_params=pltpu.CompilerParams(vmem_limit_bytes=VMEM_LIMIT),
        cost_estimate=pl.CostEstimate(
            flops=flops, transcendentals=QUERY_HEADS * rows * rows, bytes_accessed=16 << 20
        ),
        name="attention_forward",
    )(x, pack, gain_one, gain_two, ids[None, :], ids[:, None], *tables, picks)


def slot_marks(sel_ref, gate_rows, upper_ref, local):
    picked = mm(sel_ref[...], gate_rows)
    rows = picked.shape[1] // 2
    gates = picked[:, :rows] + picked[:, rows:]
    used = gates != 0.0
    rank = mm(used.astype(F32).astype(BF), upper_ref[...])
    slots = jnp.where(used, rank, -1.0)
    places = lax.broadcasted_iota(jnp.int32, (CAP, rows), 0).astype(F32)
    hits = [places == slots[e : e + 1, :] for e in range(local)]
    return gates, hits


def fill_upper(upper_ref):
    rows = upper_ref.shape[0]
    upper = lax.broadcasted_iota(jnp.int32, (rows, rows), 0) < lane_iota((rows, rows))
    upper_ref[...] = jnp.where(upper, 1.0, 0.0).astype(BF)


def dispatch_kernel(sel_ref, pay_ref, grad_ref, *refs, local):
    rows_ref, slot_ref, upper_ref = refs[-3:]

    @pl.when(pl.program_id(0) == 0)
    def _():
        fill_upper(upper_ref)

    rows = grad_ref.shape[1]
    gates, hits = slot_marks(sel_ref, pay_ref[0, rows:, :], upper_ref, local)
    marks = jnp.concatenate([jnp.where(h, 1.0, 0.0).astype(BF) for h in hits], axis=0)
    column = jnp.concatenate(
        [
            jnp.sum(jnp.where(h, gates[e : e + 1, :], 0.0), axis=1, keepdims=True)
            for e, h in enumerate(hits)
        ],
        axis=0,
    )
    moved = mm(marks, pay_ref[0, :rows, :]).astype(BF)
    grads = (column * (RESIDUAL_SCALE * mm(marks, grad_ref[0]))).astype(BF)
    for e in range(local):
        rows_ref[e, 0, 0] = moved[e * CAP : (e + 1) * CAP]
        slot_ref[e, 0, 0] = grads[e * CAP : (e + 1) * CAP]


def dispatch(sel, pays, grads, place, places, local, carried):
    count, rows, width = grads.shape
    shape = jax.ShapeDtypeStruct((local, places, count, CAP, width), BF)
    out_spec = pl.BlockSpec((local, 1, 1, CAP, width), lambda s: (0, place, s, 0, 0))
    in_specs = [
        pl.BlockSpec(sel.shape, lambda s: (0, 0)),
        pl.BlockSpec((1,) + pays.shape[1:], lambda s: (s, 0, 0)),
        pl.BlockSpec((1, rows, width), lambda s: (s, 0, 0)),
    ]
    operands = [sel, pays, grads]
    aliases = {}
    if carried is not None:
        operands += list(carried)
        in_specs += [pl.BlockSpec(memory_space=pl.ANY)] * 2
        aliases = {3: 0, 4: 1}
    return pl.pallas_call(
        functools.partial(dispatch_kernel, local=local),
        out_shape=(shape, shape),
        grid=(count,),
        in_specs=in_specs,
        out_specs=(out_spec, out_spec),
        scratch_shapes=[pltpu.VMEM((rows, rows), BF)],
        input_output_aliases=aliases,
        compiler_params=pltpu.CompilerParams(vmem_limit_bytes=VMEM_LIMIT),
        cost_estimate=pl.CostEstimate(
            flops=4 * count * local * CAP * rows * width, transcendentals=0, bytes_accessed=20 << 20
        ),
        name="dispatch",
    )(*operands)


def expert_kernel(x_ref, s_ref, w_ref, *refs, chunk, tile, last, carried):
    if carried:
        prior_ref, refs = refs[0], refs[1:]
    (
        pr_ref, dg_ref, dot_ref, grad_ref,
        gate_ref, up_ref, down_ref, act_ref, both_ref, acc_in_ref, acc_down_ref,
    ) = refs
    rows, width = x_ref.shape[-2:]
    hidden = gate_ref.shape[-1]
    owners = grad_ref.shape[0]
    in_rows, down_rows = width // owners, hidden // owners
    step = pl.program_id(1)
    pieces = width // hidden

    @pl.when(step == 0)
    def _():
        for o in range(owners):
            gate_ref[o * in_rows : (o + 1) * in_rows, :] = w_ref[o, 0, :in_rows, :]
            up_ref[o * in_rows : (o + 1) * in_rows, :] = w_ref[o, 0, in_rows : 2 * in_rows, :]
            for c in range(pieces):
                first = 2 * in_rows + c * down_rows
                down_ref[o * down_rows : (o + 1) * down_rows, c * hidden : (c + 1) * hidden] = w_ref[
                    o, 0, first : first + down_rows, :
                ]

    def chunk_body(c, carry):
        here = tile_ds(c, chunk)
        x = x_ref[0, here, :]
        s = s_ref[0, here, :]
        pre_gate = mm(x, gate_ref[...])
        pre_up = mm(x, up_ref[...])
        act_grad = mm_nt(s, down_ref[...])
        logistic = jax.nn.sigmoid(pre_gate)
        swish = pre_gate * logistic
        act = (swish * pre_up).astype(BF)
        gate_in = (
            act_grad * pre_up * logistic * (1.0 + pre_gate * (1.0 - logistic))
        ).astype(BF)
        up_in = (act_grad * swish).astype(BF)
        dot_ref[0, here, :] = jnp.sum(act.astype(F32) * act_grad, axis=1, keepdims=True)
        act_ref[here, :] = act
        both_ref[here, :hidden] = gate_in
        both_ref[here, hidden:] = up_in
        pr_ref[0, here, :] = mm(act, down_ref[...]).astype(BF)
        dg_ref[0, here, :] = (mm_nt(gate_in, gate_ref[...]) + mm_nt(up_in, up_ref[...])).astype(BF)
        return carry

    lax.fori_loop(0, rows // chunk, chunk_body, 0)

    def put(owner, first, value):
        count = value.shape[0]
        if carried:
            value = value + prior_ref[owner, 0, first : first + count, :].astype(F32)
        grad_ref[owner, 0, first : first + count, :] = value.astype(BF)

    def accumulate(acc_ref, here, part, emit):
        if last == 0:
            emit(part)
            return

        @pl.when(step == 0)
        def _():
            acc_ref[here, :] = part

        if last > 1:

            @pl.when((step > 0) & (step < last))
            def _():
                acc_ref[here, :] = acc_ref[here, :] + part

        @pl.when(step == last)
        def _():
            emit(acc_ref[here, :] + part)

    def in_body(t, carry):
        here = tile_ds(t, tile)

        def emit(total):
            for i in range(tile // in_rows):
                piece = total[i * in_rows : (i + 1) * in_rows]
                owner = t * (tile // in_rows) + i
                put(owner, 0, piece[:, :hidden])
                put(owner, in_rows, piece[:, hidden:])

        accumulate(acc_in_ref, here, mm_tn(x_ref[0, :, here], both_ref[...]), emit)
        return carry

    lax.fori_loop(0, width // tile, in_body, 0)

    def down_body(t, carry):
        here = tile_ds(t, tile)

        def emit(total):
            for i in range(tile // down_rows):
                piece = total[i * down_rows : (i + 1) * down_rows]
                owner = t * (tile // down_rows) + i
                for c in range(pieces):
                    put(owner, 2 * in_rows + c * down_rows, piece[:, c * hidden : (c + 1) * hidden])

        accumulate(acc_down_ref, here, mm_tn(act_ref[:, here], s_ref[0]), emit)
        return carry

    lax.fori_loop(0, hidden // tile, down_body, 0)


def experts_step(first, weights, rows_in, slot_grad, prior):
    owners, count, packed, hidden = weights.shape
    _, total, width = rows_in.shape
    rows = 8 * CAP
    steps = total // rows
    out_shape = (
        jax.ShapeDtypeStruct((count, total, width), BF),
        jax.ShapeDtypeStruct((count, total, width), BF),
        jax.ShapeDtypeStruct((count, total, 1), F32),
        jax.ShapeDtypeStruct(weights.shape, BF),
    )
    in_spec = pl.BlockSpec((1, rows, width), lambda e, t: (first + e, t, 0))
    pack_spec = pl.BlockSpec((owners, 1, packed, hidden), lambda e, t: (0, e, 0, 0))
    row_spec = lambda last: pl.BlockSpec((1, rows, last), lambda e, t: (e, t, 0))
    operands = [rows_in, slot_grad, weights]
    in_specs = [in_spec, in_spec, pack_spec]
    if prior is not None:
        operands.append(prior)
        in_specs.append(pack_spec)
    kept = 0 if steps == 1 else 1
    return pl.pallas_call(
        functools.partial(
            expert_kernel, chunk=rows // 3, tile=256, last=steps - 1, carried=prior is not None
        ),
        out_shape=out_shape,
        grid=(count, steps),
        in_specs=in_specs,
        out_specs=(row_spec(width), row_spec(width), row_spec(1), pack_spec),
        scratch_shapes=[
            pltpu.VMEM((width, hidden), BF),
            pltpu.VMEM((width, hidden), BF),
            pltpu.VMEM((hidden, width), BF),
            pltpu.VMEM((rows, hidden), BF),
            pltpu.VMEM((rows, 2 * hidden), BF),
            pltpu.VMEM((width, 2 * hidden) if kept else (8, LANES), F32),
            pltpu.VMEM((hidden, width) if kept else (8, LANES), F32),
        ],
        compiler_params=pltpu.CompilerParams(vmem_limit_bytes=VMEM_LIMIT),
        cost_estimate=pl.CostEstimate(
            flops=18 * count * total * width * hidden, transcendentals=count * total * hidden,
            bytes_accessed=30 << 20,
        ),
        name="experts",
    )(*operands)


def combine_kernel(sel_ref, pay_ref, *refs, groups, local, received):
    produced, returned, dots = (refs[i * groups : (i + 1) * groups] for i in range(3))
    rest = refs[3 * groups :]
    if received:
        other_ref, rest = rest[0], rest[1:]
    out_refs, upper_ref = rest[:-1], rest[-1]
    each = local // groups

    @pl.when(pl.program_id(0) == 0)
    def _():
        fill_upper(upper_ref)

    rows = upper_ref.shape[0]
    gates, hits = slot_marks(sel_ref, pay_ref[0], upper_ref, local)
    weighted = jnp.concatenate(
        [jnp.where(h, gates[e : e + 1, :], 0.0).astype(BF) for e, h in enumerate(hits)], axis=0
    )
    plain = jnp.concatenate([jnp.where(h, 1.0, 0.0).astype(BF) for h in hits], axis=0)
    made = jnp.concatenate([r[e, 0] for r in produced for e in range(each)], axis=0)
    back = jnp.concatenate([r[e, 0] for r in returned for e in range(each)], axis=0)
    out = mm_tn(weighted, made)
    grads = mm_tn(plain, back)
    pad = jnp.zeros((8 - local, rows), F32)
    dot_rows = jnp.concatenate(
        [
            jnp.sum(jnp.where(h, dots[e // each][e % each, 0], 0.0), axis=0, keepdims=True)
            for e, h in enumerate(hits)
        ]
        + ([pad] if local < 8 else []),
        axis=0,
    )
    high = dot_rows.astype(BF)
    low = (dot_rows - high.astype(F32)).astype(BF)
    tail = jnp.concatenate([mm_tn(sel_ref[...], high), mm_tn(sel_ref[...], low)], axis=1)
    half = tail.shape[0] // 2
    first = jnp.concatenate([out, tail[:half]], axis=0)
    second = jnp.concatenate([tail[half:], grads], axis=0)
    if received:
        first = first + other_ref[0, : rows + half, :].astype(F32)
        second = second + other_ref[0, rows + half :, :].astype(F32)

        def put(index):
            out_refs[2 * index][...] = first.astype(BF)
            out_refs[2 * index + 1][...] = second.astype(BF)

        for index in range(len(out_refs) // 2):
            pl.when(pl.program_id(0) == index)(functools.partial(put, index))
    else:
        out_refs[0][0, : rows + half, :] = first.astype(BF)
        out_refs[0][0, rows + half :, :] = second.astype(BF)


def combine(sel, pays, produced, returned, dots, side, other):
    count, total_rows, width = pays.shape
    groups, each = len(produced), produced[0].shape[0]
    local = groups * each
    experts = sel.shape[1]
    rows = total_rows - experts
    pick = lambda last: pl.BlockSpec((each, 1, CAP, last), lambda s: (0, side * count + s, 0, 0))
    in_specs = [
        pl.BlockSpec(sel.shape, lambda s: (0, 0)),
        pl.BlockSpec((1, experts, width), lambda s: (s, rows // experts, 0)),
    ]
    in_specs += [pick(width)] * (2 * groups) + [pick(1)] * groups
    operands = [sel, pays, *produced, *returned, *dots]
    total = 2 * rows + experts
    out_spec = pl.BlockSpec((1, total, width), lambda s: (s, 0, 0))
    out_shape = (jax.ShapeDtypeStruct((count, total, width), BF),)
    out_specs = (out_spec,)
    if other is not None:
        operands.append(other)
        in_specs.append(out_spec)
        out_shape = (jax.ShapeDtypeStruct((total // 2, width), BF),) * (2 * count)
        out_specs = (pl.BlockSpec((total // 2, width), lambda s: (0, 0)),) * (2 * count)
    return pl.pallas_call(
        functools.partial(combine_kernel, groups=groups, local=local, received=other is not None),
        out_shape=out_shape,
        grid=(count,),
        in_specs=in_specs,
        out_specs=out_specs,
        scratch_shapes=[pltpu.VMEM((rows, rows), BF)],
        compiler_params=pltpu.CompilerParams(vmem_limit_bytes=VMEM_LIMIT),
        cost_estimate=pl.CostEstimate(
            flops=4 * count * local * CAP * rows * width, transcendentals=0, bytes_accessed=20 << 20
        ),
        name="combine",
    )(*operands)


def attention_backward_kernel(
    *refs, terms, q_width, kv_width, experts, carried,
):
    (
        x_ref, w_ref, gain_one_ref, gain_two_ref, id_row_ref, id_col_ref, cos_ref, sin_ref,
        grad_ref, q_ref, k_ref, v_ref, att_ref, lse_ref, res_ref, pay_ref, gate_ref,
    ) = refs[:17]
    term_refs = refs[17 : 17 + 2 * terms]
    rest = refs[17 + 2 * terms :]
    if carried:
        prior_ref, rest = rest[0], rest[1:]
    out_ref, in_grad_ref, pack_ref, bias_ref, wide_ref, att_grad_ref, qkv_grad_ref, branch_ref, normed_ref = rest
    rows, width = x_ref.shape
    step = 256
    start = q_width + 2 * kv_width

    def put(row_slice, cols, value):
        if carried:
            value = value + prior_ref[row_slice, cols].astype(F32)
        pack_ref[row_slice, cols] = value.astype(BF)

    def gathered(which, low, high):
        total = term_refs[which][low:high, :].astype(F32)
        for ref in term_refs[2 + which :: 2]:
            total = total + ref[low:high, :].astype(F32)
        return total

    half = experts // 2
    residual = res_ref[...]
    out_ref[...] = (residual + RESIDUAL_SCALE * gathered(0, 0, rows)).astype(BF)
    tail = jnp.concatenate([gathered(0, rows, rows + half), gathered(1, 0, half)], axis=0)
    weighted = tail[:, :rows] + tail[:, rows:]
    chosen = weighted - gate_ref[...] * jnp.sum(weighted, axis=0, keepdims=True)
    chosen = jnp.concatenate([chosen, jnp.zeros((LANES - experts, rows), F32)], axis=0)
    logit_grad = chosen.T.astype(BF)
    moe_grad = gathered(1, half, half + rows) + mm_nt(logit_grad, w_ref[:, start + width :])
    last = mm_tn(pay_ref[:rows, :], logit_grad)
    scale = lax.rsqrt(jnp.mean(residual * residual, axis=1, keepdims=True) + EPS)
    gain_two_grad = jnp.sum(moe_grad * residual * scale, axis=0, keepdims=True)
    u = moe_grad * gain_two_ref[...]
    inner = jnp.sum(u * residual, axis=1, keepdims=True) * (1.0 / width)
    res_grad = grad_ref[...].astype(F32) + scale * u - residual * (scale * scale * scale * inner)
    in_grad_ref[...] = res_grad
    branch_ref[...] = (RESIDUAL_SCALE * res_grad).astype(BF)
    bias_ref[...] = jnp.where(id_col_ref[...] <= id_row_ref[...], 0.0, NEG_FILL)

    def branch_body(j, carry):
        here = tile_ds(j, step)
        att_grad_ref[:, here] = mm_nt(
            branch_ref[...], w_ref[here, start : start + width]
        ).astype(BF)
        part = mm_tn(att_ref[:, here], branch_ref[...])
        put(here, slice(start, start + width), part)
        return carry

    lax.fori_loop(0, q_width // step, branch_body, 0)

    lower = lane_iota((rows, LANES)) < HEAD_SIZE

    def pair_body(j, carry):
        k_block = k_ref[:, tile_ds(j, LANES)].astype(F32)
        v_block = v_ref[:, tile_ds(j, LANES)].astype(F32)
        k_sums, v_sums = [], []
        for place in range(2):
            keys = [h.astype(BF) for h in head_pair(k_block, place)]
            vals = [h.astype(BF) for h in head_pair(v_block, place)]
            group = 2 * j + place
            here = tile_ds(group, LANES)
            q_block = q_ref[:, here]
            g_block = att_grad_ref[:, here]
            q_out = None
            k_parts, v_parts = [], []
            for side in range(2):
                scores = mm_nt(keys[side], q_block) * SCORE_SCALE + bias_ref[...]
                probs = jnp.exp(scores - lse_ref[pl.ds(2 * group + side, 1), :])
                weight_grad = mm_nt(vals[side], g_block)
                v_parts.append(mm(probs.astype(BF), g_block))
                dots = jnp.sum(probs * weight_grad, axis=0, keepdims=True)
                score_grad = (probs * (weight_grad - dots)).astype(BF)
                k_parts.append(mm(score_grad, q_block))
                part = mm_tn(keys[side], score_grad)
                q_out = part if q_out is None else q_out + part
            q_turned = turn(q_out.T * SCORE_SCALE, cos_ref[...], -sin_ref[...])
            qkv_grad_ref[:, here] = q_turned.astype(BF)
            for parts, sums in ((k_parts, k_sums), (v_parts, v_sums)):
                mixed = jnp.where(lower, parts[0], parts[1])
                sums.append(mixed + pltpu.roll(mixed, HEAD_SIZE, 1))
        k_total = jnp.where(lower, k_sums[0], k_sums[1]) * SCORE_SCALE
        v_total = jnp.where(lower, v_sums[0], v_sums[1])
        k_here = pl.ds(pl.multiple_of(q_width + j * LANES, LANES), LANES)
        v_here = pl.ds(pl.multiple_of(q_width + kv_width + j * LANES, LANES), LANES)
        qkv_grad_ref[:, k_here] = turn(k_total, cos_ref[...], -sin_ref[...]).astype(BF)
        qkv_grad_ref[:, v_here] = v_total.astype(BF)
        return carry

    lax.fori_loop(0, KEY_VALUE_HEADS // 2, pair_body, 0)

    x = x_ref[...].astype(F32)
    scale = lax.rsqrt(jnp.mean(x * x, axis=1, keepdims=True) + EPS)
    normed_ref[...] = (x * scale * gain_one_ref[...]).astype(BF)

    def norm_body(j, carry):
        here = tile_ds(j, step)
        grad = mm_nt(qkv_grad_ref[...], w_ref[here, :start])
        put(here, slice(0, start), mm_tn(normed_ref[:, here], qkv_grad_ref[...]))
        wide_ref[:, here] = grad
        return carry

    lax.fori_loop(0, width // step, norm_body, 0)
    normed_grad = wide_ref[...]
    gain_one_grad = jnp.sum(normed_grad * x * scale, axis=0, keepdims=True)
    u = normed_grad * gain_one_ref[...]
    inner = jnp.sum(u * x, axis=1, keepdims=True) * (1.0 / width)
    in_grad_ref[...] = in_grad_ref[...] + scale * u - x * (scale * scale * scale * inner)
    lanes = lane_iota((width, LANES))
    one = jnp.broadcast_to(gain_one_grad, (LANES, width)).T
    two = jnp.broadcast_to(gain_two_grad, (LANES, width)).T
    last = jnp.where(lanes == experts, one, last)
    last = jnp.where(lanes == experts + 1, two, last)
    put(slice(0, width), slice(start + width, start + width + LANES), last)


def attention_backward(
    x, pack, gain_one, gain_two, ids, tables, grad, saved, terms, prior, q_width, kv_width, experts
):
    rows, width = x.shape
    operands = [x, pack, gain_one, gain_two, ids[None, :], ids[:, None], *tables, grad, *saved, *terms]
    if prior is not None:
        operands.append(prior)
    flops = 4 * rows * width * (q_width + 2 * kv_width + width) + 20 * QUERY_HEADS * rows * rows * 128
    return pl.pallas_call(
        functools.partial(
            attention_backward_kernel, terms=len(terms) // 2, q_width=q_width, kv_width=kv_width,
            experts=experts, carried=prior is not None,
        ),
        out_shape=(
            jax.ShapeDtypeStruct((rows, width), BF),
            jax.ShapeDtypeStruct((rows, width), F32),
            jax.ShapeDtypeStruct(pack.shape, BF),
        ),
        scratch_shapes=[
            pltpu.VMEM((rows, rows), F32),
            pltpu.VMEM((rows, width), F32),
            pltpu.VMEM((rows, q_width), BF),
            pltpu.VMEM((rows, q_width + 2 * kv_width), BF),
            pltpu.VMEM((rows, width), BF),
            pltpu.VMEM((rows, width), BF),
        ],
        compiler_params=pltpu.CompilerParams(vmem_limit_bytes=VMEM_LIMIT),
        cost_estimate=pl.CostEstimate(
            flops=flops, transcendentals=QUERY_HEADS * rows * rows, bytes_accessed=40 << 20
        ),
        name="attention_backward",
    )(*operands)


def peer_chip(chip, distance):
    total = 0
    for bit in (1, 2, 4):
        total = total + bit * ((chip // bit + (distance // bit) % 2) % 2)
    return total


def where_am_i():
    f, d = lax.axis_index("fsdp"), lax.axis_index("dp")
    return f // 2, f % 2, d


def meet(peers):
    barrier = pltpu.get_barrier_semaphore()
    for peer in peers:
        pl.semaphore_signal(
            barrier, inc=1, device_id=peer, device_id_type=pl.DeviceIdType.MESH
        )
    pl.semaphore_wait(barrier, len(peers))


def push(src, dst, send, receive, peer):
    copy = pltpu.make_async_remote_copy(
        src_ref=src, dst_ref=dst, send_sem=send, recv_sem=receive, device_id=peer,
        device_id_type=pl.DeviceIdType.MESH,
    )
    copy.start()
    return copy


def gather_layer_kernel(
    w_ref, out_ref, own_sem, z_send, z_receive, x_send, x_receive, s_send, s_receive, *, chips, depth
):
    chip, core, d = where_am_i()
    rows = w_ref.shape[0]
    others = [peer_chip(chip, r) for r in range(1, chips)]
    f, sibling = chip * 2 + core, chip * 2 + 1 - core

    def block(owner, layer):
        first = pl.multiple_of((owner * depth + layer) * rows, rows)
        return out_ref.at[pl.ds(first, rows), :]

    peers = [(f, (d + i) % depth) for i in range(1, depth)]
    peers += [(c * 2 + core, d) for c in others] + [(sibling, d)]
    meet(peers)
    own = pltpu.make_async_copy(w_ref, block(f, d), own_sem)
    own.start()
    z_copies = [
        push(w_ref, block(f, d), z_send.at[i - 1], z_receive.at[i - 1], (f, (d + i) % depth))
        for i in range(1, depth)
    ]
    x_copies, s_copies = [], []
    layers = [(d + depth - i) % depth for i in range(depth)]
    for i, layer in enumerate(layers):
        if i:
            z_copies[i - 1].wait_recv()
        src = block(f, layer) if i else w_ref
        for r, c in enumerate(others):
            x_copies.append(
                push(src, block(f, layer), x_send.at[i, r], x_receive.at[i, r], (c * 2 + core, d))
            )
        s_copies.append(
            push(src, block(f, layer), s_send.at[i, 0], s_receive.at[i, 0], (sibling, d))
        )
    for i, layer in enumerate(layers):
        for r, c in enumerate(others):
            x_copies[i * (chips - 1) + r].wait_recv()
            there = block(c * 2 + core, layer)
            s_copies.append(
                push(there, there, s_send.at[i, r + 1], s_receive.at[i, r + 1], (sibling, d))
            )
    own.wait()
    for copy in z_copies + x_copies:
        copy.wait_send()
    for copy in s_copies:
        copy.wait()


def gather_layer(pack, chips, depth):
    dma = pltpu.SemaphoreType.DMA
    rows, width = pack.shape
    return pl.pallas_call(
        functools.partial(gather_layer_kernel, chips=chips, depth=depth),
        out_shape=jax.ShapeDtypeStruct((rows * 2 * chips * depth, width), pack.dtype),
        in_specs=[pl.BlockSpec(memory_space=pl.ANY)],
        out_specs=pl.BlockSpec(memory_space=pl.ANY),
        scratch_shapes=[
            dma(()), dma((depth - 1,)), dma((depth - 1,)), dma((depth, chips - 1)),
            dma((depth, chips - 1)), dma((depth, chips)), dma((depth, chips)),
        ],
        compiler_params=pltpu.CompilerParams(collective_id=1, has_side_effects=True),
        name="gather_layer",
    )(pack)


def reduce_layer_kernel(
    pack_ref, out_ref, s_buf, s_sum, x_buf, x_sum, z_buf,
    s_send, s_receive, x_send, x_receive, z_send, z_receive,
    *, chips, depth, parts,
):
    chip, core, d = where_am_i()
    total, width = pack_ref.shape
    rows = total // (2 * chips * depth)
    span = rows * depth
    step = width // parts
    distances = list(range(1, chips))
    others = [peer_chip(chip, r) for r in distances]
    f, sibling = chip * 2 + core, chip * 2 + 1 - core
    peers = [(f, (d + i) % depth) for i in range(1, depth)]
    peers += [(c * 2 + core, d) for c in others] + [(sibling, d)]
    meet(peers)

    def band(p):
        return slice(p * step, (p + 1) * step)

    def mine(c, k):
        return pl.ds(pl.multiple_of((c * 2 + k) * span, span), span)

    order = [(r, c) for r, c in zip(distances, others)][::-1] + [(0, chip)]
    s_copies = {}
    for p in range(parts):
        for r, c in order:
            s_copies[p, r] = push(
                pack_ref.at[mine(c, 1 - core), band(p)], s_buf.at[r, :, band(p)],
                s_send.at[p, r], s_receive.at[p, r], (sibling, d),
            )
    x_copies, z_copies = {}, {}

    def sum_chip(p):
        for r, c in order:
            s_copies[p, r].wait_recv()
            value = pack_ref[mine(c, core), band(p)].astype(F32) + s_buf[r, :, band(p)].astype(F32)
            s_sum[r, :, band(p)] = value.astype(s_sum.dtype)

    def send_chip(p):
        for r, c in order[:-1]:
            x_copies[p, r] = push(
                s_sum.at[r, :, band(p)], x_buf.at[r - 1, :, band(p)], x_send.at[p, r - 1],
                x_receive.at[p, r - 1], (c * 2 + core, d),
            )

    def sum_plane(p):
        value = s_sum[0, :, band(p)].astype(F32)
        for r in distances:
            x_copies[p, r].wait_recv()
            value = value + x_buf[r - 1, :, band(p)].astype(F32)
        x_sum[:, :, band(p)] = value.reshape(depth, rows, step).astype(x_sum.dtype)

    def send_plane(p):
        for i in range(1, depth):
            to = (d + i) % depth
            z_copies[p, i] = push(
                x_sum.at[to, :, band(p)], z_buf.at[i - 1, :, band(p)], z_send.at[p, i - 1],
                z_receive.at[p, i - 1], (f, to),
            )

    def finish(p):
        value = x_sum[d, :, band(p)].astype(F32)
        for i in range(1, depth):
            z_copies[p, i].wait_recv()
            value = value + z_buf[i - 1, :, band(p)].astype(F32)
        out_ref[:, band(p)] = value

    for p in range(parts + 1):
        if p < parts:
            sum_chip(p)
        if p > 0:
            send_chip(p - 1)
    for p in range(parts + 1):
        if p < parts:
            sum_plane(p)
        if p > 0:
            send_plane(p - 1)
    for p in range(parts):
        finish(p)
    for copy in [*s_copies.values(), *x_copies.values(), *z_copies.values()]:
        copy.wait_send()


def reduce_layer(pack, chips, depth, parts):
    dma = pltpu.SemaphoreType.DMA
    total, width = pack.shape
    rows = total // (2 * chips * depth)
    kind = BF if rows % 16 == 0 else F32
    return pl.pallas_call(
        functools.partial(reduce_layer_kernel, chips=chips, depth=depth, parts=parts),
        out_shape=jax.ShapeDtypeStruct((rows, width), F32),
        in_specs=[pl.BlockSpec(memory_space=pltpu.VMEM)],
        out_specs=pl.BlockSpec(memory_space=pltpu.VMEM),
        scratch_shapes=[
            pltpu.VMEM((chips, rows * depth, width), BF),
            pltpu.VMEM((chips, rows * depth, width), BF),
            pltpu.VMEM((chips - 1, rows * depth, width), BF),
            pltpu.VMEM((depth, rows, width), kind),
            pltpu.VMEM((depth - 1, rows, width), kind),
            dma((parts, chips)), dma((parts, chips)), dma((parts, chips - 1)), dma((parts, chips - 1)),
            dma((parts, depth - 1)), dma((parts, depth - 1)),
        ],
        compiler_params=pltpu.CompilerParams(
            collective_id=2, has_side_effects=True, vmem_limit_bytes=VMEM_LIMIT
        ),
        name="reduce_layer",
    )(pack)


def swap(value, distance, size):
    return lax.ppermute(value, "fsdp", [(i, i ^ distance) for i in range(size)])


def gather_chips(value, size):
    chips = size // 2
    if chips != 4:
        return jnp.stack([value] + [swap(value, 2 * r, size) for r in range(1, chips)])
    half = value.shape[0] // 2
    one, two = swap(value, 2, size), swap(value, 4, size)
    three = jnp.concatenate([swap(one[:half], 4, size), swap(two[half:], 2, size)])
    return jnp.stack([value, one, two, three])


def scatter_chips(kept, size):
    chips = size // 2
    if chips != 4:
        return [kept[0], kept[1]] + [swap(kept[2 * r + h], 2 * r, size) for r in range(1, chips) for h in range(2)]
    add = lambda a, b: (a.astype(F32) + b.astype(F32)).astype(BF)
    by_one = swap(kept[6], 2, size)
    by_two = swap(kept[7], 4, size)
    one_first = swap(kept[2], 2, size)
    two_second = swap(kept[5], 4, size)
    one_second = swap(add(kept[3], by_two), 2, size)
    two_first = swap(add(kept[4], by_one), 4, size)
    return [kept[0], kept[1], one_first, one_second, two_first, two_second]


def local(
    inputs, block_ids, routes, out_grad, norm_gain, w_query, key_weight, value_weight, w_output,
    moe_gain, w_router, w_gate, w_up, w_down,
):
    micro, _, rows, width = inputs.shape
    experts = w_router.shape[1]
    held, in_rows, hidden = w_gate.shape
    down_rows = w_down.shape[1]
    q_width, kv_width = w_query.shape[1], key_weight.shape[1]
    owners = lax.axis_size("fsdp")
    depth = lax.axis_size("dp")
    chips = owners // 2
    tables = tuple(jnp.asarray(t) for t in rope_tables(rows))
    start = q_width + 2 * kv_width + width
    group = max(1, held // 2)
    cuts = width // hidden

    split_down = w_down.reshape(held, down_rows, cuts, hidden).transpose(0, 2, 1, 3)
    packed = jnp.concatenate(
        [w_gate, w_up, split_down.reshape(held, cuts * down_rows, hidden)], axis=1
    )
    weights = [
        lax.all_gather(packed[g : g + group], "dp", axis=0, tiled=False)
        for g in range(0, held, group)
    ]
    pieces = [
        w_query, key_weight, value_weight, w_output, w_router, norm_gain[:, None], moe_gain[:, None]
    ]
    filled = sum(p.shape[1] for p in pieces)
    pieces.append(jnp.zeros((w_query.shape[0], start + LANES - filled), BF))
    pack = gather_layer(jnp.concatenate(pieces, axis=1), chips, depth)
    gain_one = pack[:, start + experts].astype(F32)[None, :]
    gain_two = pack[:, start + experts + 1].astype(F32)[None, :]
    first = lax.axis_index("fsdp") * held
    places = jnp.arange(8)[:, None]
    sel = ((jnp.arange(experts)[None, :] == first + places) & (places < held)).astype(BF)
    later, _ = lax.optimization_barrier((out_grad, pack))

    saved, pays, grads = [], [], []
    for m in range(micro):
        x = inputs[m, 0]
        q, k, v, att, lse, res, pay, gates = attention_forward(
            x, pack, gain_one, gain_two, block_ids[m, 0], routes[m, 0], tables, q_width, kv_width, experts
        )
        saved.append((q, k, v, att, lse, res, pay, gates))
        mine = gather_chips(later[m, 0], owners)
        grads.append((mine, swap(mine, 1, owners)))
        mine = gather_chips(pay, owners)
        pays.append((mine, swap(mine, 1, owners)))
    moved = []
    for m in range(micro):
        carried = None
        for side in range(2):
            carried = dispatch(sel, pays[m][side], grads[m][side], side, 2, held, carried)
        moved.append([c.reshape(held, 2 * chips * CAP, width) for c in carried])
    order = [(m, g) for m in range(micro) for g in range(len(weights))]
    done = {}
    for m, g in order:
        prior = done[m - 1, g][3] if m else None
        done[m, g] = experts_step(g * group, weights[g], *moved[m], prior)
    sums = [
        lax.psum_scatter(done[micro - 1, g][3], "dp", scatter_dimension=0, tiled=True)[0]
        for g in range(len(weights))
    ]
    terms = []
    for m in range(micro):
        parts = [
            [done[m, g][i].reshape(group, 2 * chips, CAP, -1) for g in range(len(weights))]
            for i in range(3)
        ]
        (sent,) = combine(sel, pays[m][1], *parts, 1, None)
        kept = combine(sel, pays[m][0], *parts, 0, swap(sent, 1, owners))
        terms.append(scatter_chips(kept, owners))
    outputs, input_grads = [], []
    prior = None
    for m in range(micro):
        out, in_grad, prior = attention_backward(
            inputs[m, 0], pack, gain_one, gain_two, block_ids[m, 0], tables, out_grad[m, 0], saved[m],
            terms[m], prior, q_width, kv_width, experts,
        )
        outputs.append(out)
        input_grads.append(in_grad)
    layer = reduce_layer(prior, chips, depth, 5)
    marks = np.cumsum([0, q_width, kv_width, kv_width, width, experts, 1, 1])
    cut = [layer[:, a:b] for a, b in zip(marks[:-1], marks[1:])]
    stacked = jnp.concatenate(sums, axis=0).astype(F32)
    grad_down = stacked[:, 2 * in_rows :].reshape(held, cuts, down_rows, hidden)
    grad_down = grad_down.transpose(0, 2, 1, 3).reshape(held, down_rows, width)
    return (
        jnp.stack(outputs)[:, None],
        jnp.stack(input_grads)[:, None],
        cut[5][:, 0], cut[0], cut[1], cut[2], cut[3], cut[6][:, 0], cut[4],
        stacked[:, :in_rows], stacked[:, in_rows : 2 * in_rows], grad_down,
    )


def solution(mesh):
    rows = ("fsdp", "dp")
    split = lambda rank: P(None, rows, *([None] * (rank - 2)))
    flat = P(rows, None)
    expert_spec = P("fsdp", "dp", None)
    in_specs = (
        split(4), split(3), split(4), split(4), P(rows), flat, flat, flat, flat, P(rows), flat,
        expert_spec, expert_spec, expert_spec,
    )
    out_specs = (
        split(4), split(4), P(rows), flat, flat, flat, flat, P(rows), flat,
        expert_spec, expert_spec, expert_spec,
    )
    return jax.shard_map(local, mesh=mesh, in_specs=in_specs, out_specs=out_specs, check_vma=False)
```

```python
import functools

import jax
import jax.numpy as jnp
import numpy as np
from jax import lax
from jax.experimental import pallas as pl
from jax.experimental.pallas import tpu as pltpu
from jax.sharding import PartitionSpec as P

QUERY_HEADS = 16
KEY_VALUE_HEADS = 8
HEAD_SIZE = 64
CAP = 144
EPS = 1e-06
RESIDUAL_SCALE = 0.22
SCORE_SCALE = 0.015625
THETA = 10000.0
NEG_FILL = -1e30
LANES = 128

BF = jnp.bfloat16
F32 = jnp.float32
VMEM_LIMIT = 64 * 1024 * 1024 - 128 * 1024


def mm(a, b):
    return jnp.dot(a, b, preferred_element_type=F32)


def mm_nt(a, b):
    return lax.dot_general(a, b, (((1,), (1,)), ((), ())), preferred_element_type=F32)


def mm_tn(a, b):
    return lax.dot_general(a, b, (((0,), (0,)), ((), ())), preferred_element_type=F32)


def rope_tables(sequence_length):
    half = HEAD_SIZE // 2
    inverse = np.float32(THETA) ** (-(np.arange(half, dtype=np.float32) * 2.0) / HEAD_SIZE)
    angles = np.arange(sequence_length, dtype=np.float32)[:, None] * inverse.astype(np.float32)[None, :]
    cosine, sine = np.cos(angles), np.sin(angles)
    copies = LANES // HEAD_SIZE
    cosine = np.tile(np.concatenate([cosine, cosine], 1), (1, copies))
    sine = np.tile(np.concatenate([-sine, sine], 1), (1, copies))
    return cosine.astype(np.float32), sine.astype(np.float32)


def lane_iota(shape):
    return lax.broadcasted_iota(jnp.int32, shape, len(shape) - 1)


def turn(block, cosine, sine):
    half = HEAD_SIZE // 2
    lower = (lane_iota(block.shape) % HEAD_SIZE) < half
    partner = jnp.where(
        lower, pltpu.roll(block, LANES - half, 1), pltpu.roll(block, half, 1)
    )
    return block * cosine + partner * sine


def hint(flops, transcendentals, bytes_accessed, share=16):
    return pl.CostEstimate(
        flops=flops // share, transcendentals=transcendentals // share,
        bytes_accessed=bytes_accessed // share,
    )


def tile_ds(index, width):
    return pl.ds(pl.multiple_of(index * width, width), width)


def head_pair(block, place):
    lower = lane_iota(block.shape) < HEAD_SIZE
    moved = pltpu.roll(block, HEAD_SIZE, 1)
    zero = jnp.zeros_like(block)
    low, high = (block, moved) if place == 0 else (moved, block)
    return jnp.where(lower, low, zero), jnp.where(lower, zero, high)


def attention_forward_kernel(
    x_ref, w_ref, gain_one_ref, gain_two_ref, id_row_ref, id_col_ref, cos_ref, sin_ref, picks_ref,
    q_ref, k_ref, v_ref, att_ref, lse_ref, res_ref, pay_ref, gate_ref,
    normed_ref, bias_ref,
    *, q_width, kv_width, experts,
):
    rows, width = x_ref.shape
    x = x_ref[...].astype(F32)
    scale = lax.rsqrt(jnp.mean(x * x, axis=1, keepdims=True) + EPS)
    normed_ref[...] = (x * scale * gain_one_ref[...]).astype(BF)
    bias_ref[...] = jnp.where(id_col_ref[...] <= id_row_ref[...], 0.0, NEG_FILL)
    step = 256

    def project(out_ref, start, count, rotate):
        def body(j, carry):
            cols = pl.ds(pl.multiple_of(start + j * step, step), step)
            part = mm(normed_ref[...], w_ref[:, cols])
            if rotate:
                part = jnp.concatenate(
                    [
                        turn(part[:, i * LANES : (i + 1) * LANES], cos_ref[...], sin_ref[...])
                        for i in range(step // LANES)
                    ],
                    axis=1,
                )
            out_ref[:, tile_ds(j, step)] = part.astype(BF)
            return carry

        lax.fori_loop(0, count // step, body, 0)

    project(q_ref, 0, q_width, True)
    project(k_ref, q_width, kv_width, True)
    project(v_ref, q_width + kv_width, kv_width, False)

    def pair_body(j, carry):
        k_block = k_ref[:, tile_ds(j, LANES)].astype(F32)
        v_block = v_ref[:, tile_ds(j, LANES)].astype(F32)
        for place in range(2):
            keys = head_pair(k_block, place)
            vals = head_pair(v_block, place)
            group = 2 * j + place
            q_block = q_ref[:, tile_ds(group, LANES)]
            out = None
            for side in range(2):
                scores = mm_nt(keys[side].astype(BF), q_block) * SCORE_SCALE + bias_ref[...]
                highest = jnp.max(scores, axis=0, keepdims=True)
                lifted = jnp.exp(scores - highest)
                total = jnp.sum(lifted, axis=0, keepdims=True)
                low = (lifted * (1.0 / total)).astype(BF)
                lse_ref[pl.ds(2 * group + side, 1), :] = highest + jnp.log(total)
                part = mm_tn(vals[side].astype(BF), low)
                out = part if out is None else out + part
            att_ref[:, tile_ds(group, LANES)] = out.T.astype(BF)
        return carry

    lax.fori_loop(0, KEY_VALUE_HEADS // 2, pair_body, 0)

    start = q_width + 2 * kv_width

    def out_body(j, total):
        cols = pl.ds(pl.multiple_of(start + j * step, step), step)
        here = tile_ds(j, step)
        value = x_ref[:, here].astype(F32) + RESIDUAL_SCALE * mm(att_ref[...], w_ref[:, cols])
        res_ref[:, here] = value
        return total + jnp.sum(value * value, axis=1, keepdims=True)

    square = lax.fori_loop(0, width // step, out_body, jnp.zeros((rows, 1), F32))
    scale = lax.rsqrt(square * (1.0 / width) + EPS)
    pay_ref[:rows, :] = (res_ref[...] * scale * gain_two_ref[...]).astype(BF)
    logits = mm(pay_ref[:rows, :], w_ref[:, start + width :])
    lanes = lane_iota(logits.shape)
    chosen = lanes < 0
    for k in range(picks_ref.shape[1]):
        chosen = chosen | (picks_ref[:, k : k + 1] == lanes)
    masked = jnp.where(chosen, logits, NEG_FILL)
    lifted = jnp.where(chosen, jnp.exp(masked - jnp.max(masked, axis=1, keepdims=True)), 0.0)
    gates = lifted / jnp.sum(lifted, axis=1, keepdims=True)
    across = gates.T[:experts, :]
    gate_ref[...] = across
    high = across.astype(BF)
    pay_ref[rows:, :rows] = high
    pay_ref[rows:, rows:] = (across - high.astype(F32)).astype(BF)


def attention_forward(x, pack, gain_one, gain_two, ids, picks, tables, q_width, kv_width, experts):
    rows, width = x.shape
    out_shape = (
        jax.ShapeDtypeStruct((rows, q_width), BF),
        jax.ShapeDtypeStruct((rows, kv_width), BF),
        jax.ShapeDtypeStruct((rows, kv_width), BF),
        jax.ShapeDtypeStruct((rows, q_width), BF),
        jax.ShapeDtypeStruct((QUERY_HEADS, rows), F32),
        jax.ShapeDtypeStruct((rows, width), F32),
        jax.ShapeDtypeStruct((rows + experts, width), BF),
        jax.ShapeDtypeStruct((experts, rows), F32),
    )
    flops = 2 * rows * width * (q_width + 2 * kv_width + width) + 8 * QUERY_HEADS * rows * rows * 128
    return pl.pallas_call(
        functools.partial(
            attention_forward_kernel, q_width=q_width, kv_width=kv_width, experts=experts
        ),
        out_shape=out_shape,
        scratch_shapes=[pltpu.VMEM((rows, width), BF), pltpu.VMEM((rows, rows), F32)],
        compiler_params=pltpu.CompilerParams(vmem_limit_bytes=VMEM_LIMIT),
        cost_estimate=hint(
            flops=flops, transcendentals=QUERY_HEADS * rows * rows, bytes_accessed=16 << 20
        ),
        name="attention_forward",
    )(x, pack, gain_one, gain_two, ids[None, :], ids[:, None], *tables, picks)


def slot_marks(sel_ref, gate_rows, upper_ref, local):
    picked = mm(sel_ref[...], gate_rows)
    rows = picked.shape[1] // 2
    gates = picked[:, :rows] + picked[:, rows:]
    used = gates != 0.0
    rank = mm(used.astype(F32).astype(BF), upper_ref[...])
    slots = jnp.where(used, rank, -1.0)
    places = lax.broadcasted_iota(jnp.int32, (CAP, rows), 0).astype(F32)
    hits = [places == slots[e : e + 1, :] for e in range(local)]
    return gates, hits


def fill_upper(upper_ref):
    rows = upper_ref.shape[0]
    upper = lax.broadcasted_iota(jnp.int32, (rows, rows), 0) < lane_iota((rows, rows))
    upper_ref[...] = jnp.where(upper, 1.0, 0.0).astype(BF)


def dispatch_kernel(sel_ref, pay_ref, grad_ref, *refs, local):
    rows_ref, slot_ref, upper_ref = refs[-3:]

    @pl.when(pl.program_id(0) == 0)
    def _():
        fill_upper(upper_ref)

    rows = grad_ref.shape[1]
    gates, hits = slot_marks(sel_ref, pay_ref[0, rows:, :], upper_ref, local)
    marks = jnp.concatenate([jnp.where(h, 1.0, 0.0).astype(BF) for h in hits], axis=0)
    column = jnp.concatenate(
        [
            jnp.sum(jnp.where(h, gates[e : e + 1, :], 0.0), axis=1, keepdims=True)
            for e, h in enumerate(hits)
        ],
        axis=0,
    )
    moved = mm(marks, pay_ref[0, :rows, :]).astype(BF)
    grads = (column * (RESIDUAL_SCALE * mm(marks, grad_ref[0]))).astype(BF)
    for e in range(local):
        rows_ref[e, 0, 0] = moved[e * CAP : (e + 1) * CAP]
        slot_ref[e, 0, 0] = grads[e * CAP : (e + 1) * CAP]


def dispatch(sel, pays, grads, place, places, local, carried):
    count, rows, width = grads.shape
    shape = jax.ShapeDtypeStruct((local, places, count, CAP, width), BF)
    out_spec = pl.BlockSpec((local, 1, 1, CAP, width), lambda s: (0, place, s, 0, 0))
    in_specs = [
        pl.BlockSpec(sel.shape, lambda s: (0, 0)),
        pl.BlockSpec((1,) + pays.shape[1:], lambda s: (s, 0, 0)),
        pl.BlockSpec((1, rows, width), lambda s: (s, 0, 0)),
    ]
    operands = [sel, pays, grads]
    aliases = {}
    if carried is not None:
        operands += list(carried)
        in_specs += [pl.BlockSpec(memory_space=pl.ANY)] * 2
        aliases = {3: 0, 4: 1}
    return pl.pallas_call(
        functools.partial(dispatch_kernel, local=local),
        out_shape=(shape, shape),
        grid=(count,),
        in_specs=in_specs,
        out_specs=(out_spec, out_spec),
        scratch_shapes=[pltpu.VMEM((rows, rows), BF)],
        input_output_aliases=aliases,
        compiler_params=pltpu.CompilerParams(vmem_limit_bytes=VMEM_LIMIT),
        cost_estimate=hint(
            flops=4 * count * local * CAP * rows * width, transcendentals=0, bytes_accessed=20 << 20
        ),
        name="dispatch",
    )(*operands)


def expert_kernel(x_ref, s_ref, w_ref, *refs, chunk, tile, last, carried):
    if carried:
        prior_ref, refs = refs[0], refs[1:]
    (
        pr_ref, dg_ref, dot_ref, grad_ref,
        gate_ref, up_ref, down_ref, act_ref, both_ref, acc_in_ref, acc_down_ref,
    ) = refs
    rows, width = x_ref.shape[-2:]
    hidden = gate_ref.shape[-1]
    owners = grad_ref.shape[0]
    in_rows, down_rows = width // owners, hidden // owners
    step = pl.program_id(1)
    pieces = width // hidden

    @pl.when(step == 0)
    def _():
        for o in range(owners):
            gate_ref[o * in_rows : (o + 1) * in_rows, :] = w_ref[o, 0, :in_rows, :]
            up_ref[o * in_rows : (o + 1) * in_rows, :] = w_ref[o, 0, in_rows : 2 * in_rows, :]
            for c in range(pieces):
                first = 2 * in_rows + c * down_rows
                down_ref[o * down_rows : (o + 1) * down_rows, c * hidden : (c + 1) * hidden] = w_ref[
                    o, 0, first : first + down_rows, :
                ]

    def chunk_body(c, carry):
        here = tile_ds(c, chunk)
        x = x_ref[0, here, :]
        s = s_ref[0, here, :]
        pre_gate = mm(x, gate_ref[...])
        pre_up = mm(x, up_ref[...])
        act_grad = mm_nt(s, down_ref[...])
        logistic = jax.nn.sigmoid(pre_gate)
        swish = pre_gate * logistic
        act = (swish * pre_up).astype(BF)
        gate_in = (
            act_grad * pre_up * logistic * (1.0 + pre_gate * (1.0 - logistic))
        ).astype(BF)
        up_in = (act_grad * swish).astype(BF)
        dot_ref[0, here, :] = jnp.sum(act.astype(F32) * act_grad, axis=1, keepdims=True)
        act_ref[here, :] = act
        both_ref[here, :hidden] = gate_in
        both_ref[here, hidden:] = up_in
        pr_ref[0, here, :] = mm(act, down_ref[...]).astype(BF)
        dg_ref[0, here, :] = (mm_nt(gate_in, gate_ref[...]) + mm_nt(up_in, up_ref[...])).astype(BF)
        return carry

    lax.fori_loop(0, rows // chunk, chunk_body, 0)

    def put(owner, first, value):
        count = value.shape[0]
        if carried:
            value = value + prior_ref[owner, 0, first : first + count, :].astype(F32)
        grad_ref[owner, 0, first : first + count, :] = value.astype(BF)

    def accumulate(acc_ref, here, part, emit):
        if last == 0:
            emit(part)
            return

        @pl.when(step == 0)
        def _():
            acc_ref[here, :] = part

        if last > 1:

            @pl.when((step > 0) & (step < last))
            def _():
                acc_ref[here, :] = acc_ref[here, :] + part

        @pl.when(step == last)
        def _():
            emit(acc_ref[here, :] + part)

    def in_body(t, carry):
        here = tile_ds(t, tile)

        def emit(total):
            for i in range(tile // in_rows):
                piece = total[i * in_rows : (i + 1) * in_rows]
                owner = t * (tile // in_rows) + i
                put(owner, 0, piece[:, :hidden])
                put(owner, in_rows, piece[:, hidden:])

        accumulate(acc_in_ref, here, mm_tn(x_ref[0, :, here], both_ref[...]), emit)
        return carry

    lax.fori_loop(0, width // tile, in_body, 0)

    def down_body(t, carry):
        here = tile_ds(t, tile)

        def emit(total):
            for i in range(tile // down_rows):
                piece = total[i * down_rows : (i + 1) * down_rows]
                owner = t * (tile // down_rows) + i
                for c in range(pieces):
                    put(owner, 2 * in_rows + c * down_rows, piece[:, c * hidden : (c + 1) * hidden])

        accumulate(acc_down_ref, here, mm_tn(act_ref[:, here], s_ref[0]), emit)
        return carry

    lax.fori_loop(0, hidden // tile, down_body, 0)


def experts_step(first, weights, rows_in, slot_grad, prior):
    owners, count, packed, hidden = weights.shape
    _, total, width = rows_in.shape
    rows = 8 * CAP
    steps = total // rows
    out_shape = (
        jax.ShapeDtypeStruct((count, total, width), BF),
        jax.ShapeDtypeStruct((count, total, width), BF),
        jax.ShapeDtypeStruct((count, total, 1), F32),
        jax.ShapeDtypeStruct(weights.shape, BF),
    )
    in_spec = pl.BlockSpec((1, rows, width), lambda e, t: (first + e, t, 0))
    pack_spec = pl.BlockSpec((owners, 1, packed, hidden), lambda e, t: (0, e, 0, 0))
    row_spec = lambda last: pl.BlockSpec((1, rows, last), lambda e, t: (e, t, 0))
    operands = [rows_in, slot_grad, weights]
    in_specs = [in_spec, in_spec, pack_spec]
    if prior is not None:
        operands.append(prior)
        in_specs.append(pack_spec)
    kept = 0 if steps == 1 else 1
    return pl.pallas_call(
        functools.partial(
            expert_kernel, chunk=rows // 3, tile=256, last=steps - 1, carried=prior is not None
        ),
        out_shape=out_shape,
        grid=(count, steps),
        in_specs=in_specs,
        out_specs=(row_spec(width), row_spec(width), row_spec(1), pack_spec),
        scratch_shapes=[
            pltpu.VMEM((width, hidden), BF),
            pltpu.VMEM((width, hidden), BF),
            pltpu.VMEM((hidden, width), BF),
            pltpu.VMEM((rows, hidden), BF),
            pltpu.VMEM((rows, 2 * hidden), BF),
            pltpu.VMEM((width, 2 * hidden) if kept else (8, LANES), F32),
            pltpu.VMEM((hidden, width) if kept else (8, LANES), F32),
        ],
        compiler_params=pltpu.CompilerParams(vmem_limit_bytes=VMEM_LIMIT),
        cost_estimate=hint(
            flops=18 * count * total * width * hidden, transcendentals=count * total * hidden,
            bytes_accessed=30 << 20, share=16 if prior is None else 1,
        ),
        name="experts",
    )(*operands)


def combine_kernel(sel_ref, pay_ref, *refs, groups, local, received):
    produced, returned, dots = (refs[i * groups : (i + 1) * groups] for i in range(3))
    rest = refs[3 * groups :]
    if received:
        other_ref, rest = rest[0], rest[1:]
    out_refs, upper_ref = rest[:-1], rest[-1]
    each = local // groups

    @pl.when(pl.program_id(0) == 0)
    def _():
        fill_upper(upper_ref)

    rows = upper_ref.shape[0]
    gates, hits = slot_marks(sel_ref, pay_ref[0], upper_ref, local)
    weighted = jnp.concatenate(
        [jnp.where(h, gates[e : e + 1, :], 0.0).astype(BF) for e, h in enumerate(hits)], axis=0
    )
    plain = jnp.concatenate([jnp.where(h, 1.0, 0.0).astype(BF) for h in hits], axis=0)
    made = jnp.concatenate([r[e, 0] for r in produced for e in range(each)], axis=0)
    back = jnp.concatenate([r[e, 0] for r in returned for e in range(each)], axis=0)
    out = mm_tn(weighted, made)
    grads = mm_tn(plain, back)
    pad = jnp.zeros((8 - local, rows), F32)
    dot_rows = jnp.concatenate(
        [
            jnp.sum(jnp.where(h, dots[e // each][e % each, 0], 0.0), axis=0, keepdims=True)
            for e, h in enumerate(hits)
        ]
        + ([pad] if local < 8 else []),
        axis=0,
    )
    high = dot_rows.astype(BF)
    low = (dot_rows - high.astype(F32)).astype(BF)
    tail = jnp.concatenate([mm_tn(sel_ref[...], high), mm_tn(sel_ref[...], low)], axis=1)
    half = tail.shape[0] // 2
    first = jnp.concatenate([out, tail[:half]], axis=0)
    second = jnp.concatenate([tail[half:], grads], axis=0)
    if received:
        first = first + other_ref[0, : rows + half, :].astype(F32)
        second = second + other_ref[0, rows + half :, :].astype(F32)

        def put(index):
            out_refs[2 * index][...] = first.astype(BF)
            out_refs[2 * index + 1][...] = second.astype(BF)

        for index in range(len(out_refs) // 2):
            pl.when(pl.program_id(0) == index)(functools.partial(put, index))
    else:
        out_refs[0][0, : rows + half, :] = first.astype(BF)
        out_refs[0][0, rows + half :, :] = second.astype(BF)


def combine(sel, pays, produced, returned, dots, side, other):
    count, total_rows, width = pays.shape
    groups, each = len(produced), produced[0].shape[0]
    local = groups * each
    experts = sel.shape[1]
    rows = total_rows - experts
    pick = lambda last: pl.BlockSpec((each, 1, CAP, last), lambda s: (0, side * count + s, 0, 0))
    in_specs = [
        pl.BlockSpec(sel.shape, lambda s: (0, 0)),
        pl.BlockSpec((1, experts, width), lambda s: (s, rows // experts, 0)),
    ]
    in_specs += [pick(width)] * (2 * groups) + [pick(1)] * groups
    operands = [sel, pays, *produced, *returned, *dots]
    total = 2 * rows + experts
    out_spec = pl.BlockSpec((1, total, width), lambda s: (s, 0, 0))
    out_shape = (jax.ShapeDtypeStruct((count, total, width), BF),)
    out_specs = (out_spec,)
    if other is not None:
        operands.append(other)
        in_specs.append(out_spec)
        out_shape = (jax.ShapeDtypeStruct((total // 2, width), BF),) * (2 * count)
        out_specs = (pl.BlockSpec((total // 2, width), lambda s: (0, 0)),) * (2 * count)
    return pl.pallas_call(
        functools.partial(combine_kernel, groups=groups, local=local, received=other is not None),
        out_shape=out_shape,
        grid=(count,),
        in_specs=in_specs,
        out_specs=out_specs,
        scratch_shapes=[pltpu.VMEM((rows, rows), BF)],
        compiler_params=pltpu.CompilerParams(vmem_limit_bytes=VMEM_LIMIT),
        cost_estimate=hint(
            flops=4 * count * local * CAP * rows * width, transcendentals=0, bytes_accessed=20 << 20, share=1
        ),
        name="combine",
    )(*operands)


def attention_backward_kernel(
    *refs, terms, q_width, kv_width, experts, carried,
):
    (
        x_ref, w_ref, gain_one_ref, gain_two_ref, id_row_ref, id_col_ref, cos_ref, sin_ref,
        grad_ref, q_ref, k_ref, v_ref, att_ref, lse_ref, res_ref, pay_ref, gate_ref,
    ) = refs[:17]
    term_refs = refs[17 : 17 + 2 * terms]
    rest = refs[17 + 2 * terms :]
    if carried:
        prior_ref, rest = rest[0], rest[1:]
    out_ref, in_grad_ref, pack_ref, bias_ref, wide_ref, att_grad_ref, qkv_grad_ref, branch_ref, normed_ref = rest
    rows, width = x_ref.shape
    step = 256
    start = q_width + 2 * kv_width

    def put(row_slice, cols, value):
        if carried:
            value = value + prior_ref[row_slice, cols].astype(F32)
        pack_ref[row_slice, cols] = value.astype(BF)

    def gathered(which, low, high):
        total = term_refs[which][low:high, :].astype(F32)
        for ref in term_refs[2 + which :: 2]:
            total = total + ref[low:high, :].astype(F32)
        return total

    half = experts // 2
    residual = res_ref[...]
    out_ref[...] = (residual + RESIDUAL_SCALE * gathered(0, 0, rows)).astype(BF)
    tail = jnp.concatenate([gathered(0, rows, rows + half), gathered(1, 0, half)], axis=0)
    weighted = tail[:, :rows] + tail[:, rows:]
    chosen = weighted - gate_ref[...] * jnp.sum(weighted, axis=0, keepdims=True)
    chosen = jnp.concatenate([chosen, jnp.zeros((LANES - experts, rows), F32)], axis=0)
    logit_grad = chosen.T.astype(BF)
    moe_grad = gathered(1, half, half + rows) + mm_nt(logit_grad, w_ref[:, start + width :])
    last = mm_tn(pay_ref[:rows, :], logit_grad)
    scale = lax.rsqrt(jnp.mean(residual * residual, axis=1, keepdims=True) + EPS)
    gain_two_grad = jnp.sum(moe_grad * residual * scale, axis=0, keepdims=True)
    u = moe_grad * gain_two_ref[...]
    inner = jnp.sum(u * residual, axis=1, keepdims=True) * (1.0 / width)
    res_grad = grad_ref[...].astype(F32) + scale * u - residual * (scale * scale * scale * inner)
    in_grad_ref[...] = res_grad
    branch_ref[...] = (RESIDUAL_SCALE * res_grad).astype(BF)
    bias_ref[...] = jnp.where(id_col_ref[...] <= id_row_ref[...], 0.0, NEG_FILL)

    def branch_body(j, carry):
        here = tile_ds(j, step)
        att_grad_ref[:, here] = mm_nt(
            branch_ref[...], w_ref[here, start : start + width]
        ).astype(BF)
        part = mm_tn(att_ref[:, here], branch_ref[...])
        put(here, slice(start, start + width), part)
        return carry

    lax.fori_loop(0, q_width // step, branch_body, 0)

    lower = lane_iota((rows, LANES)) < HEAD_SIZE

    def pair_body(j, carry):
        k_block = k_ref[:, tile_ds(j, LANES)].astype(F32)
        v_block = v_ref[:, tile_ds(j, LANES)].astype(F32)
        k_sums, v_sums = [], []
        for place in range(2):
            keys = [h.astype(BF) for h in head_pair(k_block, place)]
            vals = [h.astype(BF) for h in head_pair(v_block, place)]
            group = 2 * j + place
            here = tile_ds(group, LANES)
            q_block = q_ref[:, here]
            g_block = att_grad_ref[:, here]
            q_out = None
            k_parts, v_parts = [], []
            for side in range(2):
                scores = mm_nt(keys[side], q_block) * SCORE_SCALE + bias_ref[...]
                probs = jnp.exp(scores - lse_ref[pl.ds(2 * group + side, 1), :])
                weight_grad = mm_nt(vals[side], g_block)
                v_parts.append(mm(probs.astype(BF), g_block))
                dots = jnp.sum(probs * weight_grad, axis=0, keepdims=True)
                score_grad = (probs * (weight_grad - dots)).astype(BF)
                k_parts.append(mm(score_grad, q_block))
                part = mm_tn(keys[side], score_grad)
                q_out = part if q_out is None else q_out + part
            q_turned = turn(q_out.T * SCORE_SCALE, cos_ref[...], -sin_ref[...])
            qkv_grad_ref[:, here] = q_turned.astype(BF)
            for parts, sums in ((k_parts, k_sums), (v_parts, v_sums)):
                mixed = jnp.where(lower, parts[0], parts[1])
                sums.append(mixed + pltpu.roll(mixed, HEAD_SIZE, 1))
        k_total = jnp.where(lower, k_sums[0], k_sums[1]) * SCORE_SCALE
        v_total = jnp.where(lower, v_sums[0], v_sums[1])
        k_here = pl.ds(pl.multiple_of(q_width + j * LANES, LANES), LANES)
        v_here = pl.ds(pl.multiple_of(q_width + kv_width + j * LANES, LANES), LANES)
        qkv_grad_ref[:, k_here] = turn(k_total, cos_ref[...], -sin_ref[...]).astype(BF)
        qkv_grad_ref[:, v_here] = v_total.astype(BF)
        return carry

    lax.fori_loop(0, KEY_VALUE_HEADS // 2, pair_body, 0)

    x = x_ref[...].astype(F32)
    scale = lax.rsqrt(jnp.mean(x * x, axis=1, keepdims=True) + EPS)
    normed_ref[...] = (x * scale * gain_one_ref[...]).astype(BF)

    def norm_body(j, carry):
        here = tile_ds(j, step)
        grad = mm_nt(qkv_grad_ref[...], w_ref[here, :start])
        put(here, slice(0, start), mm_tn(normed_ref[:, here], qkv_grad_ref[...]))
        wide_ref[:, here] = grad
        return carry

    lax.fori_loop(0, width // step, norm_body, 0)
    normed_grad = wide_ref[...]
    gain_one_grad = jnp.sum(normed_grad * x * scale, axis=0, keepdims=True)
    u = normed_grad * gain_one_ref[...]
    inner = jnp.sum(u * x, axis=1, keepdims=True) * (1.0 / width)
    in_grad_ref[...] = in_grad_ref[...] + scale * u - x * (scale * scale * scale * inner)
    lanes = lane_iota((width, LANES))
    one = jnp.broadcast_to(gain_one_grad, (LANES, width)).T
    two = jnp.broadcast_to(gain_two_grad, (LANES, width)).T
    last = jnp.where(lanes == experts, one, last)
    last = jnp.where(lanes == experts + 1, two, last)
    put(slice(0, width), slice(start + width, start + width + LANES), last)


def attention_backward(
    x, pack, gain_one, gain_two, ids, tables, grad, saved, terms, prior, q_width, kv_width, experts
):
    rows, width = x.shape
    operands = [x, pack, gain_one, gain_two, ids[None, :], ids[:, None], *tables, grad, *saved, *terms]
    if prior is not None:
        operands.append(prior)
    flops = 4 * rows * width * (q_width + 2 * kv_width + width) + 20 * QUERY_HEADS * rows * rows * 128
    return pl.pallas_call(
        functools.partial(
            attention_backward_kernel, terms=len(terms) // 2, q_width=q_width, kv_width=kv_width,
            experts=experts, carried=prior is not None,
        ),
        out_shape=(
            jax.ShapeDtypeStruct((rows, width), BF),
            jax.ShapeDtypeStruct((rows, width), F32),
            jax.ShapeDtypeStruct(pack.shape, BF),
        ),
        scratch_shapes=[
            pltpu.VMEM((rows, rows), F32),
            pltpu.VMEM((rows, width), F32),
            pltpu.VMEM((rows, q_width), BF),
            pltpu.VMEM((rows, q_width + 2 * kv_width), BF),
            pltpu.VMEM((rows, width), BF),
            pltpu.VMEM((rows, width), BF),
        ],
        compiler_params=pltpu.CompilerParams(vmem_limit_bytes=VMEM_LIMIT),
        cost_estimate=hint(
            flops=flops, transcendentals=QUERY_HEADS * rows * rows, bytes_accessed=40 << 20, share=1
        ),
        name="attention_backward",
    )(*operands)


def peer_chip(chip, distance):
    total = 0
    for bit in (1, 2, 4):
        total = total + bit * ((chip // bit + (distance // bit) % 2) % 2)
    return total


def where_am_i():
    f, d = lax.axis_index("fsdp"), lax.axis_index("dp")
    return f // 2, f % 2, d


def meet(peers):
    barrier = pltpu.get_barrier_semaphore()
    for peer in peers:
        pl.semaphore_signal(
            barrier, inc=1, device_id=peer, device_id_type=pl.DeviceIdType.MESH
        )
    pl.semaphore_wait(barrier, len(peers))


def push(src, dst, send, receive, peer):
    copy = pltpu.make_async_remote_copy(
        src_ref=src, dst_ref=dst, send_sem=send, recv_sem=receive, device_id=peer,
        device_id_type=pl.DeviceIdType.MESH,
    )
    copy.start()
    return copy


def gather_layer_kernel(
    w_ref, out_ref, own_sem, z_send, z_receive, x_send, x_receive, s_send, s_receive, *, chips, depth
):
    chip, core, d = where_am_i()
    rows = w_ref.shape[0]
    others = [peer_chip(chip, r) for r in range(1, chips)]
    f, sibling = chip * 2 + core, chip * 2 + 1 - core

    def block(owner, layer):
        first = pl.multiple_of((owner * depth + layer) * rows, rows)
        return out_ref.at[pl.ds(first, rows), :]

    peers = [(f, (d + i) % depth) for i in range(1, depth)]
    peers += [(c * 2 + core, d) for c in others] + [(sibling, d)]
    meet(peers)
    own = pltpu.make_async_copy(w_ref, block(f, d), own_sem)
    own.start()
    z_copies = [
        push(w_ref, block(f, d), z_send.at[i - 1], z_receive.at[i - 1], (f, (d + i) % depth))
        for i in range(1, depth)
    ]
    x_copies, s_copies = [], []
    layers = [(d + depth - i) % depth for i in range(depth)]
    for i, layer in enumerate(layers):
        if i:
            z_copies[i - 1].wait_recv()
        src = block(f, layer) if i else w_ref
        for r, c in enumerate(others):
            x_copies.append(
                push(src, block(f, layer), x_send.at[i, r], x_receive.at[i, r], (c * 2 + core, d))
            )
        s_copies.append(
            push(src, block(f, layer), s_send.at[i, 0], s_receive.at[i, 0], (sibling, d))
        )
    for i, layer in enumerate(layers):
        for r, c in enumerate(others):
            x_copies[i * (chips - 1) + r].wait_recv()
            there = block(c * 2 + core, layer)
            s_copies.append(
                push(there, there, s_send.at[i, r + 1], s_receive.at[i, r + 1], (sibling, d))
            )
    own.wait()
    for copy in z_copies + x_copies:
        copy.wait_send()
    for copy in s_copies:
        copy.wait()


def gather_layer(pack, chips, depth):
    dma = pltpu.SemaphoreType.DMA
    rows, width = pack.shape
    return pl.pallas_call(
        functools.partial(gather_layer_kernel, chips=chips, depth=depth),
        out_shape=jax.ShapeDtypeStruct((rows * 2 * chips * depth, width), pack.dtype),
        in_specs=[pl.BlockSpec(memory_space=pl.ANY)],
        out_specs=pl.BlockSpec(memory_space=pl.ANY),
        scratch_shapes=[
            dma(()), dma((depth - 1,)), dma((depth - 1,)), dma((depth, chips - 1)),
            dma((depth, chips - 1)), dma((depth, chips)), dma((depth, chips)),
        ],
        compiler_params=pltpu.CompilerParams(collective_id=1, has_side_effects=True),
        name="gather_layer",
    )(pack)


def reduce_layer_kernel(
    pack_ref, out_ref, s_buf, s_sum, x_buf, x_sum, z_buf,
    s_send, s_receive, x_send, x_receive, z_send, z_receive,
    *, chips, depth, parts,
):
    chip, core, d = where_am_i()
    total, width = pack_ref.shape
    rows = total // (2 * chips * depth)
    span = rows * depth
    step = width // parts
    distances = list(range(1, chips))
    others = [peer_chip(chip, r) for r in distances]
    f, sibling = chip * 2 + core, chip * 2 + 1 - core
    peers = [(f, (d + i) % depth) for i in range(1, depth)]
    peers += [(c * 2 + core, d) for c in others] + [(sibling, d)]
    meet(peers)

    def band(p):
        return slice(p * step, (p + 1) * step)

    def mine(c, k):
        return pl.ds(pl.multiple_of((c * 2 + k) * span, span), span)

    order = [(r, c) for r, c in zip(distances, others)][::-1] + [(0, chip)]
    s_copies = {}
    for p in range(parts):
        for r, c in order:
            s_copies[p, r] = push(
                pack_ref.at[mine(c, 1 - core), band(p)], s_buf.at[r, :, band(p)],
                s_send.at[p, r], s_receive.at[p, r], (sibling, d),
            )
    x_copies, z_copies = {}, {}

    def sum_chip(p):
        for r, c in order:
            s_copies[p, r].wait_recv()
            value = pack_ref[mine(c, core), band(p)].astype(F32) + s_buf[r, :, band(p)].astype(F32)
            s_sum[r, :, band(p)] = value.astype(s_sum.dtype)

    def send_chip(p):
        for r, c in order[:-1]:
            x_copies[p, r] = push(
                s_sum.at[r, :, band(p)], x_buf.at[r - 1, :, band(p)], x_send.at[p, r - 1],
                x_receive.at[p, r - 1], (c * 2 + core, d),
            )

    def sum_plane(p):
        value = s_sum[0, :, band(p)].astype(F32)
        for r in distances:
            x_copies[p, r].wait_recv()
            value = value + x_buf[r - 1, :, band(p)].astype(F32)
        x_sum[:, :, band(p)] = value.reshape(depth, rows, step).astype(x_sum.dtype)

    def send_plane(p):
        for i in range(1, depth):
            to = (d + i) % depth
            z_copies[p, i] = push(
                x_sum.at[to, :, band(p)], z_buf.at[i - 1, :, band(p)], z_send.at[p, i - 1],
                z_receive.at[p, i - 1], (f, to),
            )

    def finish(p):
        value = x_sum[d, :, band(p)].astype(F32)
        for i in range(1, depth):
            z_copies[p, i].wait_recv()
            value = value + z_buf[i - 1, :, band(p)].astype(F32)
        out_ref[:, band(p)] = value

    for p in range(parts + 1):
        if p < parts:
            sum_chip(p)
        if p > 0:
            send_chip(p - 1)
    for p in range(parts + 1):
        if p < parts:
            sum_plane(p)
        if p > 0:
            send_plane(p - 1)
    for p in range(parts):
        finish(p)
    for copy in [*s_copies.values(), *x_copies.values(), *z_copies.values()]:
        copy.wait_send()


def reduce_layer(pack, chips, depth, parts):
    dma = pltpu.SemaphoreType.DMA
    total, width = pack.shape
    rows = total // (2 * chips * depth)
    kind = BF if rows % 16 == 0 else F32
    return pl.pallas_call(
        functools.partial(reduce_layer_kernel, chips=chips, depth=depth, parts=parts),
        out_shape=jax.ShapeDtypeStruct((rows, width), F32),
        in_specs=[pl.BlockSpec(memory_space=pltpu.VMEM)],
        out_specs=pl.BlockSpec(memory_space=pltpu.VMEM),
        scratch_shapes=[
            pltpu.VMEM((chips, rows * depth, width), BF),
            pltpu.VMEM((chips, rows * depth, width), BF),
            pltpu.VMEM((chips - 1, rows * depth, width), BF),
            pltpu.VMEM((depth, rows, width), kind),
            pltpu.VMEM((depth - 1, rows, width), kind),
            dma((parts, chips)), dma((parts, chips)), dma((parts, chips - 1)), dma((parts, chips - 1)),
            dma((parts, depth - 1)), dma((parts, depth - 1)),
        ],
        compiler_params=pltpu.CompilerParams(
            collective_id=2, has_side_effects=True, vmem_limit_bytes=VMEM_LIMIT
        ),
        cost_estimate=pl.CostEstimate(flops=0, transcendentals=0, bytes_accessed=1 << 30),
        name="reduce_layer",
    )(pack)


def swap(value, distance, size):
    return lax.ppermute(value, "fsdp", [(i, i ^ distance) for i in range(size)])


def after(value, *earlier):
    return lax.optimization_barrier((value, *earlier))[0] if earlier else value


def send_near(value, size):
    return swap(value, 2, size), swap(value, 4, size)


def gather_chips(value, near, size):
    chips = size // 2
    if near is None:
        return [value] + [swap(value, 2 * r, size) for r in range(1, chips)]
    half = value.shape[0] // 2
    one, two = near
    return [value, one, two, swap(one[:half], 4, size), swap(two[half:], 2, size)]


def both_cores(pieces, size, *earlier):
    if earlier:
        pieces = [pieces[0]] + [after(p, *earlier) for p in pieces[1:]]
    chips = size // 2
    mine = jnp.stack(pieces[: chips - 1] + [jnp.concatenate(pieces[chips - 1 :])])
    return mine, swap(mine, 1, size)


def scatter_near(kept, size, *earlier):
    chips = size // 2
    if chips != 4:
        return [swap(kept[2 * r + h], 2 * r, size) for r in range(1, chips) for h in range(2)]
    return [swap(after(kept[6], *earlier), 2, size), swap(after(kept[7], *earlier), 4, size)]


def scatter_far(kept, near, size, *earlier):
    if size != 8:
        return (), ()
    add = lambda a, b: (a.astype(F32) + b.astype(F32)).astype(BF)
    by_one, by_two = after(near[0], *earlier), after(near[1], *earlier)
    one_sum, two_sum = add(kept[3], by_two), add(kept[4], by_one)
    return (one_sum, two_sum), (swap(one_sum, 2, size), swap(two_sum, 4, size))


def scatter_rest(kept, size, *earlier):
    if size != 8:
        return ()
    return swap(after(kept[2], *earlier), 2, size), swap(after(kept[5], *earlier), 4, size)


def scattered(kept, near, far, rest):
    if not far:
        return [kept[0], kept[1]] + near
    return [kept[0], kept[1], rest[0], far[0], far[1], rest[1]]


def local(
    inputs, block_ids, routes, out_grad, norm_gain, w_query, key_weight, value_weight, w_output,
    moe_gain, w_router, w_gate, w_up, w_down,
):
    micro, _, rows, width = inputs.shape
    experts = w_router.shape[1]
    held, in_rows, hidden = w_gate.shape
    down_rows = w_down.shape[1]
    q_width, kv_width = w_query.shape[1], key_weight.shape[1]
    owners = lax.axis_size("fsdp")
    depth = lax.axis_size("dp")
    chips = owners // 2
    tables = tuple(jnp.asarray(t) for t in rope_tables(rows))
    start = q_width + 2 * kv_width + width
    group = max(1, held // 2)
    cuts = width // hidden

    split_down = w_down.reshape(held, down_rows, cuts, hidden).transpose(0, 2, 1, 3)
    packed = jnp.concatenate(
        [w_gate, w_up, split_down.reshape(held, cuts * down_rows, hidden)], axis=1
    )
    weights = [
        lax.all_gather(packed[g : g + group], "dp", axis=0, tiled=False)
        for g in range(0, held, group)
    ]
    pieces = [
        w_query, key_weight, value_weight, w_output, w_router, norm_gain[:, None], moe_gain[:, None]
    ]
    filled = sum(p.shape[1] for p in pieces)
    pieces.append(jnp.zeros((w_query.shape[0], start + LANES - filled), BF))
    pack = gather_layer(jnp.concatenate(pieces, axis=1), chips, depth)
    gain_one = pack[:, start + experts].astype(F32)[None, :]
    gain_two = pack[:, start + experts + 1].astype(F32)[None, :]
    first = lax.axis_index("fsdp") * held
    places = jnp.arange(8)[:, None]
    sel = ((jnp.arange(experts)[None, :] == first + places) & (places < held)).astype(BF)
    square = chips == 4

    def forward(m, x):
        return attention_forward(
            x, pack, gain_one, gain_two, block_ids[m, 0], routes[m, 0], tables, q_width, kv_width, experts
        )

    def dispatched(m, pay, grad):
        carried = None
        for side in range(2):
            carried = dispatch(sel, pay[side], grad[side], side, 2, held, carried)
        return [c.reshape(held, 2 * chips * CAP, width) for c in carried]

    saved, arrived, pays, moved, done, terms = [], [], [], [], {}, []
    ready = ()
    for m in range(micro):
        grad = after(out_grad[m, 0], *ready)
        grad_near = send_near(grad, owners) if square else None
        if m == 0:
            saved.append(forward(0, after(inputs[0, 0], *(grad_near if square else ()))))
            for n in range(1, micro):
                saved.append(forward(n, after(inputs[n, 0], saved[n - 1][4])))
        pay = saved[m][6]
        pay_near = None
        if square and m == 0:
            one, two = send_near(pay, owners)
            ready = (one,)
            pay_near = after(one, saved[-1][4]), after(two, saved[-1][4])
        elif m:
            pay = after(pay, *arrived[m - 1][0][1:])
            ready = (pay,)
        arrived.append((gather_chips(pay, pay_near, owners), gather_chips(grad, grad_near, owners), grad_near))

    def expert_part(m, g, *earlier):
        prior = done[m - 1, g][3] if m else None
        rows_in, slot_grad = moved[m]
        if earlier:
            rows_in = after(rows_in, *earlier)
        done[m, g] = experts_step(g * group, weights[g], rows_in, slot_grad, prior)

    def returned(m, earlier):
        parts = [
            [done[m, g][i].reshape(group, 2 * chips, CAP, -1) for g in range(len(weights))]
            for i in range(3)
        ]
        (sent,) = combine(sel, after(pays[m][1], *earlier), *parts, 1, None)
        return combine(sel, pays[m][0], *parts, 0, swap(sent, 1, owners))

    outputs, input_grads = [], []

    def backward(m, found, prior):
        out, in_grad, prior = attention_backward(
            inputs[m, 0], pack, gain_one, gain_two, block_ids[m, 0], tables, out_grad[m, 0], saved[m],
            found, prior, q_width, kv_width, experts,
        )
        outputs.append(out)
        input_grads.append(in_grad)
        return prior

    added, far, rest = (), (), ()
    for m in range(micro):
        held_back = (done[m - 1, 0][2],) if m else ()
        pay_held = arrived[m + 1][2] if m == 0 and micro > 1 and square else held_back
        pays.append(both_cores(arrived[m][0], owners, *pay_held))
        moved.append(dispatched(m, pays[m], both_cores(arrived[m][1], owners, *held_back)))
        hold = arrived[m + 1][2] if m + 1 < micro and square else ()
        if m == 0:
            expert_part(0, 0, *hold)
        else:
            for g in range(1, len(weights)):
                expert_part(m - 1, g, moved[m][0])
            kept = returned(m - 1, far)
            near = scatter_near(kept, owners, *rest)
            expert_part(m, 0, kept[-1])
            added, far = scatter_far(kept, near, owners, done[m, 0][2])
            rest = scatter_rest(kept, owners, *far)
            terms.append(scattered(kept, near, far, rest))
    for g in range(1, len(weights)):
        expert_part(micro - 1, g, *added)
    kept = returned(micro - 1, far)
    near = scatter_near(kept, owners, *rest)
    last_rest = scatter_rest(kept, owners, *rest)
    prior, held_back = None, ()
    for m in range(micro - 1):
        prior = backward(m, [after(terms[m][0], kept[-1])] + terms[m][1:], prior)
        held_back = (prior,)
    last_far = scatter_far(kept, near, owners, *held_back)[1]
    terms.append(scattered(kept, near, last_far, last_rest))
    prior = backward(micro - 1, terms[-1], prior)
    sums = []
    for g in range(len(weights)):
        summed = after(done[micro - 1, g][3], *(far if g else added))
        sums.append(lax.psum_scatter(summed, "dp", scatter_dimension=0, tiled=True)[0])
    layer = reduce_layer(prior, chips, depth, 5)
    marks = np.cumsum([0, q_width, kv_width, kv_width, width, experts, 1, 1])
    cut = [layer[:, a:b] for a, b in zip(marks[:-1], marks[1:])]
    stacked = jnp.concatenate(sums, axis=0).astype(F32)
    grad_down = stacked[:, 2 * in_rows :].reshape(held, cuts, down_rows, hidden)
    grad_down = grad_down.transpose(0, 2, 1, 3).reshape(held, down_rows, width)
    return (
        jnp.stack(outputs)[:, None],
        jnp.stack(input_grads)[:, None],
        cut[5][:, 0], cut[0], cut[1], cut[2], cut[3], cut[6][:, 0], cut[4],
        stacked[:, :in_rows], stacked[:, in_rows : 2 * in_rows], grad_down,
    )


def solution(mesh):
    rows = ("fsdp", "dp")
    split = lambda rank: P(None, rows, *([None] * (rank - 2)))
    flat = P(rows, None)
    expert_spec = P("fsdp", "dp", None)
    in_specs = (
        split(4), split(3), split(4), split(4), P(rows), flat, flat, flat, flat, P(rows), flat,
        expert_spec, expert_spec, expert_spec,
    )
    out_specs = (
        split(4), split(4), P(rows), flat, flat, flat, flat, P(rows), flat,
        expert_spec, expert_spec, expert_spec,
    )
    return jax.shard_map(local, mesh=mesh, in_specs=in_specs, out_specs=out_specs, check_vma=False)
```

```python
import functools

import jax
import jax.numpy as jnp
import numpy as np
from jax import lax
from jax.experimental import pallas as pl
from jax.experimental.pallas import tpu as pltpu
from jax.sharding import PartitionSpec as P

QUERY_HEADS = 16
KEY_VALUE_HEADS = 8
HEAD_SIZE = 64
CAP = 144
EPS = 1e-06
RESIDUAL_SCALE = 0.22
SCORE_SCALE = 0.015625
THETA = 10000.0
NEG_FILL = -1e30
LANES = 128

BF = jnp.bfloat16
F32 = jnp.float32
VMEM_LIMIT = 64 * 1024 * 1024 - 128 * 1024


def mm(a, b):
    return jnp.dot(a, b, preferred_element_type=F32)


def mm_nt(a, b):
    return lax.dot_general(a, b, (((1,), (1,)), ((), ())), preferred_element_type=F32)


def mm_tn(a, b):
    return lax.dot_general(a, b, (((0,), (0,)), ((), ())), preferred_element_type=F32)


def rope_tables(sequence_length):
    half = HEAD_SIZE // 2
    inverse = np.float32(THETA) ** (-(np.arange(half, dtype=np.float32) * 2.0) / HEAD_SIZE)
    angles = np.arange(sequence_length, dtype=np.float32)[:, None] * inverse.astype(np.float32)[None, :]
    cosine, sine = np.cos(angles), np.sin(angles)
    copies = LANES // HEAD_SIZE
    cosine = np.tile(np.concatenate([cosine, cosine], 1), (1, copies))
    sine = np.tile(np.concatenate([-sine, sine], 1), (1, copies))
    return cosine.astype(np.float32), sine.astype(np.float32)


def lane_iota(shape):
    return lax.broadcasted_iota(jnp.int32, shape, len(shape) - 1)


def turn(block, cosine, sine):
    half = HEAD_SIZE // 2
    lower = (lane_iota(block.shape) % HEAD_SIZE) < half
    partner = jnp.where(
        lower, pltpu.roll(block, LANES - half, 1), pltpu.roll(block, half, 1)
    )
    return block * cosine + partner * sine


def hint(flops, transcendentals, bytes_accessed, share=256):
    return pl.CostEstimate(
        flops=flops // share, transcendentals=transcendentals // share,
        bytes_accessed=bytes_accessed // share,
    )


def tile_ds(index, width):
    return pl.ds(pl.multiple_of(index * width, width), width)


def head_pair(block, place):
    lower = lane_iota(block.shape) < HEAD_SIZE
    moved = pltpu.roll(block, HEAD_SIZE, 1)
    zero = jnp.zeros_like(block)
    low, high = (block, moved) if place == 0 else (moved, block)
    return jnp.where(lower, low, zero), jnp.where(lower, zero, high)


def attention_forward_kernel(
    x_ref, w_ref, gain_one_ref, gain_two_ref, id_row_ref, id_col_ref, cos_ref, sin_ref, picks_ref,
    q_ref, k_ref, v_ref, att_ref, lse_ref, res_ref, pay_ref, gate_ref,
    normed_ref, bias_ref,
    *, q_width, kv_width, experts,
):
    rows, width = x_ref.shape
    x = x_ref[...].astype(F32)
    scale = lax.rsqrt(jnp.mean(x * x, axis=1, keepdims=True) + EPS)
    normed_ref[...] = (x * scale * gain_one_ref[...]).astype(BF)
    bias_ref[...] = jnp.where(id_col_ref[...] <= id_row_ref[...], 0.0, NEG_FILL)
    step = 256

    def project(out_ref, start, count, rotate):
        def body(j, carry):
            cols = pl.ds(pl.multiple_of(start + j * step, step), step)
            part = mm(normed_ref[...], w_ref[:, cols])
            if rotate:
                part = jnp.concatenate(
                    [
                        turn(part[:, i * LANES : (i + 1) * LANES], cos_ref[...], sin_ref[...])
                        for i in range(step // LANES)
                    ],
                    axis=1,
                )
            out_ref[:, tile_ds(j, step)] = part.astype(BF)
            return carry

        lax.fori_loop(0, count // step, body, 0)

    project(q_ref, 0, q_width, True)
    project(k_ref, q_width, kv_width, True)
    project(v_ref, q_width + kv_width, kv_width, False)

    def pair_body(j, carry):
        k_block = k_ref[:, tile_ds(j, LANES)].astype(F32)
        v_block = v_ref[:, tile_ds(j, LANES)].astype(F32)
        for place in range(2):
            keys = head_pair(k_block, place)
            vals = head_pair(v_block, place)
            group = 2 * j + place
            q_block = q_ref[:, tile_ds(group, LANES)]
            out = None
            for side in range(2):
                scores = mm_nt(keys[side].astype(BF), q_block) * SCORE_SCALE + bias_ref[...]
                highest = jnp.max(scores, axis=0, keepdims=True)
                lifted = jnp.exp(scores - highest)
                total = jnp.sum(lifted, axis=0, keepdims=True)
                low = (lifted * (1.0 / total)).astype(BF)
                lse_ref[pl.ds(2 * group + side, 1), :] = highest + jnp.log(total)
                part = mm_tn(vals[side].astype(BF), low)
                out = part if out is None else out + part
            att_ref[:, tile_ds(group, LANES)] = out.T.astype(BF)
        return carry

    lax.fori_loop(0, KEY_VALUE_HEADS // 2, pair_body, 0)

    start = q_width + 2 * kv_width

    def out_body(j, total):
        cols = pl.ds(pl.multiple_of(start + j * step, step), step)
        here = tile_ds(j, step)
        value = x_ref[:, here].astype(F32) + RESIDUAL_SCALE * mm(att_ref[...], w_ref[:, cols])
        res_ref[:, here] = value
        return total + jnp.sum(value * value, axis=1, keepdims=True)

    square = lax.fori_loop(0, width // step, out_body, jnp.zeros((rows, 1), F32))
    scale = lax.rsqrt(square * (1.0 / width) + EPS)
    pay_ref[:rows, :] = (res_ref[...] * scale * gain_two_ref[...]).astype(BF)
    logits = mm(pay_ref[:rows, :], w_ref[:, start + width :])
    lanes = lane_iota(logits.shape)
    chosen = lanes < 0
    for k in range(picks_ref.shape[1]):
        chosen = chosen | (picks_ref[:, k : k + 1] == lanes)
    masked = jnp.where(chosen, logits, NEG_FILL)
    lifted = jnp.where(chosen, jnp.exp(masked - jnp.max(masked, axis=1, keepdims=True)), 0.0)
    gates = lifted / jnp.sum(lifted, axis=1, keepdims=True)
    across = gates.T[:experts, :]
    gate_ref[...] = across
    high = across.astype(BF)
    pay_ref[rows:, :rows] = high
    pay_ref[rows:, rows:] = (across - high.astype(F32)).astype(BF)


def attention_forward(x, pack, gain_one, gain_two, ids, picks, tables, q_width, kv_width, experts):
    rows, width = x.shape
    out_shape = (
        jax.ShapeDtypeStruct((rows, q_width), BF),
        jax.ShapeDtypeStruct((rows, kv_width), BF),
        jax.ShapeDtypeStruct((rows, kv_width), BF),
        jax.ShapeDtypeStruct((rows, q_width), BF),
        jax.ShapeDtypeStruct((QUERY_HEADS, rows), F32),
        jax.ShapeDtypeStruct((rows, width), F32),
        jax.ShapeDtypeStruct((rows + experts, width), BF),
        jax.ShapeDtypeStruct((experts, rows), F32),
    )
    flops = 2 * rows * width * (q_width + 2 * kv_width + width) + 8 * QUERY_HEADS * rows * rows * 128
    return pl.pallas_call(
        functools.partial(
            attention_forward_kernel, q_width=q_width, kv_width=kv_width, experts=experts
        ),
        out_shape=out_shape,
        scratch_shapes=[pltpu.VMEM((rows, width), BF), pltpu.VMEM((rows, rows), F32)],
        compiler_params=pltpu.CompilerParams(vmem_limit_bytes=VMEM_LIMIT),
        cost_estimate=hint(
            flops=flops, transcendentals=QUERY_HEADS * rows * rows, bytes_accessed=16 << 20
        ),
        name="attention_forward",
    )(x, pack, gain_one, gain_two, ids[None, :], ids[:, None], *tables, picks)


def slot_marks(sel_ref, gate_rows, upper_ref, local):
    picked = mm(sel_ref[...], gate_rows)
    rows = picked.shape[1] // 2
    gates = picked[:, :rows] + picked[:, rows:]
    used = gates != 0.0
    rank = mm(used.astype(F32).astype(BF), upper_ref[...])
    slots = jnp.where(used, rank, -1.0)
    places = lax.broadcasted_iota(jnp.int32, (CAP, rows), 0).astype(F32)
    hits = [places == slots[e : e + 1, :] for e in range(local)]
    return gates, hits


def fill_upper(upper_ref):
    rows = upper_ref.shape[0]
    upper = lax.broadcasted_iota(jnp.int32, (rows, rows), 0) < lane_iota((rows, rows))
    upper_ref[...] = jnp.where(upper, 1.0, 0.0).astype(BF)


def dispatch_kernel(sel_ref, pay_ref, grad_ref, *refs, local):
    rows_ref, slot_ref, upper_ref = refs[-3:]

    @pl.when(pl.program_id(0) == 0)
    def _():
        fill_upper(upper_ref)

    rows = grad_ref.shape[1]
    gates, hits = slot_marks(sel_ref, pay_ref[0, rows:, :], upper_ref, local)
    marks = jnp.concatenate([jnp.where(h, 1.0, 0.0).astype(BF) for h in hits], axis=0)
    column = jnp.concatenate(
        [
            jnp.sum(jnp.where(h, gates[e : e + 1, :], 0.0), axis=1, keepdims=True)
            for e, h in enumerate(hits)
        ],
        axis=0,
    )
    moved = mm(marks, pay_ref[0, :rows, :]).astype(BF)
    grads = (column * (RESIDUAL_SCALE * mm(marks, grad_ref[0]))).astype(BF)
    for e in range(local):
        rows_ref[e, 0, 0] = moved[e * CAP : (e + 1) * CAP]
        slot_ref[e, 0, 0] = grads[e * CAP : (e + 1) * CAP]


def dispatch(sel, pays, grads, place, places, local, carried):
    count, rows, width = grads.shape
    shape = jax.ShapeDtypeStruct((local, places, count, CAP, width), BF)
    out_spec = pl.BlockSpec((local, 1, 1, CAP, width), lambda s: (0, place, s, 0, 0))
    in_specs = [
        pl.BlockSpec(sel.shape, lambda s: (0, 0)),
        pl.BlockSpec((1,) + pays.shape[1:], lambda s: (s, 0, 0)),
        pl.BlockSpec((1, rows, width), lambda s: (s, 0, 0)),
    ]
    operands = [sel, pays, grads]
    aliases = {}
    if carried is not None:
        operands += list(carried)
        in_specs += [pl.BlockSpec(memory_space=pl.ANY)] * 2
        aliases = {3: 0, 4: 1}
    return pl.pallas_call(
        functools.partial(dispatch_kernel, local=local),
        out_shape=(shape, shape),
        grid=(count,),
        in_specs=in_specs,
        out_specs=(out_spec, out_spec),
        scratch_shapes=[pltpu.VMEM((rows, rows), BF)],
        input_output_aliases=aliases,
        compiler_params=pltpu.CompilerParams(vmem_limit_bytes=VMEM_LIMIT),
        cost_estimate=hint(
            flops=4 * count * local * CAP * rows * width, transcendentals=0, bytes_accessed=20 << 20
        ),
        name="dispatch",
    )(*operands)


def expert_kernel(x_ref, s_ref, w_ref, *refs, chunk, tile, last, carried):
    if carried:
        prior_ref, refs = refs[0], refs[1:]
    (
        pr_ref, dg_ref, dot_ref, grad_ref,
        gate_ref, up_ref, down_ref, act_ref, both_ref, acc_in_ref, acc_down_ref,
    ) = refs
    rows, width = x_ref.shape[-2:]
    hidden = gate_ref.shape[-1]
    owners = grad_ref.shape[0]
    in_rows, down_rows = width // owners, hidden // owners
    step = pl.program_id(1)
    pieces = width // hidden

    @pl.when(step == 0)
    def _():
        for o in range(owners):
            gate_ref[o * in_rows : (o + 1) * in_rows, :] = w_ref[o, 0, :in_rows, :]
            up_ref[o * in_rows : (o + 1) * in_rows, :] = w_ref[o, 0, in_rows : 2 * in_rows, :]
            for c in range(pieces):
                first = 2 * in_rows + c * down_rows
                down_ref[o * down_rows : (o + 1) * down_rows, c * hidden : (c + 1) * hidden] = w_ref[
                    o, 0, first : first + down_rows, :
                ]

    def chunk_body(c, carry):
        here = tile_ds(c, chunk)
        x = x_ref[0, here, :]
        s = s_ref[0, here, :]
        pre_gate = mm(x, gate_ref[...])
        pre_up = mm(x, up_ref[...])
        act_grad = mm_nt(s, down_ref[...])
        logistic = jax.nn.sigmoid(pre_gate)
        swish = pre_gate * logistic
        act = (swish * pre_up).astype(BF)
        gate_in = (
            act_grad * pre_up * logistic * (1.0 + pre_gate * (1.0 - logistic))
        ).astype(BF)
        up_in = (act_grad * swish).astype(BF)
        dot_ref[0, here, :] = jnp.sum(act.astype(F32) * act_grad, axis=1, keepdims=True)
        act_ref[here, :] = act
        both_ref[here, :hidden] = gate_in
        both_ref[here, hidden:] = up_in
        pr_ref[0, here, :] = mm(act, down_ref[...]).astype(BF)
        dg_ref[0, here, :] = (mm_nt(gate_in, gate_ref[...]) + mm_nt(up_in, up_ref[...])).astype(BF)
        return carry

    lax.fori_loop(0, rows // chunk, chunk_body, 0)

    def put(owner, first, value):
        count = value.shape[0]
        if carried:
            value = value + prior_ref[owner, 0, first : first + count, :].astype(F32)
        grad_ref[owner, 0, first : first + count, :] = value.astype(BF)

    def accumulate(acc_ref, here, part, emit):
        if last == 0:
            emit(part)
            return

        @pl.when(step == 0)
        def _():
            acc_ref[here, :] = part

        if last > 1:

            @pl.when((step > 0) & (step < last))
            def _():
                acc_ref[here, :] = acc_ref[here, :] + part

        @pl.when(step == last)
        def _():
            emit(acc_ref[here, :] + part)

    def in_body(t, carry):
        here = tile_ds(t, tile)

        def emit(total):
            for i in range(tile // in_rows):
                piece = total[i * in_rows : (i + 1) * in_rows]
                owner = t * (tile // in_rows) + i
                put(owner, 0, piece[:, :hidden])
                put(owner, in_rows, piece[:, hidden:])

        accumulate(acc_in_ref, here, mm_tn(x_ref[0, :, here], both_ref[...]), emit)
        return carry

    lax.fori_loop(0, width // tile, in_body, 0)

    def down_body(t, carry):
        here = tile_ds(t, tile)

        def emit(total):
            for i in range(tile // down_rows):
                piece = total[i * down_rows : (i + 1) * down_rows]
                owner = t * (tile // down_rows) + i
                for c in range(pieces):
                    put(owner, 2 * in_rows + c * down_rows, piece[:, c * hidden : (c + 1) * hidden])

        accumulate(acc_down_ref, here, mm_tn(act_ref[:, here], s_ref[0]), emit)
        return carry

    lax.fori_loop(0, hidden // tile, down_body, 0)


def experts_step(first, weights, rows_in, slot_grad, prior):
    owners, count, packed, hidden = weights.shape
    _, total, width = rows_in.shape
    rows = 8 * CAP
    steps = total // rows
    out_shape = (
        jax.ShapeDtypeStruct((count, total, width), BF),
        jax.ShapeDtypeStruct((count, total, width), BF),
        jax.ShapeDtypeStruct((count, total, 1), F32),
        jax.ShapeDtypeStruct(weights.shape, BF),
    )
    in_spec = pl.BlockSpec((1, rows, width), lambda e, t: (first + e, t, 0))
    pack_spec = pl.BlockSpec((owners, 1, packed, hidden), lambda e, t: (0, e, 0, 0))
    row_spec = lambda last: pl.BlockSpec((1, rows, last), lambda e, t: (e, t, 0))
    operands = [rows_in, slot_grad, weights]
    in_specs = [in_spec, in_spec, pack_spec]
    if prior is not None:
        operands.append(prior)
        in_specs.append(pack_spec)
    kept = 0 if steps == 1 else 1
    return pl.pallas_call(
        functools.partial(
            expert_kernel, chunk=rows // 3, tile=256, last=steps - 1, carried=prior is not None
        ),
        out_shape=out_shape,
        grid=(count, steps),
        in_specs=in_specs,
        out_specs=(row_spec(width), row_spec(width), row_spec(1), pack_spec),
        scratch_shapes=[
            pltpu.VMEM((width, hidden), BF),
            pltpu.VMEM((width, hidden), BF),
            pltpu.VMEM((hidden, width), BF),
            pltpu.VMEM((rows, hidden), BF),
            pltpu.VMEM((rows, 2 * hidden), BF),
            pltpu.VMEM((width, 2 * hidden) if kept else (8, LANES), F32),
            pltpu.VMEM((hidden, width) if kept else (8, LANES), F32),
        ],
        compiler_params=pltpu.CompilerParams(vmem_limit_bytes=VMEM_LIMIT),
        cost_estimate=hint(
            flops=18 * count * total * width * hidden, transcendentals=count * total * hidden,
            bytes_accessed=30 << 20, share=256 if prior is None else 1,
        ),
        name="experts",
    )(*operands)


def combine_kernel(sel_ref, pay_ref, *refs, groups, local, received):
    produced, returned, dots = (refs[i * groups : (i + 1) * groups] for i in range(3))
    rest = refs[3 * groups :]
    if received:
        other_ref, rest = rest[0], rest[1:]
    out_refs, upper_ref = rest[:-1], rest[-1]
    each = local // groups

    @pl.when(pl.program_id(0) == 0)
    def _():
        fill_upper(upper_ref)

    rows = upper_ref.shape[0]
    gates, hits = slot_marks(sel_ref, pay_ref[0], upper_ref, local)
    weighted = jnp.concatenate(
        [jnp.where(h, gates[e : e + 1, :], 0.0).astype(BF) for e, h in enumerate(hits)], axis=0
    )
    plain = jnp.concatenate([jnp.where(h, 1.0, 0.0).astype(BF) for h in hits], axis=0)
    made = jnp.concatenate([r[e, 0] for r in produced for e in range(each)], axis=0)
    back = jnp.concatenate([r[e, 0] for r in returned for e in range(each)], axis=0)
    out = mm_tn(weighted, made)
    grads = mm_tn(plain, back)
    pad = jnp.zeros((8 - local, rows), F32)
    dot_rows = jnp.concatenate(
        [
            jnp.sum(jnp.where(h, dots[e // each][e % each, 0], 0.0), axis=0, keepdims=True)
            for e, h in enumerate(hits)
        ]
        + ([pad] if local < 8 else []),
        axis=0,
    )
    high = dot_rows.astype(BF)
    low = (dot_rows - high.astype(F32)).astype(BF)
    tail = jnp.concatenate([mm_tn(sel_ref[...], high), mm_tn(sel_ref[...], low)], axis=1)
    half = tail.shape[0] // 2
    first = jnp.concatenate([out, tail[:half]], axis=0)
    second = jnp.concatenate([tail[half:], grads], axis=0)
    if received:
        first = first + other_ref[0, : rows + half, :].astype(F32)
        second = second + other_ref[0, rows + half :, :].astype(F32)

        def put(index):
            out_refs[2 * index][...] = first.astype(BF)
            out_refs[2 * index + 1][...] = second.astype(BF)

        for index in range(len(out_refs) // 2):
            pl.when(pl.program_id(0) == index)(functools.partial(put, index))
    else:
        out_refs[0][0, : rows + half, :] = first.astype(BF)
        out_refs[0][0, rows + half :, :] = second.astype(BF)


def combine(sel, pays, produced, returned, dots, side, first, span, other):
    count, total_rows, width = pays.shape
    groups, each = len(produced), produced[0].shape[0]
    local = groups * each
    experts = sel.shape[1]
    rows = total_rows - experts
    pick = lambda last: pl.BlockSpec((each, 1, CAP, last), lambda s: (0, side * count + first + s, 0, 0))
    in_specs = [
        pl.BlockSpec(sel.shape, lambda s: (0, 0)),
        pl.BlockSpec((1, experts, width), lambda s: (first + s, rows // experts, 0)),
    ]
    in_specs += [pick(width)] * (2 * groups) + [pick(1)] * groups
    operands = [sel, pays, *produced, *returned, *dots]
    total = 2 * rows + experts
    out_spec = pl.BlockSpec((1, total, width), lambda s: (s, 0, 0))
    out_shape = (jax.ShapeDtypeStruct((span, total, width), BF),)
    out_specs = (out_spec,)
    if other is not None:
        operands.append(other)
        in_specs.append(out_spec)
        out_shape = (jax.ShapeDtypeStruct((total // 2, width), BF),) * (2 * span)
        out_specs = (pl.BlockSpec((total // 2, width), lambda s: (0, 0)),) * (2 * span)
    return pl.pallas_call(
        functools.partial(combine_kernel, groups=groups, local=local, received=other is not None),
        out_shape=out_shape,
        grid=(span,),
        in_specs=in_specs,
        out_specs=out_specs,
        scratch_shapes=[pltpu.VMEM((rows, rows), BF)],
        compiler_params=pltpu.CompilerParams(vmem_limit_bytes=VMEM_LIMIT),
        cost_estimate=hint(
            flops=4 * span * local * CAP * rows * width, transcendentals=0, bytes_accessed=20 << 20, share=1
        ),
        name="combine",
    )(*operands)


def attention_backward_kernel(
    *refs, terms, q_width, kv_width, experts, carried,
):
    (
        x_ref, w_ref, gain_one_ref, gain_two_ref, id_row_ref, id_col_ref, cos_ref, sin_ref,
        grad_ref, q_ref, k_ref, v_ref, att_ref, lse_ref, res_ref, pay_ref, gate_ref,
    ) = refs[:17]
    term_refs = refs[17 : 17 + 2 * terms]
    rest = refs[17 + 2 * terms :]
    if carried:
        prior_ref, rest = rest[0], rest[3:]
    out_ref, in_grad_ref, pack_ref, bias_ref, wide_ref, att_grad_ref, qkv_grad_ref, branch_ref, normed_ref = rest
    rows, width = x_ref.shape
    step = 256
    start = q_width + 2 * kv_width

    def put(row_slice, cols, value):
        if carried:
            value = value + prior_ref[row_slice, cols].astype(F32)
        pack_ref[row_slice, cols] = value.astype(BF)

    def gathered(which, low, high):
        total = term_refs[which][low:high, :].astype(F32)
        for ref in term_refs[2 + which :: 2]:
            total = total + ref[low:high, :].astype(F32)
        return total

    half = experts // 2
    residual = res_ref[...]
    out_ref[0] = (residual + RESIDUAL_SCALE * gathered(0, 0, rows)).astype(BF)
    tail = jnp.concatenate([gathered(0, rows, rows + half), gathered(1, 0, half)], axis=0)
    weighted = tail[:, :rows] + tail[:, rows:]
    chosen = weighted - gate_ref[...] * jnp.sum(weighted, axis=0, keepdims=True)
    chosen = jnp.concatenate([chosen, jnp.zeros((LANES - experts, rows), F32)], axis=0)
    logit_grad = chosen.T.astype(BF)
    moe_grad = gathered(1, half, half + rows) + mm_nt(logit_grad, w_ref[:, start + width :])
    last = mm_tn(pay_ref[:rows, :], logit_grad)
    scale = lax.rsqrt(jnp.mean(residual * residual, axis=1, keepdims=True) + EPS)
    gain_two_grad = jnp.sum(moe_grad * residual * scale, axis=0, keepdims=True)
    u = moe_grad * gain_two_ref[...]
    inner = jnp.sum(u * residual, axis=1, keepdims=True) * (1.0 / width)
    res_grad = grad_ref[...].astype(F32) + scale * u - residual * (scale * scale * scale * inner)
    in_grad_ref[0] = res_grad
    branch_ref[...] = (RESIDUAL_SCALE * res_grad).astype(BF)
    bias_ref[...] = jnp.where(id_col_ref[...] <= id_row_ref[...], 0.0, NEG_FILL)

    def branch_body(j, carry):
        here = tile_ds(j, step)
        att_grad_ref[:, here] = mm_nt(
            branch_ref[...], w_ref[here, start : start + width]
        ).astype(BF)
        part = mm_tn(att_ref[:, here], branch_ref[...])
        put(here, slice(start, start + width), part)
        return carry

    lax.fori_loop(0, q_width // step, branch_body, 0)

    lower = lane_iota((rows, LANES)) < HEAD_SIZE

    def pair_body(j, carry):
        k_block = k_ref[:, tile_ds(j, LANES)].astype(F32)
        v_block = v_ref[:, tile_ds(j, LANES)].astype(F32)
        k_sums, v_sums = [], []
        for place in range(2):
            keys = [h.astype(BF) for h in head_pair(k_block, place)]
            vals = [h.astype(BF) for h in head_pair(v_block, place)]
            group = 2 * j + place
            here = tile_ds(group, LANES)
            q_block = q_ref[:, here]
            g_block = att_grad_ref[:, here]
            q_out = None
            k_parts, v_parts = [], []
            for side in range(2):
                scores = mm_nt(keys[side], q_block) * SCORE_SCALE + bias_ref[...]
                probs = jnp.exp(scores - lse_ref[pl.ds(2 * group + side, 1), :])
                weight_grad = mm_nt(vals[side], g_block)
                v_parts.append(mm(probs.astype(BF), g_block))
                dots = jnp.sum(probs * weight_grad, axis=0, keepdims=True)
                score_grad = (probs * (weight_grad - dots)).astype(BF)
                k_parts.append(mm(score_grad, q_block))
                part = mm_tn(keys[side], score_grad)
                q_out = part if q_out is None else q_out + part
            q_turned = turn(q_out.T * SCORE_SCALE, cos_ref[...], -sin_ref[...])
            qkv_grad_ref[:, here] = q_turned.astype(BF)
            for parts, sums in ((k_parts, k_sums), (v_parts, v_sums)):
                mixed = jnp.where(lower, parts[0], parts[1])
                sums.append(mixed + pltpu.roll(mixed, HEAD_SIZE, 1))
        k_total = jnp.where(lower, k_sums[0], k_sums[1]) * SCORE_SCALE
        v_total = jnp.where(lower, v_sums[0], v_sums[1])
        k_here = pl.ds(pl.multiple_of(q_width + j * LANES, LANES), LANES)
        v_here = pl.ds(pl.multiple_of(q_width + kv_width + j * LANES, LANES), LANES)
        qkv_grad_ref[:, k_here] = turn(k_total, cos_ref[...], -sin_ref[...]).astype(BF)
        qkv_grad_ref[:, v_here] = v_total.astype(BF)
        return carry

    lax.fori_loop(0, KEY_VALUE_HEADS // 2, pair_body, 0)

    x = x_ref[...].astype(F32)
    scale = lax.rsqrt(jnp.mean(x * x, axis=1, keepdims=True) + EPS)
    normed_ref[...] = (x * scale * gain_one_ref[...]).astype(BF)

    def norm_body(j, carry):
        here = tile_ds(j, step)
        grad = mm_nt(qkv_grad_ref[...], w_ref[here, :start])
        put(here, slice(0, start), mm_tn(normed_ref[:, here], qkv_grad_ref[...]))
        wide_ref[:, here] = grad
        return carry

    lax.fori_loop(0, width // step, norm_body, 0)
    normed_grad = wide_ref[...]
    gain_one_grad = jnp.sum(normed_grad * x * scale, axis=0, keepdims=True)
    u = normed_grad * gain_one_ref[...]
    inner = jnp.sum(u * x, axis=1, keepdims=True) * (1.0 / width)
    in_grad_ref[0] = in_grad_ref[0] + scale * u - x * (scale * scale * scale * inner)
    lanes = lane_iota((width, LANES))
    one = jnp.broadcast_to(gain_one_grad, (LANES, width)).T
    two = jnp.broadcast_to(gain_two_grad, (LANES, width)).T
    last = jnp.where(lanes == experts, one, last)
    last = jnp.where(lanes == experts + 1, two, last)
    put(slice(0, width), slice(start + width, start + width + LANES), last)


def attention_backward(
    index, micro, x, pack, gain_one, gain_two, ids, tables, grad, saved, terms, prior, made, q_width, kv_width,
    experts,
):
    rows, width = x.shape
    operands = [x, pack, gain_one, gain_two, ids[None, :], ids[:, None], *tables, grad, *saved, *terms]
    whole = pl.BlockSpec(memory_space=pltpu.VMEM)
    in_specs = [whole] * len(operands)
    aliases = {}
    if prior is not None:
        operands += [prior, *made]
        in_specs += [whole] + [pl.BlockSpec(memory_space=pl.ANY)] * 2
        aliases = {len(operands) - 2: 0, len(operands) - 1: 1}
    row_spec = pl.BlockSpec((1, rows, width), lambda i: (index, 0, 0))
    flops = 4 * rows * width * (q_width + 2 * kv_width + width) + 20 * QUERY_HEADS * rows * rows * 128
    return pl.pallas_call(
        functools.partial(
            attention_backward_kernel, terms=len(terms) // 2, q_width=q_width, kv_width=kv_width,
            experts=experts, carried=prior is not None,
        ),
        out_shape=(
            jax.ShapeDtypeStruct((micro, rows, width), BF),
            jax.ShapeDtypeStruct((micro, rows, width), F32),
            jax.ShapeDtypeStruct(pack.shape, BF),
        ),
        grid=(1,),
        in_specs=in_specs,
        out_specs=(row_spec, row_spec, whole),
        input_output_aliases=aliases,
        scratch_shapes=[
            pltpu.VMEM((rows, rows), F32),
            pltpu.VMEM((rows, width), F32),
            pltpu.VMEM((rows, q_width), BF),
            pltpu.VMEM((rows, q_width + 2 * kv_width), BF),
            pltpu.VMEM((rows, width), BF),
            pltpu.VMEM((rows, width), BF),
        ],
        compiler_params=pltpu.CompilerParams(vmem_limit_bytes=VMEM_LIMIT),
        cost_estimate=hint(
            flops=flops, transcendentals=QUERY_HEADS * rows * rows, bytes_accessed=40 << 20, share=1
        ),
        name="attention_backward",
    )(*operands)


def peer_chip(chip, distance):
    total = 0
    for bit in (1, 2, 4):
        total = total + bit * ((chip // bit + (distance // bit) % 2) % 2)
    return total


def where_am_i():
    f, d = lax.axis_index("fsdp"), lax.axis_index("dp")
    return f // 2, f % 2, d


def meet(peers):
    barrier = pltpu.get_barrier_semaphore()
    for peer in peers:
        pl.semaphore_signal(
            barrier, inc=1, device_id=peer, device_id_type=pl.DeviceIdType.MESH
        )
    pl.semaphore_wait(barrier, len(peers))


def push(src, dst, send, receive, peer):
    copy = pltpu.make_async_remote_copy(
        src_ref=src, dst_ref=dst, send_sem=send, recv_sem=receive, device_id=peer,
        device_id_type=pl.DeviceIdType.MESH,
    )
    copy.start()
    return copy


def gather_layer_kernel(
    w_ref, out_ref, own_sem, z_send, z_receive, x_send, x_receive, s_send, s_receive, *, chips, depth
):
    chip, core, d = where_am_i()
    rows = w_ref.shape[0]
    others = [peer_chip(chip, r) for r in range(1, chips)]
    f, sibling = chip * 2 + core, chip * 2 + 1 - core

    def block(owner, layer):
        first = pl.multiple_of((owner * depth + layer) * rows, rows)
        return out_ref.at[pl.ds(first, rows), :]

    peers = [(f, (d + i) % depth) for i in range(1, depth)]
    peers += [(c * 2 + core, d) for c in others] + [(sibling, d)]
    meet(peers)
    own = pltpu.make_async_copy(w_ref, block(f, d), own_sem)
    own.start()
    z_copies = [
        push(w_ref, block(f, d), z_send.at[i - 1], z_receive.at[i - 1], (f, (d + i) % depth))
        for i in range(1, depth)
    ]
    x_copies, s_copies = [], []
    layers = [(d + depth - i) % depth for i in range(depth)]
    for i, layer in enumerate(layers):
        if i:
            z_copies[i - 1].wait_recv()
        src = block(f, layer) if i else w_ref
        for r, c in enumerate(others):
            x_copies.append(
                push(src, block(f, layer), x_send.at[i, r], x_receive.at[i, r], (c * 2 + core, d))
            )
        s_copies.append(
            push(src, block(f, layer), s_send.at[i, 0], s_receive.at[i, 0], (sibling, d))
        )
    for i, layer in enumerate(layers):
        for r, c in enumerate(others):
            x_copies[i * (chips - 1) + r].wait_recv()
            there = block(c * 2 + core, layer)
            s_copies.append(
                push(there, there, s_send.at[i, r + 1], s_receive.at[i, r + 1], (sibling, d))
            )
    own.wait()
    for copy in z_copies + x_copies:
        copy.wait_send()
    for copy in s_copies:
        copy.wait()


def gather_layer(pack, chips, depth):
    dma = pltpu.SemaphoreType.DMA
    rows, width = pack.shape
    return pl.pallas_call(
        functools.partial(gather_layer_kernel, chips=chips, depth=depth),
        out_shape=jax.ShapeDtypeStruct((rows * 2 * chips * depth, width), pack.dtype),
        in_specs=[pl.BlockSpec(memory_space=pl.ANY)],
        out_specs=pl.BlockSpec(memory_space=pl.ANY),
        scratch_shapes=[
            dma(()), dma((depth - 1,)), dma((depth - 1,)), dma((depth, chips - 1)),
            dma((depth, chips - 1)), dma((depth, chips)), dma((depth, chips)),
        ],
        compiler_params=pltpu.CompilerParams(collective_id=1, has_side_effects=True),
        name="gather_layer",
    )(pack)


def reduce_layer_kernel(
    pack_ref, out_ref, s_buf, s_sum, x_buf, x_sum, z_buf,
    s_send, s_receive, x_send, x_receive, z_send, z_receive,
    *, chips, depth, parts,
):
    chip, core, d = where_am_i()
    total, width = pack_ref.shape
    rows = total // (2 * chips * depth)
    span = rows * depth
    step = width // parts
    distances = list(range(1, chips))
    others = [peer_chip(chip, r) for r in distances]
    f, sibling = chip * 2 + core, chip * 2 + 1 - core
    peers = [(f, (d + i) % depth) for i in range(1, depth)]
    peers += [(c * 2 + core, d) for c in others] + [(sibling, d)]
    meet(peers)

    def band(p):
        return slice(p * step, (p + 1) * step)

    def mine(c, k):
        return pl.ds(pl.multiple_of((c * 2 + k) * span, span), span)

    order = [(r, c) for r, c in zip(distances, others)][::-1] + [(0, chip)]
    s_copies = {}
    for p in range(parts):
        for r, c in order:
            s_copies[p, r] = push(
                pack_ref.at[mine(c, 1 - core), band(p)], s_buf.at[r, :, band(p)],
                s_send.at[p, r], s_receive.at[p, r], (sibling, d),
            )
    x_copies, z_copies = {}, {}

    def sum_chip(p):
        for r, c in order:
            s_copies[p, r].wait_recv()
            value = pack_ref[mine(c, core), band(p)].astype(F32) + s_buf[r, :, band(p)].astype(F32)
            s_sum[r, :, band(p)] = value.astype(s_sum.dtype)

    def send_chip(p):
        for r, c in order[:-1]:
            x_copies[p, r] = push(
                s_sum.at[r, :, band(p)], x_buf.at[r - 1, :, band(p)], x_send.at[p, r - 1],
                x_receive.at[p, r - 1], (c * 2 + core, d),
            )

    def sum_plane(p):
        value = s_sum[0, :, band(p)].astype(F32)
        for r in distances:
            x_copies[p, r].wait_recv()
            value = value + x_buf[r - 1, :, band(p)].astype(F32)
        x_sum[:, :, band(p)] = value.reshape(depth, rows, step).astype(x_sum.dtype)

    def send_plane(p):
        for i in range(1, depth):
            to = (d + i) % depth
            z_copies[p, i] = push(
                x_sum.at[to, :, band(p)], z_buf.at[i - 1, :, band(p)], z_send.at[p, i - 1],
                z_receive.at[p, i - 1], (f, to),
            )

    def finish(p):
        value = x_sum[d, :, band(p)].astype(F32)
        for i in range(1, depth):
            z_copies[p, i].wait_recv()
            value = value + z_buf[i - 1, :, band(p)].astype(F32)
        out_ref[:, band(p)] = value

    for p in range(parts + 1):
        if p < parts:
            sum_chip(p)
        if p > 0:
            send_chip(p - 1)
    for p in range(parts + 1):
        if p < parts:
            sum_plane(p)
        if p > 0:
            send_plane(p - 1)
    for p in range(parts):
        finish(p)
    for copy in [*s_copies.values(), *x_copies.values(), *z_copies.values()]:
        copy.wait_send()


def reduce_layer(pack, chips, depth, parts):
    dma = pltpu.SemaphoreType.DMA
    total, width = pack.shape
    rows = total // (2 * chips * depth)
    kind = BF if rows % 16 == 0 else F32
    return pl.pallas_call(
        functools.partial(reduce_layer_kernel, chips=chips, depth=depth, parts=parts),
        out_shape=jax.ShapeDtypeStruct((rows, width), F32),
        in_specs=[pl.BlockSpec(memory_space=pltpu.VMEM)],
        out_specs=pl.BlockSpec(memory_space=pltpu.VMEM),
        scratch_shapes=[
            pltpu.VMEM((chips, rows * depth, width), BF),
            pltpu.VMEM((chips, rows * depth, width), BF),
            pltpu.VMEM((chips - 1, rows * depth, width), BF),
            pltpu.VMEM((depth, rows, width), kind),
            pltpu.VMEM((depth - 1, rows, width), kind),
            dma((parts, chips)), dma((parts, chips)), dma((parts, chips - 1)), dma((parts, chips - 1)),
            dma((parts, depth - 1)), dma((parts, depth - 1)),
        ],
        compiler_params=pltpu.CompilerParams(
            collective_id=2, has_side_effects=True, vmem_limit_bytes=VMEM_LIMIT
        ),
        cost_estimate=pl.CostEstimate(flops=0, transcendentals=0, bytes_accessed=1 << 30),
        name="reduce_layer",
    )(pack)


def swap(value, distance, size):
    return lax.ppermute(value, "fsdp", [(i, i ^ distance) for i in range(size)])


def after(value, *earlier):
    return lax.optimization_barrier((value, *earlier))[0] if earlier else value


def send_near(value, size):
    return swap(value, 2, size), swap(value, 4, size)


def gather_chips(value, near, size):
    chips = size // 2
    if near is None:
        return [value] + [swap(value, 2 * r, size) for r in range(1, chips)]
    half = value.shape[0] // 2
    one, two = near
    return [value, one, two, swap(one[:half], 4, size), swap(two[half:], 2, size)]


def both_cores(pieces, size, *earlier):
    if earlier:
        pieces = [pieces[0]] + [after(p, *earlier) for p in pieces[1:]]
    chips = size // 2
    mine = jnp.stack(pieces[: chips - 1] + [jnp.concatenate(pieces[chips - 1 :])])
    return mine, swap(mine, 1, size)


def scatter_near(kept, size, *earlier):
    chips = size // 2
    if chips != 4:
        return [swap(kept[2 * r + h], 2 * r, size) for r in range(1, chips) for h in range(2)]
    return [swap(after(kept[6], *earlier), 2, size), swap(after(kept[7], *earlier), 4, size)]


def scatter_far(kept, near, size, *earlier):
    if size != 8:
        return (), ()
    add = lambda a, b: (a.astype(F32) + b.astype(F32)).astype(BF)
    by_one, by_two = after(near[0], *earlier), after(near[1], *earlier)
    one_sum, two_sum = add(kept[3], by_two), add(kept[4], by_one)
    return (one_sum, two_sum), (swap(one_sum, 2, size), swap(two_sum, 4, size))


def scatter_rest(kept, size, *earlier):
    if size != 8:
        return ()
    return swap(after(kept[2], *earlier), 2, size), swap(after(kept[5], *earlier), 4, size)


def scattered(kept, near, far, rest):
    if not far:
        return [kept[0], kept[1]] + near
    return [kept[0], kept[1], rest[0], far[0], far[1], rest[1]]


def local(
    inputs, block_ids, routes, out_grad, norm_gain, w_query, key_weight, value_weight, w_output,
    moe_gain, w_router, w_gate, w_up, w_down,
):
    micro, _, rows, width = inputs.shape
    experts = w_router.shape[1]
    held, in_rows, hidden = w_gate.shape
    down_rows = w_down.shape[1]
    q_width, kv_width = w_query.shape[1], key_weight.shape[1]
    owners = lax.axis_size("fsdp")
    depth = lax.axis_size("dp")
    chips = owners // 2
    tables = tuple(jnp.asarray(t) for t in rope_tables(rows))
    start = q_width + 2 * kv_width + width
    group = max(1, held // 2)
    cuts = width // hidden

    split_down = w_down.reshape(held, down_rows, cuts, hidden).transpose(0, 2, 1, 3)
    packed = jnp.concatenate(
        [w_gate, w_up, split_down.reshape(held, cuts * down_rows, hidden)], axis=1
    )
    weights = [
        lax.all_gather(packed[g : g + group], "dp", axis=0, tiled=False)
        for g in range(0, held, group)
    ]
    pieces = [
        w_query, key_weight, value_weight, w_output, w_router, norm_gain[:, None], moe_gain[:, None]
    ]
    filled = sum(p.shape[1] for p in pieces)
    pieces.append(jnp.zeros((w_query.shape[0], start + LANES - filled), BF))
    pack = gather_layer(jnp.concatenate(pieces, axis=1), chips, depth)
    gain_one = pack[:, start + experts].astype(F32)[None, :]
    gain_two = pack[:, start + experts + 1].astype(F32)[None, :]
    first = lax.axis_index("fsdp") * held
    places = jnp.arange(8)[:, None]
    sel = ((jnp.arange(experts)[None, :] == first + places) & (places < held)).astype(BF)
    square = chips == 4

    def forward(m, x):
        return attention_forward(
            x, pack, gain_one, gain_two, block_ids[m, 0], routes[m, 0], tables, q_width, kv_width, experts
        )

    def dispatched(m, pay, grad):
        carried = None
        for side in range(2):
            carried = dispatch(sel, pay[side], grad[side], side, 2, held, carried)
        return [c.reshape(held, 2 * chips * CAP, width) for c in carried]

    saved, arrived, pays, moved, done, terms = [], [], [], [], {}, []
    ready = ()
    for m in range(micro):
        grad = after(out_grad[m, 0], *ready)
        grad_near = send_near(grad, owners) if square else None
        if m == 0:
            saved.append(forward(0, after(inputs[0, 0], *(grad_near if square else ()))))
            for n in range(1, micro):
                saved.append(forward(n, after(inputs[n, 0], saved[n - 1][4])))
        pay = saved[m][6]
        pay_near = None
        if square and m == 0:
            one, two = send_near(pay, owners)
            ready = (saved[-1][4],)
            pay_near = after(one, saved[-1][4]), after(two, saved[-1][4])
        elif m:
            pay = after(pay, *arrived[m - 1][0][1:])
            ready = (pay,)
        arrived.append((gather_chips(pay, pay_near, owners), gather_chips(grad, grad_near, owners), grad_near))

    def expert_part(m, g, *earlier):
        prior = done[m - 1, g][3] if m else None
        rows_in, slot_grad = moved[m]
        if earlier:
            rows_in = after(rows_in, *earlier)
        done[m, g] = experts_step(g * group, weights[g], rows_in, slot_grad, prior)

    def returned(m, earlier):
        parts = [
            [done[m, g][i].reshape(group, 2 * chips, CAP, -1) for g in range(len(weights))]
            for i in range(3)
        ]
        kept, before = [], earlier
        sent = {}
        span = chips // 2
        for first in (span, 0):
            (sent[first],) = combine(sel, after(pays[m][1], *before), *parts, 1, first, span, None)
            before = (sent[first],)
        for first in (span, 0):
            found = combine(
                sel, after(pays[m][0], *before), *parts, 0, first, span, swap(sent[first], 1, owners)
            )
            before = (found[0],)
            kept = list(found) + kept
        return kept

    def backward(m, found, made, prior):
        out, in_grad, prior = attention_backward(
            m, micro, inputs[m, 0], pack, gain_one, gain_two, block_ids[m, 0], tables, out_grad[m, 0],
            saved[m], found, prior, made, q_width, kv_width, experts,
        )
        return (out, in_grad), prior

    added, far, rest = (), (), ()
    for m in range(micro):
        held_back = (done[m - 1, 0][2],) if m else ()
        pay_held = arrived[m + 1][2] if m == 0 and micro > 1 and square else held_back
        pays.append(both_cores(arrived[m][0], owners, *pay_held))
        moved.append(dispatched(m, pays[m], both_cores(arrived[m][1], owners, *held_back)))
        hold = arrived[m + 1][2] if m + 1 < micro and square else ()
        if m == 0:
            expert_part(0, 0, *hold)
        else:
            for g in range(1, len(weights)):
                expert_part(m - 1, g, moved[m][0])
            kept = returned(m - 1, far)
            near = scatter_near(kept, owners, *rest)
            expert_part(m, 0, kept[0], kept[-1])
            added, far = scatter_far(kept, near, owners, done[m, 0][2])
            rest = scatter_rest(kept, owners, *far)
            terms.append(scattered(kept, near, far, rest))
    for g in range(1, len(weights)):
        expert_part(micro - 1, g, *added)
    kept = returned(micro - 1, far)
    near = scatter_near(kept, owners, *rest)
    last_rest = scatter_rest(kept, owners, *rest)
    made, prior, held_back = None, None, ()
    for m in range(micro - 1):
        made, prior = backward(m, [after(terms[m][0], kept[0], kept[-1])] + terms[m][1:], made, prior)
        held_back = (prior,)
    last_far = scatter_far(kept, near, owners, *held_back)[1]
    terms.append(scattered(kept, near, last_far, last_rest))
    made, prior = backward(micro - 1, terms[-1], made, prior)
    sums = []
    for g in range(len(weights)):
        summed = after(done[micro - 1, g][3], *(far if g else added))
        sums.append(lax.psum_scatter(summed, "dp", scatter_dimension=0, tiled=True)[0])
    layer = reduce_layer(prior, chips, depth, 5)
    marks = np.cumsum([0, q_width, kv_width, kv_width, width, experts, 1, 1])
    cut = [layer[:, a:b] for a, b in zip(marks[:-1], marks[1:])]
    stacked = jnp.concatenate(sums, axis=0).astype(F32)
    grad_down = stacked[:, 2 * in_rows :].reshape(held, cuts, down_rows, hidden)
    grad_down = grad_down.transpose(0, 2, 1, 3).reshape(held, down_rows, width)
    return (
        made[0][:, None],
        made[1][:, None],
        cut[5][:, 0], cut[0], cut[1], cut[2], cut[3], cut[6][:, 0], cut[4],
        stacked[:, :in_rows], stacked[:, in_rows : 2 * in_rows], grad_down,
    )


def solution(mesh):
    rows = ("fsdp", "dp")
    split = lambda rank: P(None, rows, *([None] * (rank - 2)))
    flat = P(rows, None)
    expert_spec = P("fsdp", "dp", None)
    in_specs = (
        split(4), split(3), split(4), split(4), P(rows), flat, flat, flat, flat, P(rows), flat,
        expert_spec, expert_spec, expert_spec,
    )
    out_specs = (
        split(4), split(4), P(rows), flat, flat, flat, flat, P(rows), flat,
        expert_spec, expert_spec, expert_spec,
    )
    return jax.shard_map(local, mesh=mesh, in_specs=in_specs, out_specs=out_specs, check_vma=False)
```

```python
import functools

import jax
import jax.numpy as jnp
import numpy as np
from jax import lax
from jax.experimental import pallas as pl
from jax.experimental.pallas import tpu as pltpu
from jax.sharding import PartitionSpec as P

QUERY_HEADS = 16
KEY_VALUE_HEADS = 8
HEAD_SIZE = 64
CAP = 144
EPS = 1e-06
RESIDUAL_SCALE = 0.22
SCORE_SCALE = 0.015625
THETA = 10000.0
NEG_FILL = -1e30
LANES = 128

BF = jnp.bfloat16
F32 = jnp.float32
VMEM_LIMIT = 64 * 1024 * 1024 - 128 * 1024


def mm(a, b):
    return jnp.dot(a, b, preferred_element_type=F32)


def mm_nt(a, b):
    return lax.dot_general(a, b, (((1,), (1,)), ((), ())), preferred_element_type=F32)


def mm_tn(a, b):
    return lax.dot_general(a, b, (((0,), (0,)), ((), ())), preferred_element_type=F32)


def rope_tables(sequence_length):
    half = HEAD_SIZE // 2
    inverse = np.float32(THETA) ** (-(np.arange(half, dtype=np.float32) * 2.0) / HEAD_SIZE)
    angles = np.arange(sequence_length, dtype=np.float32)[:, None] * inverse.astype(np.float32)[None, :]
    cosine, sine = np.cos(angles), np.sin(angles)
    copies = LANES // HEAD_SIZE
    cosine = np.tile(np.concatenate([cosine, cosine], 1), (1, copies))
    sine = np.tile(np.concatenate([-sine, sine], 1), (1, copies))
    return cosine.astype(np.float32), sine.astype(np.float32)


def lane_iota(shape):
    return lax.broadcasted_iota(jnp.int32, shape, len(shape) - 1)


def turn(block, cosine, sine):
    half = HEAD_SIZE // 2
    lower = (lane_iota(block.shape) % HEAD_SIZE) < half
    partner = jnp.where(
        lower, pltpu.roll(block, LANES - half, 1), pltpu.roll(block, half, 1)
    )
    return block * cosine + partner * sine


def hint(flops, transcendentals, bytes_accessed, share=256):
    return pl.CostEstimate(
        flops=flops // share, transcendentals=transcendentals // share,
        bytes_accessed=bytes_accessed // share,
    )


def tile_ds(index, width):
    return pl.ds(pl.multiple_of(index * width, width), width)


def head_pair(block, place):
    lower = lane_iota(block.shape) < HEAD_SIZE
    moved = pltpu.roll(block, HEAD_SIZE, 1)
    zero = jnp.zeros_like(block)
    low, high = (block, moved) if place == 0 else (moved, block)
    return jnp.where(lower, low, zero), jnp.where(lower, zero, high)


def attention_forward_kernel(
    x_ref, w_ref, gain_one_ref, gain_two_ref, id_row_ref, id_col_ref, cos_ref, sin_ref, picks_ref,
    q_ref, k_ref, v_ref, att_ref, lse_ref, res_ref, pay_ref, gate_ref,
    normed_ref, bias_ref,
    *, q_width, kv_width, experts,
):
    rows, width = x_ref.shape
    x = x_ref[...].astype(F32)
    scale = lax.rsqrt(jnp.mean(x * x, axis=1, keepdims=True) + EPS)
    normed_ref[...] = (x * scale * gain_one_ref[...]).astype(BF)
    bias_ref[...] = jnp.where(id_col_ref[...] <= id_row_ref[...], 0.0, NEG_FILL)
    step = 256

    def project(out_ref, start, count, rotate):
        def body(j, carry):
            cols = pl.ds(pl.multiple_of(start + j * step, step), step)
            part = mm(normed_ref[...], w_ref[:, cols])
            if rotate:
                part = jnp.concatenate(
                    [
                        turn(part[:, i * LANES : (i + 1) * LANES], cos_ref[...], sin_ref[...])
                        for i in range(step // LANES)
                    ],
                    axis=1,
                )
            out_ref[:, tile_ds(j, step)] = part.astype(BF)
            return carry

        lax.fori_loop(0, count // step, body, 0)

    project(q_ref, 0, q_width, True)
    project(k_ref, q_width, kv_width, True)
    project(v_ref, q_width + kv_width, kv_width, False)

    def pair_body(j, carry):
        k_block = k_ref[:, tile_ds(j, LANES)].astype(F32)
        v_block = v_ref[:, tile_ds(j, LANES)].astype(F32)
        for place in range(2):
            keys = head_pair(k_block, place)
            vals = head_pair(v_block, place)
            group = 2 * j + place
            q_block = q_ref[:, tile_ds(group, LANES)]
            out = None
            for side in range(2):
                scores = mm_nt(keys[side].astype(BF), q_block) * SCORE_SCALE + bias_ref[...]
                highest = jnp.max(scores, axis=0, keepdims=True)
                lifted = jnp.exp(scores - highest)
                total = jnp.sum(lifted, axis=0, keepdims=True)
                low = (lifted * (1.0 / total)).astype(BF)
                lse_ref[pl.ds(2 * group + side, 1), :] = highest + jnp.log(total)
                part = mm_tn(vals[side].astype(BF), low)
                out = part if out is None else out + part
            att_ref[:, tile_ds(group, LANES)] = out.T.astype(BF)
        return carry

    lax.fori_loop(0, KEY_VALUE_HEADS // 2, pair_body, 0)

    start = q_width + 2 * kv_width

    def out_body(j, total):
        cols = pl.ds(pl.multiple_of(start + j * step, step), step)
        here = tile_ds(j, step)
        value = x_ref[:, here].astype(F32) + RESIDUAL_SCALE * mm(att_ref[...], w_ref[:, cols])
        res_ref[:, here] = value
        return total + jnp.sum(value * value, axis=1, keepdims=True)

    square = lax.fori_loop(0, width // step, out_body, jnp.zeros((rows, 1), F32))
    scale = lax.rsqrt(square * (1.0 / width) + EPS)
    pay_ref[:rows, :] = (res_ref[...] * scale * gain_two_ref[...]).astype(BF)
    logits = mm(pay_ref[:rows, :], w_ref[:, start + width :])
    lanes = lane_iota(logits.shape)
    chosen = lanes < 0
    for k in range(picks_ref.shape[1]):
        chosen = chosen | (picks_ref[:, k : k + 1] == lanes)
    masked = jnp.where(chosen, logits, NEG_FILL)
    lifted = jnp.where(chosen, jnp.exp(masked - jnp.max(masked, axis=1, keepdims=True)), 0.0)
    gates = lifted / jnp.sum(lifted, axis=1, keepdims=True)
    across = gates.T[:experts, :]
    gate_ref[...] = across
    high = across.astype(BF)
    pay_ref[rows:, :rows] = high
    pay_ref[rows:, rows:] = (across - high.astype(F32)).astype(BF)


def attention_forward(x, pack, gain_one, gain_two, ids, picks, tables, q_width, kv_width, experts):
    rows, width = x.shape
    out_shape = (
        jax.ShapeDtypeStruct((rows, q_width), BF),
        jax.ShapeDtypeStruct((rows, kv_width), BF),
        jax.ShapeDtypeStruct((rows, kv_width), BF),
        jax.ShapeDtypeStruct((rows, q_width), BF),
        jax.ShapeDtypeStruct((QUERY_HEADS, rows), F32),
        jax.ShapeDtypeStruct((rows, width), F32),
        jax.ShapeDtypeStruct((rows + experts, width), BF),
        jax.ShapeDtypeStruct((experts, rows), F32),
    )
    flops = 2 * rows * width * (q_width + 2 * kv_width + width) + 8 * QUERY_HEADS * rows * rows * 128
    return pl.pallas_call(
        functools.partial(
            attention_forward_kernel, q_width=q_width, kv_width=kv_width, experts=experts
        ),
        out_shape=out_shape,
        scratch_shapes=[pltpu.VMEM((rows, width), BF), pltpu.VMEM((rows, rows), F32)],
        compiler_params=pltpu.CompilerParams(vmem_limit_bytes=VMEM_LIMIT),
        cost_estimate=hint(
            flops=flops, transcendentals=QUERY_HEADS * rows * rows, bytes_accessed=16 << 20
        ),
        name="attention_forward",
    )(x, pack, gain_one, gain_two, ids[None, :], ids[:, None], *tables, picks)


def slot_marks(sel_ref, gate_rows, upper_ref, local):
    picked = mm(sel_ref[...], gate_rows)
    rows = picked.shape[1] // 2
    gates = picked[:, :rows] + picked[:, rows:]
    used = gates != 0.0
    rank = mm(used.astype(F32).astype(BF), upper_ref[...])
    slots = jnp.where(used, rank, -1.0)
    places = lax.broadcasted_iota(jnp.int32, (CAP, rows), 0).astype(F32)
    hits = [places == slots[e : e + 1, :] for e in range(local)]
    return gates, hits


def fill_upper(upper_ref):
    rows = upper_ref.shape[0]
    upper = lax.broadcasted_iota(jnp.int32, (rows, rows), 0) < lane_iota((rows, rows))
    upper_ref[...] = jnp.where(upper, 1.0, 0.0).astype(BF)


def dispatch_kernel(sel_ref, pay_ref, grad_ref, *refs, local):
    rows_ref, slot_ref, upper_ref = refs[-3:]

    @pl.when(pl.program_id(0) == 0)
    def _():
        fill_upper(upper_ref)

    rows = grad_ref.shape[1]
    gates, hits = slot_marks(sel_ref, pay_ref[0, rows:, :], upper_ref, local)
    marks = jnp.concatenate([jnp.where(h, 1.0, 0.0).astype(BF) for h in hits], axis=0)
    column = jnp.concatenate(
        [
            jnp.sum(jnp.where(h, gates[e : e + 1, :], 0.0), axis=1, keepdims=True)
            for e, h in enumerate(hits)
        ],
        axis=0,
    )
    moved = mm(marks, pay_ref[0, :rows, :]).astype(BF)
    grads = (column * (RESIDUAL_SCALE * mm(marks, grad_ref[0]))).astype(BF)
    for e in range(local):
        rows_ref[e, 0, 0] = moved[e * CAP : (e + 1) * CAP]
        slot_ref[e, 0, 0] = grads[e * CAP : (e + 1) * CAP]


def dispatch(sel, pays, grads, place, places, local, carried):
    count, rows, width = grads.shape
    shape = jax.ShapeDtypeStruct((local, places, count, CAP, width), BF)
    out_spec = pl.BlockSpec((local, 1, 1, CAP, width), lambda s: (0, place, s, 0, 0))
    in_specs = [
        pl.BlockSpec(sel.shape, lambda s: (0, 0)),
        pl.BlockSpec((1,) + pays.shape[1:], lambda s: (s, 0, 0)),
        pl.BlockSpec((1, rows, width), lambda s: (s, 0, 0)),
    ]
    operands = [sel, pays, grads]
    aliases = {}
    if carried is not None:
        operands += list(carried)
        in_specs += [pl.BlockSpec(memory_space=pl.ANY)] * 2
        aliases = {3: 0, 4: 1}
    return pl.pallas_call(
        functools.partial(dispatch_kernel, local=local),
        out_shape=(shape, shape),
        grid=(count,),
        in_specs=in_specs,
        out_specs=(out_spec, out_spec),
        scratch_shapes=[pltpu.VMEM((rows, rows), BF)],
        input_output_aliases=aliases,
        compiler_params=pltpu.CompilerParams(vmem_limit_bytes=VMEM_LIMIT),
        cost_estimate=hint(
            flops=4 * count * local * CAP * rows * width, transcendentals=0, bytes_accessed=20 << 20
        ),
        name="dispatch",
    )(*operands)


def expert_kernel(x_ref, s_ref, w_ref, *refs, chunk, tile, last, carried):
    if carried:
        prior_ref, refs = refs[0], refs[1:]
    (
        pr_ref, dg_ref, dot_ref, grad_ref,
        gate_ref, up_ref, down_ref, act_ref, both_ref, acc_in_ref, acc_down_ref,
    ) = refs
    rows, width = x_ref.shape[-2:]
    hidden = gate_ref.shape[-1]
    owners = grad_ref.shape[0]
    in_rows, down_rows = width // owners, hidden // owners
    step = pl.program_id(1)
    pieces = width // hidden

    @pl.when(step == 0)
    def _():
        for o in range(owners):
            gate_ref[o * in_rows : (o + 1) * in_rows, :] = w_ref[o, 0, :in_rows, :]
            up_ref[o * in_rows : (o + 1) * in_rows, :] = w_ref[o, 0, in_rows : 2 * in_rows, :]
            for c in range(pieces):
                first = 2 * in_rows + c * down_rows
                down_ref[o * down_rows : (o + 1) * down_rows, c * hidden : (c + 1) * hidden] = w_ref[
                    o, 0, first : first + down_rows, :
                ]

    def chunk_body(c, carry):
        here = tile_ds(c, chunk)
        x = x_ref[0, here, :]
        s = s_ref[0, here, :]
        pre_gate = mm(x, gate_ref[...])
        pre_up = mm(x, up_ref[...])
        act_grad = mm_nt(s, down_ref[...])
        logistic = jax.nn.sigmoid(pre_gate)
        swish = pre_gate * logistic
        act = (swish * pre_up).astype(BF)
        gate_in = (
            act_grad * pre_up * logistic * (1.0 + pre_gate * (1.0 - logistic))
        ).astype(BF)
        up_in = (act_grad * swish).astype(BF)
        dot_ref[0, here, :] = jnp.sum(act.astype(F32) * act_grad, axis=1, keepdims=True)
        act_ref[here, :] = act
        both_ref[here, :hidden] = gate_in
        both_ref[here, hidden:] = up_in
        pr_ref[0, here, :] = mm(act, down_ref[...]).astype(BF)
        dg_ref[0, here, :] = (mm_nt(gate_in, gate_ref[...]) + mm_nt(up_in, up_ref[...])).astype(BF)
        return carry

    lax.fori_loop(0, rows // chunk, chunk_body, 0)

    def put(owner, first, value):
        count = value.shape[0]
        if carried:
            value = value + prior_ref[owner, 0, first : first + count, :].astype(F32)
        grad_ref[owner, 0, first : first + count, :] = value.astype(BF)

    def accumulate(acc_ref, here, part, emit):
        if last == 0:
            emit(part)
            return

        @pl.when(step == 0)
        def _():
            acc_ref[here, :] = part

        if last > 1:

            @pl.when((step > 0) & (step < last))
            def _():
                acc_ref[here, :] = acc_ref[here, :] + part

        @pl.when(step == last)
        def _():
            emit(acc_ref[here, :] + part)

    def in_body(t, carry):
        here = tile_ds(t, tile)

        def emit(total):
            for i in range(tile // in_rows):
                piece = total[i * in_rows : (i + 1) * in_rows]
                owner = t * (tile // in_rows) + i
                put(owner, 0, piece[:, :hidden])
                put(owner, in_rows, piece[:, hidden:])

        accumulate(acc_in_ref, here, mm_tn(x_ref[0, :, here], both_ref[...]), emit)
        return carry

    lax.fori_loop(0, width // tile, in_body, 0)

    def down_body(t, carry):
        here = tile_ds(t, tile)

        def emit(total):
            for i in range(tile // down_rows):
                piece = total[i * down_rows : (i + 1) * down_rows]
                owner = t * (tile // down_rows) + i
                for c in range(pieces):
                    put(owner, 2 * in_rows + c * down_rows, piece[:, c * hidden : (c + 1) * hidden])

        accumulate(acc_down_ref, here, mm_tn(act_ref[:, here], s_ref[0]), emit)
        return carry

    lax.fori_loop(0, hidden // tile, down_body, 0)


def experts_step(first, weights, rows_in, slot_grad, prior):
    owners, count, packed, hidden = weights.shape
    _, total, width = rows_in.shape
    rows = 8 * CAP
    steps = total // rows
    out_shape = (
        jax.ShapeDtypeStruct((count, total, width), BF),
        jax.ShapeDtypeStruct((count, total, width), BF),
        jax.ShapeDtypeStruct((count, total, 1), F32),
        jax.ShapeDtypeStruct(weights.shape, BF),
    )
    in_spec = pl.BlockSpec((1, rows, width), lambda e, t: (first + e, t, 0))
    pack_spec = pl.BlockSpec((owners, 1, packed, hidden), lambda e, t: (0, e, 0, 0))
    row_spec = lambda last: pl.BlockSpec((1, rows, last), lambda e, t: (e, t, 0))
    operands = [rows_in, slot_grad, weights]
    in_specs = [in_spec, in_spec, pack_spec]
    if prior is not None:
        operands.append(prior)
        in_specs.append(pack_spec)
    kept = 0 if steps == 1 else 1
    return pl.pallas_call(
        functools.partial(
            expert_kernel, chunk=rows // 3, tile=256, last=steps - 1, carried=prior is not None
        ),
        out_shape=out_shape,
        grid=(count, steps),
        in_specs=in_specs,
        out_specs=(row_spec(width), row_spec(width), row_spec(1), pack_spec),
        scratch_shapes=[
            pltpu.VMEM((width, hidden), BF),
            pltpu.VMEM((width, hidden), BF),
            pltpu.VMEM((hidden, width), BF),
            pltpu.VMEM((rows, hidden), BF),
            pltpu.VMEM((rows, 2 * hidden), BF),
            pltpu.VMEM((width, 2 * hidden) if kept else (8, LANES), F32),
            pltpu.VMEM((hidden, width) if kept else (8, LANES), F32),
        ],
        compiler_params=pltpu.CompilerParams(vmem_limit_bytes=VMEM_LIMIT),
        cost_estimate=hint(
            flops=18 * count * total * width * hidden, transcendentals=count * total * hidden,
            bytes_accessed=30 << 20, share=256 if prior is None else 1,
        ),
        name="experts",
    )(*operands)


def combine_kernel(sel_ref, pay_ref, *refs, groups, local, received):
    produced, returned, dots = (refs[i * groups : (i + 1) * groups] for i in range(3))
    rest = refs[3 * groups :]
    if received:
        other_ref, rest = rest[0], rest[1:]
    out_refs, upper_ref = rest[:-1], rest[-1]
    each = local // groups

    @pl.when(pl.program_id(0) == 0)
    def _():
        fill_upper(upper_ref)

    rows = upper_ref.shape[0]
    gates, hits = slot_marks(sel_ref, pay_ref[0], upper_ref, local)
    weighted = jnp.concatenate(
        [jnp.where(h, gates[e : e + 1, :], 0.0).astype(BF) for e, h in enumerate(hits)], axis=0
    )
    plain = jnp.concatenate([jnp.where(h, 1.0, 0.0).astype(BF) for h in hits], axis=0)
    made = jnp.concatenate([r[e, 0] for r in produced for e in range(each)], axis=0)
    back = jnp.concatenate([r[e, 0] for r in returned for e in range(each)], axis=0)
    out = mm_tn(weighted, made)
    grads = mm_tn(plain, back)
    pad = jnp.zeros((8 - local, rows), F32)
    dot_rows = jnp.concatenate(
        [
            jnp.sum(jnp.where(h, dots[e // each][e % each, 0], 0.0), axis=0, keepdims=True)
            for e, h in enumerate(hits)
        ]
        + ([pad] if local < 8 else []),
        axis=0,
    )
    high = dot_rows.astype(BF)
    low = (dot_rows - high.astype(F32)).astype(BF)
    tail = jnp.concatenate([mm_tn(sel_ref[...], high), mm_tn(sel_ref[...], low)], axis=1)
    half = tail.shape[0] // 2
    first = jnp.concatenate([out, tail[:half]], axis=0)
    second = jnp.concatenate([tail[half:], grads], axis=0)
    if received:
        first = first + other_ref[0, : rows + half, :].astype(F32)
        second = second + other_ref[0, rows + half :, :].astype(F32)

        def put(index):
            out_refs[2 * index][...] = first.astype(BF)
            out_refs[2 * index + 1][...] = second.astype(BF)

        for index in range(len(out_refs) // 2):
            pl.when(pl.program_id(0) == index)(functools.partial(put, index))
    else:
        out_refs[0][0, : rows + half, :] = first.astype(BF)
        out_refs[0][0, rows + half :, :] = second.astype(BF)


def combine(sel, pays, produced, returned, dots, side, first, span, other):
    count, total_rows, width = pays.shape
    groups, each = len(produced), produced[0].shape[0]
    local = groups * each
    experts = sel.shape[1]
    rows = total_rows - experts
    pick = lambda last: pl.BlockSpec((each, 1, CAP, last), lambda s: (0, side * count + first + s, 0, 0))
    in_specs = [
        pl.BlockSpec(sel.shape, lambda s: (0, 0)),
        pl.BlockSpec((1, experts, width), lambda s: (first + s, rows // experts, 0)),
    ]
    in_specs += [pick(width)] * (2 * groups) + [pick(1)] * groups
    operands = [sel, pays, *produced, *returned, *dots]
    total = 2 * rows + experts
    out_spec = pl.BlockSpec((1, total, width), lambda s: (s, 0, 0))
    out_shape = (jax.ShapeDtypeStruct((span, total, width), BF),)
    out_specs = (out_spec,)
    if other is not None:
        operands.append(other)
        in_specs.append(out_spec)
        out_shape = (jax.ShapeDtypeStruct((total // 2, width), BF),) * (2 * span)
        out_specs = (pl.BlockSpec((total // 2, width), lambda s: (0, 0)),) * (2 * span)
    return pl.pallas_call(
        functools.partial(combine_kernel, groups=groups, local=local, received=other is not None),
        out_shape=out_shape,
        grid=(span,),
        in_specs=in_specs,
        out_specs=out_specs,
        scratch_shapes=[pltpu.VMEM((rows, rows), BF)],
        compiler_params=pltpu.CompilerParams(vmem_limit_bytes=VMEM_LIMIT),
        cost_estimate=hint(
            flops=4 * span * local * CAP * rows * width, transcendentals=0, bytes_accessed=20 << 20, share=1
        ),
        name="combine",
    )(*operands)


def attention_backward_kernel(
    *refs, terms, q_width, kv_width, experts, carried,
):
    (
        x_ref, w_ref, gain_one_ref, gain_two_ref, id_row_ref, id_col_ref, cos_ref, sin_ref,
        grad_ref, q_ref, k_ref, v_ref, att_ref, lse_ref, res_ref, pay_ref, gate_ref,
    ) = refs[:17]
    term_refs = refs[17 : 17 + 2 * terms]
    rest = refs[17 + 2 * terms :]
    if carried:
        prior_ref, rest = rest[0], rest[3:]
    out_ref, in_grad_ref, pack_ref, bias_ref, wide_ref, att_grad_ref, qkv_grad_ref, branch_ref, normed_ref = rest
    rows, width = x_ref.shape
    step = 256
    start = q_width + 2 * kv_width

    def put(row_slice, cols, value):
        if carried:
            value = value + prior_ref[row_slice, cols].astype(F32)
        pack_ref[row_slice, cols] = value.astype(BF)

    def gathered(which, low, high):
        total = term_refs[which][low:high, :].astype(F32)
        for ref in term_refs[2 + which :: 2]:
            total = total + ref[low:high, :].astype(F32)
        return total

    half = experts // 2
    residual = res_ref[...]
    out_ref[0] = (residual + RESIDUAL_SCALE * gathered(0, 0, rows)).astype(BF)
    tail = jnp.concatenate([gathered(0, rows, rows + half), gathered(1, 0, half)], axis=0)
    weighted = tail[:, :rows] + tail[:, rows:]
    chosen = weighted - gate_ref[...] * jnp.sum(weighted, axis=0, keepdims=True)
    chosen = jnp.concatenate([chosen, jnp.zeros((LANES - experts, rows), F32)], axis=0)
    logit_grad = chosen.T.astype(BF)
    moe_grad = gathered(1, half, half + rows) + mm_nt(logit_grad, w_ref[:, start + width :])
    last = mm_tn(pay_ref[:rows, :], logit_grad)
    scale = lax.rsqrt(jnp.mean(residual * residual, axis=1, keepdims=True) + EPS)
    gain_two_grad = jnp.sum(moe_grad * residual * scale, axis=0, keepdims=True)
    u = moe_grad * gain_two_ref[...]
    inner = jnp.sum(u * residual, axis=1, keepdims=True) * (1.0 / width)
    res_grad = grad_ref[...].astype(F32) + scale * u - residual * (scale * scale * scale * inner)
    in_grad_ref[0] = res_grad
    branch_ref[...] = (RESIDUAL_SCALE * res_grad).astype(BF)
    bias_ref[...] = jnp.where(id_col_ref[...] <= id_row_ref[...], 0.0, NEG_FILL)

    def branch_body(j, carry):
        here = tile_ds(j, step)
        att_grad_ref[:, here] = mm_nt(
            branch_ref[...], w_ref[here, start : start + width]
        ).astype(BF)
        part = mm_tn(att_ref[:, here], branch_ref[...])
        put(here, slice(start, start + width), part)
        return carry

    lax.fori_loop(0, q_width // step, branch_body, 0)

    lower = lane_iota((rows, LANES)) < HEAD_SIZE

    def pair_body(j, carry):
        k_block = k_ref[:, tile_ds(j, LANES)].astype(F32)
        v_block = v_ref[:, tile_ds(j, LANES)].astype(F32)
        k_sums, v_sums = [], []
        for place in range(2):
            keys = [h.astype(BF) for h in head_pair(k_block, place)]
            vals = [h.astype(BF) for h in head_pair(v_block, place)]
            group = 2 * j + place
            here = tile_ds(group, LANES)
            q_block = q_ref[:, here]
            g_block = att_grad_ref[:, here]
            q_out = None
            k_parts, v_parts = [], []
            for side in range(2):
                scores = mm_nt(keys[side], q_block) * SCORE_SCALE + bias_ref[...]
                probs = jnp.exp(scores - lse_ref[pl.ds(2 * group + side, 1), :])
                weight_grad = mm_nt(vals[side], g_block)
                v_parts.append(mm(probs.astype(BF), g_block))
                dots = jnp.sum(probs * weight_grad, axis=0, keepdims=True)
                score_grad = (probs * (weight_grad - dots)).astype(BF)
                k_parts.append(mm(score_grad, q_block))
                part = mm_tn(keys[side], score_grad)
                q_out = part if q_out is None else q_out + part
            q_turned = turn(q_out.T * SCORE_SCALE, cos_ref[...], -sin_ref[...])
            qkv_grad_ref[:, here] = q_turned.astype(BF)
            for parts, sums in ((k_parts, k_sums), (v_parts, v_sums)):
                mixed = jnp.where(lower, parts[0], parts[1])
                sums.append(mixed + pltpu.roll(mixed, HEAD_SIZE, 1))
        k_total = jnp.where(lower, k_sums[0], k_sums[1]) * SCORE_SCALE
        v_total = jnp.where(lower, v_sums[0], v_sums[1])
        k_here = pl.ds(pl.multiple_of(q_width + j * LANES, LANES), LANES)
        v_here = pl.ds(pl.multiple_of(q_width + kv_width + j * LANES, LANES), LANES)
        qkv_grad_ref[:, k_here] = turn(k_total, cos_ref[...], -sin_ref[...]).astype(BF)
        qkv_grad_ref[:, v_here] = v_total.astype(BF)
        return carry

    lax.fori_loop(0, KEY_VALUE_HEADS // 2, pair_body, 0)

    x = x_ref[...].astype(F32)
    scale = lax.rsqrt(jnp.mean(x * x, axis=1, keepdims=True) + EPS)
    normed_ref[...] = (x * scale * gain_one_ref[...]).astype(BF)

    def norm_body(j, carry):
        here = tile_ds(j, step)
        grad = mm_nt(qkv_grad_ref[...], w_ref[here, :start])
        put(here, slice(0, start), mm_tn(normed_ref[:, here], qkv_grad_ref[...]))
        wide_ref[:, here] = grad
        return carry

    lax.fori_loop(0, width // step, norm_body, 0)
    normed_grad = wide_ref[...]
    gain_one_grad = jnp.sum(normed_grad * x * scale, axis=0, keepdims=True)
    u = normed_grad * gain_one_ref[...]
    inner = jnp.sum(u * x, axis=1, keepdims=True) * (1.0 / width)
    in_grad_ref[0] = in_grad_ref[0] + scale * u - x * (scale * scale * scale * inner)
    lanes = lane_iota((width, LANES))
    one = jnp.broadcast_to(gain_one_grad, (LANES, width)).T
    two = jnp.broadcast_to(gain_two_grad, (LANES, width)).T
    last = jnp.where(lanes == experts, one, last)
    last = jnp.where(lanes == experts + 1, two, last)
    put(slice(0, width), slice(start + width, start + width + LANES), last)


def attention_backward(
    index, micro, x, pack, gain_one, gain_two, ids, tables, grad, saved, terms, prior, made, q_width, kv_width,
    experts,
):
    rows, width = x.shape
    operands = [x, pack, gain_one, gain_two, ids[None, :], ids[:, None], *tables, grad, *saved, *terms]
    whole = pl.BlockSpec(memory_space=pltpu.VMEM)
    in_specs = [whole] * len(operands)
    aliases = {}
    if prior is not None:
        operands += [prior, *made]
        in_specs += [whole] + [pl.BlockSpec(memory_space=pl.ANY)] * 2
        aliases = {len(operands) - 2: 0, len(operands) - 1: 1}
    row_spec = pl.BlockSpec((1, rows, width), lambda i: (index, 0, 0))
    flops = 4 * rows * width * (q_width + 2 * kv_width + width) + 20 * QUERY_HEADS * rows * rows * 128
    return pl.pallas_call(
        functools.partial(
            attention_backward_kernel, terms=len(terms) // 2, q_width=q_width, kv_width=kv_width,
            experts=experts, carried=prior is not None,
        ),
        out_shape=(
            jax.ShapeDtypeStruct((micro, rows, width), BF),
            jax.ShapeDtypeStruct((micro, rows, width), F32),
            jax.ShapeDtypeStruct(pack.shape, BF),
        ),
        grid=(1,),
        in_specs=in_specs,
        out_specs=(row_spec, row_spec, whole),
        input_output_aliases=aliases,
        scratch_shapes=[
            pltpu.VMEM((rows, rows), F32),
            pltpu.VMEM((rows, width), F32),
            pltpu.VMEM((rows, q_width), BF),
            pltpu.VMEM((rows, q_width + 2 * kv_width), BF),
            pltpu.VMEM((rows, width), BF),
            pltpu.VMEM((rows, width), BF),
        ],
        compiler_params=pltpu.CompilerParams(vmem_limit_bytes=VMEM_LIMIT),
        cost_estimate=hint(
            flops=flops, transcendentals=QUERY_HEADS * rows * rows, bytes_accessed=40 << 20, share=1
        ),
        name="attention_backward",
    )(*operands)


def peer_chip(chip, distance):
    total = 0
    for bit in (1, 2, 4):
        total = total + bit * ((chip // bit + (distance // bit) % 2) % 2)
    return total


def where_am_i():
    f, d = lax.axis_index("fsdp"), lax.axis_index("dp")
    return f // 2, f % 2, d


def meet(peers):
    barrier = pltpu.get_barrier_semaphore()
    for peer in peers:
        pl.semaphore_signal(
            barrier, inc=1, device_id=peer, device_id_type=pl.DeviceIdType.MESH
        )
    pl.semaphore_wait(barrier, len(peers))


def push(src, dst, send, receive, peer):
    copy = pltpu.make_async_remote_copy(
        src_ref=src, dst_ref=dst, send_sem=send, recv_sem=receive, device_id=peer,
        device_id_type=pl.DeviceIdType.MESH,
    )
    copy.start()
    return copy


def gather_layer_kernel(
    w_ref, out_ref, own_sem, z_send, z_receive, x_send, x_receive, s_send, s_receive, *, chips, depth
):
    chip, core, d = where_am_i()
    rows = w_ref.shape[0]
    others = [peer_chip(chip, r) for r in range(1, chips)]
    f, sibling = chip * 2 + core, chip * 2 + 1 - core

    def block(owner, layer):
        first = pl.multiple_of((owner * depth + layer) * rows, rows)
        return out_ref.at[pl.ds(first, rows), :]

    peers = [(f, (d + i) % depth) for i in range(1, depth)]
    peers += [(c * 2 + core, d) for c in others] + [(sibling, d)]
    meet(peers)
    own = pltpu.make_async_copy(w_ref, block(f, d), own_sem)
    own.start()
    z_copies = [
        push(w_ref, block(f, d), z_send.at[i - 1], z_receive.at[i - 1], (f, (d + i) % depth))
        for i in range(1, depth)
    ]
    x_copies, s_copies = [], []
    layers = [(d + depth - i) % depth for i in range(depth)]
    for i, layer in enumerate(layers):
        if i:
            z_copies[i - 1].wait_recv()
        src = block(f, layer) if i else w_ref
        for r, c in enumerate(others):
            x_copies.append(
                push(src, block(f, layer), x_send.at[i, r], x_receive.at[i, r], (c * 2 + core, d))
            )
        s_copies.append(
            push(src, block(f, layer), s_send.at[i, 0], s_receive.at[i, 0], (sibling, d))
        )
    for i, layer in enumerate(layers):
        for r, c in enumerate(others):
            x_copies[i * (chips - 1) + r].wait_recv()
            there = block(c * 2 + core, layer)
            s_copies.append(
                push(there, there, s_send.at[i, r + 1], s_receive.at[i, r + 1], (sibling, d))
            )
    own.wait()
    for copy in z_copies + x_copies:
        copy.wait_send()
    for copy in s_copies:
        copy.wait()


def gather_layer(pack, chips, depth):
    dma = pltpu.SemaphoreType.DMA
    rows, width = pack.shape
    return pl.pallas_call(
        functools.partial(gather_layer_kernel, chips=chips, depth=depth),
        out_shape=jax.ShapeDtypeStruct((rows * 2 * chips * depth, width), pack.dtype),
        in_specs=[pl.BlockSpec(memory_space=pl.ANY)],
        out_specs=pl.BlockSpec(memory_space=pl.ANY),
        scratch_shapes=[
            dma(()), dma((depth - 1,)), dma((depth - 1,)), dma((depth, chips - 1)),
            dma((depth, chips - 1)), dma((depth, chips)), dma((depth, chips)),
        ],
        compiler_params=pltpu.CompilerParams(collective_id=1, has_side_effects=True),
        name="gather_layer",
    )(pack)


def reduce_layer_kernel(
    pack_ref, out_ref, s_buf, s_sum, x_buf, x_sum, z_buf,
    s_send, s_receive, x_send, x_receive, z_send, z_receive,
    *, chips, depth, parts,
):
    chip, core, d = where_am_i()
    total, width = pack_ref.shape
    rows = total // (2 * chips * depth)
    span = rows * depth
    step = width // parts
    distances = list(range(1, chips))
    others = [peer_chip(chip, r) for r in distances]
    f, sibling = chip * 2 + core, chip * 2 + 1 - core
    peers = [(f, (d + i) % depth) for i in range(1, depth)]
    peers += [(c * 2 + core, d) for c in others] + [(sibling, d)]
    meet(peers)

    def band(p):
        return slice(p * step, (p + 1) * step)

    def mine(c, k):
        return pl.ds(pl.multiple_of((c * 2 + k) * span, span), span)

    order = [(r, c) for r, c in zip(distances, others)][::-1] + [(0, chip)]
    s_copies = {}
    for p in range(parts):
        for r, c in order:
            s_copies[p, r] = push(
                pack_ref.at[mine(c, 1 - core), band(p)], s_buf.at[r, :, band(p)],
                s_send.at[p, r], s_receive.at[p, r], (sibling, d),
            )
    x_copies, z_copies = {}, {}

    def sum_chip(p):
        for r, c in order:
            s_copies[p, r].wait_recv()
            value = pack_ref[mine(c, core), band(p)].astype(F32) + s_buf[r, :, band(p)].astype(F32)
            s_sum[r, :, band(p)] = value.astype(s_sum.dtype)

    def send_chip(p):
        for r, c in order[:-1]:
            x_copies[p, r] = push(
                s_sum.at[r, :, band(p)], x_buf.at[r - 1, :, band(p)], x_send.at[p, r - 1],
                x_receive.at[p, r - 1], (c * 2 + core, d),
            )

    def sum_plane(p):
        value = s_sum[0, :, band(p)].astype(F32)
        for r in distances:
            x_copies[p, r].wait_recv()
            value = value + x_buf[r - 1, :, band(p)].astype(F32)
        x_sum[:, :, band(p)] = value.reshape(depth, rows, step).astype(x_sum.dtype)

    def send_plane(p):
        for i in range(1, depth):
            to = (d + i) % depth
            z_copies[p, i] = push(
                x_sum.at[to, :, band(p)], z_buf.at[i - 1, :, band(p)], z_send.at[p, i - 1],
                z_receive.at[p, i - 1], (f, to),
            )

    def finish(p):
        value = x_sum[d, :, band(p)].astype(F32)
        for i in range(1, depth):
            z_copies[p, i].wait_recv()
            value = value + z_buf[i - 1, :, band(p)].astype(F32)
        out_ref[:, band(p)] = value

    for p in range(parts + 1):
        if p < parts:
            sum_chip(p)
        if p > 0:
            send_chip(p - 1)
    for p in range(parts + 1):
        if p < parts:
            sum_plane(p)
        if p > 0:
            send_plane(p - 1)
    for p in range(parts):
        finish(p)
    for copy in [*s_copies.values(), *x_copies.values(), *z_copies.values()]:
        copy.wait_send()


def reduce_layer(pack, chips, depth, parts):
    dma = pltpu.SemaphoreType.DMA
    total, width = pack.shape
    rows = total // (2 * chips * depth)
    kind = BF if rows % 16 == 0 else F32
    return pl.pallas_call(
        functools.partial(reduce_layer_kernel, chips=chips, depth=depth, parts=parts),
        out_shape=jax.ShapeDtypeStruct((rows, width), F32),
        in_specs=[pl.BlockSpec(memory_space=pltpu.VMEM)],
        out_specs=pl.BlockSpec(memory_space=pltpu.VMEM),
        scratch_shapes=[
            pltpu.VMEM((chips, rows * depth, width), BF),
            pltpu.VMEM((chips, rows * depth, width), BF),
            pltpu.VMEM((chips - 1, rows * depth, width), BF),
            pltpu.VMEM((depth, rows, width), kind),
            pltpu.VMEM((depth - 1, rows, width), kind),
            dma((parts, chips)), dma((parts, chips)), dma((parts, chips - 1)), dma((parts, chips - 1)),
            dma((parts, depth - 1)), dma((parts, depth - 1)),
        ],
        compiler_params=pltpu.CompilerParams(
            collective_id=2, has_side_effects=True, vmem_limit_bytes=VMEM_LIMIT
        ),
        cost_estimate=pl.CostEstimate(flops=0, transcendentals=0, bytes_accessed=1 << 30),
        name="reduce_layer",
    )(pack)


def swap(value, distance, size):
    return lax.ppermute(value, "fsdp", [(i, i ^ distance) for i in range(size)])


def after(value, *earlier):
    return lax.optimization_barrier((value, *earlier))[0] if earlier else value


def send_near(value, size):
    return swap(value, 2, size), swap(value, 4, size)


def gather_chips(value, near, size):
    chips = size // 2
    if near is None:
        return [value] + [swap(value, 2 * r, size) for r in range(1, chips)]
    half = value.shape[0] // 2
    one, two = near
    return [value, one, two, swap(one[:half], 4, size), swap(two[half:], 2, size)]


def both_cores(pieces, size, *earlier):
    if earlier:
        pieces = [pieces[0]] + [after(p, *earlier) for p in pieces[1:]]
    chips = size // 2
    last = pieces[chips - 1 :]
    mine = jnp.stack(pieces[: chips - 1] + [jnp.concatenate(last) if last[1:] else last[0]])
    return mine, swap(mine, 1, size)


def scatter_near(kept, size, *earlier):
    chips = size // 2
    if chips != 4:
        return [swap(kept[2 * r + h], 2 * r, size) for r in range(1, chips) for h in range(2)]
    return [swap(after(kept[6], *earlier), 2, size), swap(after(kept[7], *earlier), 4, size)]


def scatter_far(kept, near, size, *earlier):
    if size != 8:
        return (), ()
    add = lambda a, b: (a.astype(F32) + b.astype(F32)).astype(BF)
    by_one, by_two = after(near[0], *earlier), after(near[1], *earlier)
    one_sum, two_sum = add(kept[3], by_two), add(kept[4], by_one)
    return (one_sum, two_sum), (swap(one_sum, 2, size), swap(two_sum, 4, size))


def scatter_rest(kept, size, *earlier):
    if size != 8:
        return ()
    return swap(after(kept[2], *earlier), 2, size), swap(after(kept[5], *earlier), 4, size)


def scattered(kept, near, far, rest):
    if not far:
        return [kept[0], kept[1]] + near
    return [kept[0], kept[1], rest[0], far[0], far[1], rest[1]]


def local(
    inputs, block_ids, routes, out_grad, norm_gain, w_query, key_weight, value_weight, w_output,
    moe_gain, w_router, w_gate, w_up, w_down,
):
    micro, _, rows, width = inputs.shape
    experts = w_router.shape[1]
    held, in_rows, hidden = w_gate.shape
    down_rows = w_down.shape[1]
    q_width, kv_width = w_query.shape[1], key_weight.shape[1]
    owners = lax.axis_size("fsdp")
    depth = lax.axis_size("dp")
    chips = owners // 2
    tables = tuple(jnp.asarray(t) for t in rope_tables(rows))
    start = q_width + 2 * kv_width + width
    group = max(1, held // 2)
    cuts = width // hidden

    split_down = w_down.reshape(held, down_rows, cuts, hidden).transpose(0, 2, 1, 3)
    packed = jnp.concatenate(
        [w_gate, w_up, split_down.reshape(held, cuts * down_rows, hidden)], axis=1
    )
    weights = [
        lax.all_gather(packed[g : g + group], "dp", axis=0, tiled=False)
        for g in range(0, held, group)
    ]
    pieces = [
        w_query, key_weight, value_weight, w_output, w_router, norm_gain[:, None], moe_gain[:, None]
    ]
    filled = sum(p.shape[1] for p in pieces)
    pieces.append(jnp.zeros((w_query.shape[0], start + LANES - filled), BF))
    pack = gather_layer(jnp.concatenate(pieces, axis=1), chips, depth)
    gain_one = pack[:, start + experts].astype(F32)[None, :]
    gain_two = pack[:, start + experts + 1].astype(F32)[None, :]
    first = lax.axis_index("fsdp") * held
    places = jnp.arange(8)[:, None]
    sel = ((jnp.arange(experts)[None, :] == first + places) & (places < held)).astype(BF)
    square = chips == 4

    def forward(m, x):
        return attention_forward(
            x, pack, gain_one, gain_two, block_ids[m, 0], routes[m, 0], tables, q_width, kv_width, experts
        )

    def dispatched(pay, grad, carried):
        side = 0 if carried is None else 1
        return dispatch(sel, pay[side], grad[side], side, 2, held, carried)

    def flat(carried):
        return [c.reshape(held, 2 * chips * CAP, width) for c in carried]

    saved, arrived, pays, moved, done, terms = [], [], [], [], {}, []
    ready = ()
    for m in range(micro):
        grad = after(out_grad[m, 0], *ready)
        grad_near = None
        if square and m:
            grad_near = tuple(after(near, first_half[0]) for near in send_near(grad, owners))
        found_grad = gather_chips(grad, grad_near, owners)
        if m == 0:
            saved.append(forward(0, after(inputs[0, 0], *found_grad[1:])))
            for n in range(1, micro):
                saved.append(forward(n, after(inputs[n, 0], saved[n - 1][4])))
        pay = after(saved[m][6], *ready, *(grad_near or ()))
        pay_near = None
        if square and m == 0:
            one, two = send_near(pay, owners)
            pay_near = after(one, saved[-1][4]), after(two, saved[-1][4])
        found_pay = gather_chips(pay, pay_near, owners)
        ready = tuple(found_pay[chips - 1 :])
        arrived.append((found_pay, found_grad, grad_near))
        if m == 0:
            first_grad = both_cores(found_grad, owners)
            pays.append(both_cores(found_pay, owners, first_grad[0]))
            first_half = dispatched(pays[0], first_grad, None)

    def expert_part(m, g, *earlier):
        prior = done[m - 1, g][3] if m else None
        rows_in, slot_grad = moved[m]
        if earlier:
            rows_in = after(rows_in, *earlier)
        done[m, g] = experts_step(g * group, weights[g], rows_in, slot_grad, prior)

    def returned(m, earlier):
        parts = [
            [done[m, g][i].reshape(group, 2 * chips, CAP, -1) for g in range(len(weights))]
            for i in range(3)
        ]
        kept, before = [], earlier
        sent = {}
        span = chips // 2
        for first in (span, 0):
            (sent[first],) = combine(sel, after(pays[m][1], *before), *parts, 1, first, span, None)
            before = (sent[first],)
        for first in (span, 0):
            found = combine(
                sel, after(pays[m][0], *before), *parts, 0, first, span, swap(sent[first], 1, owners)
            )
            before = (found[0],)
            kept = list(found) + kept
        return kept

    def backward(m, found, made, prior):
        out, in_grad, prior = attention_backward(
            m, micro, inputs[m, 0], pack, gain_one, gain_two, block_ids[m, 0], tables, out_grad[m, 0],
            saved[m], found, prior, made, q_width, kv_width, experts,
        )
        return (out, in_grad), prior

    added, far, rest = (), (), ()
    for m in range(micro):
        if m == 0:
            moved.append(flat(dispatched(pays[0], first_grad, first_half)))
            hold = arrived[1][2] if micro > 1 and square else ()
            expert_part(0, 0, *hold)
        else:
            found_grad = both_cores(arrived[m][1], owners, done[m - 1, 0][2])
            pays.append(both_cores(arrived[m][0], owners, found_grad[0]))
            half = dispatched(pays[m], found_grad, None)
            for g in range(1, len(weights)):
                expert_part(m - 1, g, half[0])
            kept = returned(m - 1, far)
            other = after(pays[m][1], kept[0], kept[-1])
            moved.append(flat(dispatched((None, other), found_grad, half)))
            near = scatter_near(kept, owners, *rest)
            expert_part(m, 0, kept[0], kept[-1])
            added, far = scatter_far(kept, near, owners, done[m, 0][2])
            rest = scatter_rest(kept, owners, *far)
            terms.append(scattered(kept, near, far, rest))
    for g in range(1, len(weights)):
        expert_part(micro - 1, g, *added)
    kept = returned(micro - 1, far)
    near = scatter_near(kept, owners, *rest)
    last_rest = scatter_rest(kept, owners, *rest)
    made, prior, held_back = None, None, ()
    for m in range(micro - 1):
        made, prior = backward(m, [after(terms[m][0], kept[0], kept[-1])] + terms[m][1:], made, prior)
        held_back = (prior,)
    last_far = scatter_far(kept, near, owners, *held_back)[1]
    terms.append(scattered(kept, near, last_far, last_rest))
    made, prior = backward(micro - 1, terms[-1], made, prior)
    sums = []
    for g in range(len(weights)):
        summed = after(done[micro - 1, g][3], *(far if g else added))
        sums.append(lax.psum_scatter(summed, "dp", scatter_dimension=0, tiled=True)[0])
    layer = reduce_layer(prior, chips, depth, 5)
    marks = np.cumsum([0, q_width, kv_width, kv_width, width, experts, 1, 1])
    cut = [layer[:, a:b] for a, b in zip(marks[:-1], marks[1:])]
    stacked = jnp.concatenate(sums, axis=0).astype(F32)
    grad_down = stacked[:, 2 * in_rows :].reshape(held, cuts, down_rows, hidden)
    grad_down = grad_down.transpose(0, 2, 1, 3).reshape(held, down_rows, width)
    return (
        made[0][:, None],
        made[1][:, None],
        cut[5][:, 0], cut[0], cut[1], cut[2], cut[3], cut[6][:, 0], cut[4],
        stacked[:, :in_rows], stacked[:, in_rows : 2 * in_rows], grad_down,
    )


def solution(mesh):
    rows = ("fsdp", "dp")
    split = lambda rank: P(None, rows, *([None] * (rank - 2)))
    flat = P(rows, None)
    expert_spec = P("fsdp", "dp", None)
    in_specs = (
        split(4), split(3), split(4), split(4), P(rows), flat, flat, flat, flat, P(rows), flat,
        expert_spec, expert_spec, expert_spec,
    )
    out_specs = (
        split(4), split(4), P(rows), flat, flat, flat, flat, P(rows), flat,
        expert_spec, expert_spec, expert_spec,
    )
    return jax.shard_map(local, mesh=mesh, in_specs=in_specs, out_specs=out_specs, check_vma=False)
```

```python
import functools

import jax
import jax.numpy as jnp
import numpy as np
from jax import lax
from jax.experimental import pallas as pl
from jax.experimental.pallas import tpu as pltpu
from jax.sharding import PartitionSpec as P

QUERY_HEADS = 16
KEY_VALUE_HEADS = 8
HEAD_SIZE = 64
CAP = 144
EPS = 1e-06
RESIDUAL_SCALE = 0.22
SCORE_SCALE = 0.015625
THETA = 10000.0
NEG_FILL = -1e30
LANES = 128

BF = jnp.bfloat16
F32 = jnp.float32
VMEM_LIMIT = 64 * 1024 * 1024 - 128 * 1024


def mm(a, b):
    return jnp.dot(a, b, preferred_element_type=F32)


def mm_nt(a, b):
    return lax.dot_general(a, b, (((1,), (1,)), ((), ())), preferred_element_type=F32)


def mm_tn(a, b):
    return lax.dot_general(a, b, (((0,), (0,)), ((), ())), preferred_element_type=F32)


def rope_tables(sequence_length):
    half = HEAD_SIZE // 2
    inverse = np.float32(THETA) ** (-(np.arange(half, dtype=np.float32) * 2.0) / HEAD_SIZE)
    angles = np.arange(sequence_length, dtype=np.float32)[:, None] * inverse.astype(np.float32)[None, :]
    cosine, sine = np.cos(angles), np.sin(angles)
    copies = LANES // HEAD_SIZE
    cosine = np.tile(np.concatenate([cosine, cosine], 1), (1, copies))
    sine = np.tile(np.concatenate([-sine, sine], 1), (1, copies))
    return cosine.astype(np.float32), sine.astype(np.float32)


def lane_iota(shape):
    return lax.broadcasted_iota(jnp.int32, shape, len(shape) - 1)


def turn(block, cosine, sine):
    half = HEAD_SIZE // 2
    lower = (lane_iota(block.shape) % HEAD_SIZE) < half
    partner = jnp.where(
        lower, pltpu.roll(block, LANES - half, 1), pltpu.roll(block, half, 1)
    )
    return block * cosine + partner * sine


def hint(flops, transcendentals, bytes_accessed, share=256):
    return pl.CostEstimate(
        flops=flops // share, transcendentals=transcendentals // share,
        bytes_accessed=bytes_accessed // share,
    )


def tile_ds(index, width):
    return pl.ds(pl.multiple_of(index * width, width), width)


def head_pair(block, place):
    lower = lane_iota(block.shape) < HEAD_SIZE
    moved = pltpu.roll(block, HEAD_SIZE, 1)
    zero = jnp.zeros_like(block)
    low, high = (block, moved) if place == 0 else (moved, block)
    return jnp.where(lower, low, zero), jnp.where(lower, zero, high)


def attention_forward_kernel(
    x_ref, w_ref, gain_one_ref, gain_two_ref, id_row_ref, id_col_ref, cos_ref, sin_ref, picks_ref,
    q_ref, k_ref, v_ref, att_ref, lse_ref, res_ref, pay_ref, gate_ref,
    normed_ref, bias_ref,
    *, q_width, kv_width, experts,
):
    rows, width = x_ref.shape
    x = x_ref[...].astype(F32)
    scale = lax.rsqrt(jnp.mean(x * x, axis=1, keepdims=True) + EPS)
    normed_ref[...] = (x * scale * gain_one_ref[...]).astype(BF)
    bias_ref[...] = jnp.where(id_col_ref[...] <= id_row_ref[...], 0.0, NEG_FILL)
    step = 256

    def project(out_ref, start, count, rotate):
        def body(j, carry):
            cols = pl.ds(pl.multiple_of(start + j * step, step), step)
            part = mm(normed_ref[...], w_ref[:, cols])
            if rotate:
                part = jnp.concatenate(
                    [
                        turn(part[:, i * LANES : (i + 1) * LANES], cos_ref[...], sin_ref[...])
                        for i in range(step // LANES)
                    ],
                    axis=1,
                )
            out_ref[:, tile_ds(j, step)] = part.astype(BF)
            return carry

        lax.fori_loop(0, count // step, body, 0)

    project(q_ref, 0, q_width, True)
    project(k_ref, q_width, kv_width, True)
    project(v_ref, q_width + kv_width, kv_width, False)

    def pair_body(j, carry):
        k_block = k_ref[:, tile_ds(j, LANES)].astype(F32)
        v_block = v_ref[:, tile_ds(j, LANES)].astype(F32)
        for place in range(2):
            keys = head_pair(k_block, place)
            vals = head_pair(v_block, place)
            group = 2 * j + place
            q_block = q_ref[:, tile_ds(group, LANES)]
            out = None
            for side in range(2):
                scores = mm_nt(keys[side].astype(BF), q_block) * SCORE_SCALE + bias_ref[...]
                highest = jnp.max(scores, axis=0, keepdims=True)
                lifted = jnp.exp(scores - highest)
                total = jnp.sum(lifted, axis=0, keepdims=True)
                low = (lifted * (1.0 / total)).astype(BF)
                lse_ref[pl.ds(2 * group + side, 1), :] = highest + jnp.log(total)
                part = mm_tn(vals[side].astype(BF), low)
                out = part if out is None else out + part
            att_ref[:, tile_ds(group, LANES)] = out.T.astype(BF)
        return carry

    lax.fori_loop(0, KEY_VALUE_HEADS // 2, pair_body, 0)

    start = q_width + 2 * kv_width

    def out_body(j, total):
        cols = pl.ds(pl.multiple_of(start + j * step, step), step)
        here = tile_ds(j, step)
        value = x_ref[:, here].astype(F32) + RESIDUAL_SCALE * mm(att_ref[...], w_ref[:, cols])
        res_ref[:, here] = value
        return total + jnp.sum(value * value, axis=1, keepdims=True)

    square = lax.fori_loop(0, width // step, out_body, jnp.zeros((rows, 1), F32))
    scale = lax.rsqrt(square * (1.0 / width) + EPS)
    pay_ref[:rows, :] = (res_ref[...] * scale * gain_two_ref[...]).astype(BF)
    logits = mm(pay_ref[:rows, :], w_ref[:, start + width :])
    lanes = lane_iota(logits.shape)
    chosen = lanes < 0
    for k in range(picks_ref.shape[1]):
        chosen = chosen | (picks_ref[:, k : k + 1] == lanes)
    masked = jnp.where(chosen, logits, NEG_FILL)
    lifted = jnp.where(chosen, jnp.exp(masked - jnp.max(masked, axis=1, keepdims=True)), 0.0)
    gates = lifted / jnp.sum(lifted, axis=1, keepdims=True)
    across = gates.T[:experts, :]
    gate_ref[...] = across
    high = across.astype(BF)
    pay_ref[rows:, :rows] = high
    pay_ref[rows:, rows:] = (across - high.astype(F32)).astype(BF)


def attention_forward(x, pack, gain_one, gain_two, ids, picks, tables, q_width, kv_width, experts):
    rows, width = x.shape
    out_shape = (
        jax.ShapeDtypeStruct((rows, q_width), BF),
        jax.ShapeDtypeStruct((rows, kv_width), BF),
        jax.ShapeDtypeStruct((rows, kv_width), BF),
        jax.ShapeDtypeStruct((rows, q_width), BF),
        jax.ShapeDtypeStruct((QUERY_HEADS, rows), F32),
        jax.ShapeDtypeStruct((rows, width), F32),
        jax.ShapeDtypeStruct((rows + experts, width), BF),
        jax.ShapeDtypeStruct((experts, rows), F32),
    )
    flops = 2 * rows * width * (q_width + 2 * kv_width + width) + 8 * QUERY_HEADS * rows * rows * 128
    return pl.pallas_call(
        functools.partial(
            attention_forward_kernel, q_width=q_width, kv_width=kv_width, experts=experts
        ),
        out_shape=out_shape,
        scratch_shapes=[pltpu.VMEM((rows, width), BF), pltpu.VMEM((rows, rows), F32)],
        compiler_params=pltpu.CompilerParams(vmem_limit_bytes=VMEM_LIMIT),
        cost_estimate=hint(
            flops=flops, transcendentals=QUERY_HEADS * rows * rows, bytes_accessed=64 << 20, share=1
        ),
        name="attention_forward",
    )(x, pack, gain_one, gain_two, ids[None, :], ids[:, None], *tables, picks)


def slot_marks(sel_ref, gate_rows, upper_ref, local):
    picked = mm(sel_ref[...], gate_rows)
    rows = picked.shape[1] // 2
    gates = picked[:, :rows] + picked[:, rows:]
    used = gates != 0.0
    rank = mm(used.astype(F32).astype(BF), upper_ref[...])
    slots = jnp.where(used, rank, -1.0)
    places = lax.broadcasted_iota(jnp.int32, (CAP, rows), 0).astype(F32)
    hits = [places == slots[e : e + 1, :] for e in range(local)]
    return gates, hits


def fill_upper(upper_ref):
    rows = upper_ref.shape[0]
    upper = lax.broadcasted_iota(jnp.int32, (rows, rows), 0) < lane_iota((rows, rows))
    upper_ref[...] = jnp.where(upper, 1.0, 0.0).astype(BF)


def dispatch_kernel(sel_ref, pay_ref, grad_ref, *refs, local):
    rows_ref, slot_ref, upper_ref = refs[-3:]

    @pl.when(pl.program_id(0) == 0)
    def _():
        fill_upper(upper_ref)

    rows = grad_ref.shape[1]
    gates, hits = slot_marks(sel_ref, pay_ref[0, rows:, :], upper_ref, local)
    marks = jnp.concatenate([jnp.where(h, 1.0, 0.0).astype(BF) for h in hits], axis=0)
    column = jnp.concatenate(
        [
            jnp.sum(jnp.where(h, gates[e : e + 1, :], 0.0), axis=1, keepdims=True)
            for e, h in enumerate(hits)
        ],
        axis=0,
    )
    moved = mm(marks, pay_ref[0, :rows, :]).astype(BF)
    grads = (column * (RESIDUAL_SCALE * mm(marks, grad_ref[0]))).astype(BF)
    for e in range(local):
        rows_ref[e, 0, 0] = moved[e * CAP : (e + 1) * CAP]
        slot_ref[e, 0, 0] = grads[e * CAP : (e + 1) * CAP]


def dispatch(sel, pays, grads, place, places, local, carried):
    count, rows, width = grads.shape
    shape = jax.ShapeDtypeStruct((local, places, count, CAP, width), BF)
    out_spec = pl.BlockSpec((local, 1, 1, CAP, width), lambda s: (0, place, s, 0, 0))
    in_specs = [
        pl.BlockSpec(sel.shape, lambda s: (0, 0)),
        pl.BlockSpec((1,) + pays.shape[1:], lambda s: (s, 0, 0)),
        pl.BlockSpec((1, rows, width), lambda s: (s, 0, 0)),
    ]
    operands = [sel, pays, grads]
    aliases = {}
    if carried is not None:
        operands += list(carried)
        in_specs += [pl.BlockSpec(memory_space=pl.ANY)] * 2
        aliases = {3: 0, 4: 1}
    return pl.pallas_call(
        functools.partial(dispatch_kernel, local=local),
        out_shape=(shape, shape),
        grid=(count,),
        in_specs=in_specs,
        out_specs=(out_spec, out_spec),
        scratch_shapes=[pltpu.VMEM((rows, rows), BF)],
        input_output_aliases=aliases,
        compiler_params=pltpu.CompilerParams(vmem_limit_bytes=VMEM_LIMIT),
        cost_estimate=hint(
            flops=4 * count * local * CAP * rows * width, transcendentals=0, bytes_accessed=20 << 20
        ),
        name="dispatch",
    )(*operands)


def expert_kernel(x_ref, s_ref, w_ref, *refs, chunk, tile, last, carried):
    if carried:
        prior_ref, refs = refs[0], refs[1:]
    (
        pr_ref, dg_ref, dot_ref, grad_ref,
        gate_ref, up_ref, down_ref, act_ref, both_ref, acc_in_ref, acc_down_ref,
    ) = refs
    rows, width = x_ref.shape[-2:]
    hidden = gate_ref.shape[-1]
    owners = grad_ref.shape[0]
    in_rows, down_rows = width // owners, hidden // owners
    step = pl.program_id(1)
    pieces = width // hidden

    @pl.when(step == 0)
    def _():
        for o in range(owners):
            gate_ref[o * in_rows : (o + 1) * in_rows, :] = w_ref[o, 0, :in_rows, :]
            up_ref[o * in_rows : (o + 1) * in_rows, :] = w_ref[o, 0, in_rows : 2 * in_rows, :]
            for c in range(pieces):
                first = 2 * in_rows + c * down_rows
                down_ref[o * down_rows : (o + 1) * down_rows, c * hidden : (c + 1) * hidden] = w_ref[
                    o, 0, first : first + down_rows, :
                ]

    def chunk_body(c, carry):
        here = tile_ds(c, chunk)
        x = x_ref[0, here, :]
        s = s_ref[0, here, :]
        pre_gate = mm(x, gate_ref[...])
        pre_up = mm(x, up_ref[...])
        act_grad = mm_nt(s, down_ref[...])
        logistic = jax.nn.sigmoid(pre_gate)
        swish = pre_gate * logistic
        act = (swish * pre_up).astype(BF)
        gate_in = (
            act_grad * pre_up * logistic * (1.0 + pre_gate * (1.0 - logistic))
        ).astype(BF)
        up_in = (act_grad * swish).astype(BF)
        dot_ref[0, here, :] = jnp.sum(act.astype(F32) * act_grad, axis=1, keepdims=True)
        act_ref[here, :] = act
        both_ref[here, :hidden] = gate_in
        both_ref[here, hidden:] = up_in
        pr_ref[0, here, :] = mm(act, down_ref[...]).astype(BF)
        dg_ref[0, here, :] = (mm_nt(gate_in, gate_ref[...]) + mm_nt(up_in, up_ref[...])).astype(BF)
        return carry

    lax.fori_loop(0, rows // chunk, chunk_body, 0)

    def put(owner, first, value):
        count = value.shape[0]
        if carried:
            value = value + prior_ref[owner, 0, first : first + count, :].astype(F32)
        grad_ref[owner, 0, first : first + count, :] = value.astype(BF)

    def accumulate(acc_ref, here, part, emit):
        if last == 0:
            emit(part)
            return

        @pl.when(step == 0)
        def _():
            acc_ref[here, :] = part

        if last > 1:

            @pl.when((step > 0) & (step < last))
            def _():
                acc_ref[here, :] = acc_ref[here, :] + part

        @pl.when(step == last)
        def _():
            emit(acc_ref[here, :] + part)

    def in_body(t, carry):
        here = tile_ds(t, tile)

        def emit(total):
            for i in range(tile // in_rows):
                piece = total[i * in_rows : (i + 1) * in_rows]
                owner = t * (tile // in_rows) + i
                put(owner, 0, piece[:, :hidden])
                put(owner, in_rows, piece[:, hidden:])

        accumulate(acc_in_ref, here, mm_tn(x_ref[0, :, here], both_ref[...]), emit)
        return carry

    lax.fori_loop(0, width // tile, in_body, 0)

    def down_body(t, carry):
        here = tile_ds(t, tile)

        def emit(total):
            for i in range(tile // down_rows):
                piece = total[i * down_rows : (i + 1) * down_rows]
                owner = t * (tile // down_rows) + i
                for c in range(pieces):
                    put(owner, 2 * in_rows + c * down_rows, piece[:, c * hidden : (c + 1) * hidden])

        accumulate(acc_down_ref, here, mm_tn(act_ref[:, here], s_ref[0]), emit)
        return carry

    lax.fori_loop(0, hidden // tile, down_body, 0)


def experts_step(first, weights, rows_in, slot_grad, prior):
    owners, count, packed, hidden = weights.shape
    _, total, width = rows_in.shape
    rows = 8 * CAP
    steps = total // rows
    out_shape = (
        jax.ShapeDtypeStruct((count, total, width), BF),
        jax.ShapeDtypeStruct((count, total, width), BF),
        jax.ShapeDtypeStruct((count, total, 1), F32),
        jax.ShapeDtypeStruct(weights.shape, BF),
    )
    in_spec = pl.BlockSpec((1, rows, width), lambda e, t: (first + e, t, 0))
    pack_spec = pl.BlockSpec((owners, 1, packed, hidden), lambda e, t: (0, e, 0, 0))
    row_spec = lambda last: pl.BlockSpec((1, rows, last), lambda e, t: (e, t, 0))
    operands = [rows_in, slot_grad, weights]
    in_specs = [in_spec, in_spec, pack_spec]
    if prior is not None:
        operands.append(prior)
        in_specs.append(pack_spec)
    kept = 0 if steps == 1 else 1
    return pl.pallas_call(
        functools.partial(
            expert_kernel, chunk=rows // 3, tile=256, last=steps - 1, carried=prior is not None
        ),
        out_shape=out_shape,
        grid=(count, steps),
        in_specs=in_specs,
        out_specs=(row_spec(width), row_spec(width), row_spec(1), pack_spec),
        scratch_shapes=[
            pltpu.VMEM((width, hidden), BF),
            pltpu.VMEM((width, hidden), BF),
            pltpu.VMEM((hidden, width), BF),
            pltpu.VMEM((rows, hidden), BF),
            pltpu.VMEM((rows, 2 * hidden), BF),
            pltpu.VMEM((width, 2 * hidden) if kept else (8, LANES), F32),
            pltpu.VMEM((hidden, width) if kept else (8, LANES), F32),
        ],
        compiler_params=pltpu.CompilerParams(vmem_limit_bytes=VMEM_LIMIT),
        cost_estimate=hint(
            flops=18 * count * total * width * hidden, transcendentals=count * total * hidden,
            bytes_accessed=30 << 20, share=256 if prior is None else 1,
        ),
        name="experts",
    )(*operands)


def combine_kernel(sel_ref, pay_ref, *refs, groups, local, received):
    produced, returned, dots = (refs[i * groups : (i + 1) * groups] for i in range(3))
    rest = refs[3 * groups :]
    if received:
        other_ref, rest = rest[0], rest[1:]
    out_refs, upper_ref = rest[:-1], rest[-1]
    each = local // groups

    @pl.when(pl.program_id(0) == 0)
    def _():
        fill_upper(upper_ref)

    rows = upper_ref.shape[0]
    gates, hits = slot_marks(sel_ref, pay_ref[0], upper_ref, local)
    weighted = jnp.concatenate(
        [jnp.where(h, gates[e : e + 1, :], 0.0).astype(BF) for e, h in enumerate(hits)], axis=0
    )
    plain = jnp.concatenate([jnp.where(h, 1.0, 0.0).astype(BF) for h in hits], axis=0)
    made = jnp.concatenate([r[e, 0] for r in produced for e in range(each)], axis=0)
    back = jnp.concatenate([r[e, 0] for r in returned for e in range(each)], axis=0)
    out = mm_tn(weighted, made)
    grads = mm_tn(plain, back)
    pad = jnp.zeros((8 - local, rows), F32)
    dot_rows = jnp.concatenate(
        [
            jnp.sum(jnp.where(h, dots[e // each][e % each, 0], 0.0), axis=0, keepdims=True)
            for e, h in enumerate(hits)
        ]
        + ([pad] if local < 8 else []),
        axis=0,
    )
    high = dot_rows.astype(BF)
    low = (dot_rows - high.astype(F32)).astype(BF)
    tail = jnp.concatenate([mm_tn(sel_ref[...], high), mm_tn(sel_ref[...], low)], axis=1)
    half = tail.shape[0] // 2
    first = jnp.concatenate([out, tail[:half]], axis=0)
    second = jnp.concatenate([tail[half:], grads], axis=0)
    if received:
        first = first + other_ref[0, : rows + half, :].astype(F32)
        second = second + other_ref[0, rows + half :, :].astype(F32)

        def put(index):
            out_refs[2 * index][...] = first.astype(BF)
            out_refs[2 * index + 1][...] = second.astype(BF)

        for index in range(len(out_refs) // 2):
            pl.when(pl.program_id(0) == index)(functools.partial(put, index))
    else:
        out_refs[0][0, : rows + half, :] = first.astype(BF)
        out_refs[0][0, rows + half :, :] = second.astype(BF)


def combine(sel, pays, produced, returned, dots, side, first, span, other):
    count, total_rows, width = pays.shape
    groups, each = len(produced), produced[0].shape[0]
    local = groups * each
    experts = sel.shape[1]
    rows = total_rows - experts
    pick = lambda last: pl.BlockSpec((each, 1, CAP, last), lambda s: (0, side * count + first + s, 0, 0))
    in_specs = [
        pl.BlockSpec(sel.shape, lambda s: (0, 0)),
        pl.BlockSpec((1, experts, width), lambda s: (first + s, rows // experts, 0)),
    ]
    in_specs += [pick(width)] * (2 * groups) + [pick(1)] * groups
    operands = [sel, pays, *produced, *returned, *dots]
    total = 2 * rows + experts
    out_spec = pl.BlockSpec((1, total, width), lambda s: (s, 0, 0))
    out_shape = (jax.ShapeDtypeStruct((span, total, width), BF),)
    out_specs = (out_spec,)
    if other is not None:
        operands.append(other)
        in_specs.append(out_spec)
        out_shape = (jax.ShapeDtypeStruct((total // 2, width), BF),) * (2 * span)
        out_specs = (pl.BlockSpec((total // 2, width), lambda s: (0, 0)),) * (2 * span)
    return pl.pallas_call(
        functools.partial(combine_kernel, groups=groups, local=local, received=other is not None),
        out_shape=out_shape,
        grid=(span,),
        in_specs=in_specs,
        out_specs=out_specs,
        scratch_shapes=[pltpu.VMEM((rows, rows), BF)],
        compiler_params=pltpu.CompilerParams(vmem_limit_bytes=VMEM_LIMIT),
        cost_estimate=hint(
            flops=4 * span * local * CAP * rows * width, transcendentals=0, bytes_accessed=20 << 20, share=1
        ),
        name="combine",
    )(*operands)


def attention_backward_kernel(
    *refs, terms, q_width, kv_width, experts, carried,
):
    (
        x_ref, w_ref, gain_one_ref, gain_two_ref, id_row_ref, id_col_ref, cos_ref, sin_ref,
        grad_ref, q_ref, k_ref, v_ref, att_ref, lse_ref, res_ref, pay_ref, gate_ref,
    ) = refs[:17]
    term_refs = refs[17 : 17 + 2 * terms]
    rest = refs[17 + 2 * terms :]
    if carried:
        prior_ref, rest = rest[0], rest[3:]
    out_ref, in_grad_ref, pack_ref, bias_ref, wide_ref, att_grad_ref, qkv_grad_ref, branch_ref, normed_ref = rest
    rows, width = x_ref.shape
    step = 256
    start = q_width + 2 * kv_width

    def put(row_slice, cols, value):
        if carried:
            value = value + prior_ref[row_slice, cols].astype(F32)
        pack_ref[row_slice, cols] = value.astype(BF)

    def gathered(which, low, high):
        total = term_refs[which][low:high, :].astype(F32)
        for ref in term_refs[2 + which :: 2]:
            total = total + ref[low:high, :].astype(F32)
        return total

    half = experts // 2
    residual = res_ref[...]
    out_ref[0] = (residual + RESIDUAL_SCALE * gathered(0, 0, rows)).astype(BF)
    tail = jnp.concatenate([gathered(0, rows, rows + half), gathered(1, 0, half)], axis=0)
    weighted = tail[:, :rows] + tail[:, rows:]
    chosen = weighted - gate_ref[...] * jnp.sum(weighted, axis=0, keepdims=True)
    chosen = jnp.concatenate([chosen, jnp.zeros((LANES - experts, rows), F32)], axis=0)
    logit_grad = chosen.T.astype(BF)
    moe_grad = gathered(1, half, half + rows) + mm_nt(logit_grad, w_ref[:, start + width :])
    last = mm_tn(pay_ref[:rows, :], logit_grad)
    scale = lax.rsqrt(jnp.mean(residual * residual, axis=1, keepdims=True) + EPS)
    gain_two_grad = jnp.sum(moe_grad * residual * scale, axis=0, keepdims=True)
    u = moe_grad * gain_two_ref[...]
    inner = jnp.sum(u * residual, axis=1, keepdims=True) * (1.0 / width)
    res_grad = grad_ref[...].astype(F32) + scale * u - residual * (scale * scale * scale * inner)
    in_grad_ref[0] = res_grad
    branch_ref[...] = (RESIDUAL_SCALE * res_grad).astype(BF)
    bias_ref[...] = jnp.where(id_col_ref[...] <= id_row_ref[...], 0.0, NEG_FILL)

    def branch_body(j, carry):
        here = tile_ds(j, step)
        att_grad_ref[:, here] = mm_nt(
            branch_ref[...], w_ref[here, start : start + width]
        ).astype(BF)
        part = mm_tn(att_ref[:, here], branch_ref[...])
        put(here, slice(start, start + width), part)
        return carry

    lax.fori_loop(0, q_width // step, branch_body, 0)

    lower = lane_iota((rows, LANES)) < HEAD_SIZE

    def pair_body(j, carry):
        k_block = k_ref[:, tile_ds(j, LANES)].astype(F32)
        v_block = v_ref[:, tile_ds(j, LANES)].astype(F32)
        k_sums, v_sums = [], []
        for place in range(2):
            keys = [h.astype(BF) for h in head_pair(k_block, place)]
            vals = [h.astype(BF) for h in head_pair(v_block, place)]
            group = 2 * j + place
            here = tile_ds(group, LANES)
            q_block = q_ref[:, here]
            g_block = att_grad_ref[:, here]
            q_out = None
            k_parts, v_parts = [], []
            for side in range(2):
                scores = mm_nt(keys[side], q_block) * SCORE_SCALE + bias_ref[...]
                probs = jnp.exp(scores - lse_ref[pl.ds(2 * group + side, 1), :])
                weight_grad = mm_nt(vals[side], g_block)
                v_parts.append(mm(probs.astype(BF), g_block))
                dots = jnp.sum(probs * weight_grad, axis=0, keepdims=True)
                score_grad = (probs * (weight_grad - dots)).astype(BF)
                k_parts.append(mm(score_grad, q_block))
                part = mm_tn(keys[side], score_grad)
                q_out = part if q_out is None else q_out + part
            q_turned = turn(q_out.T * SCORE_SCALE, cos_ref[...], -sin_ref[...])
            qkv_grad_ref[:, here] = q_turned.astype(BF)
            for parts, sums in ((k_parts, k_sums), (v_parts, v_sums)):
                mixed = jnp.where(lower, parts[0], parts[1])
                sums.append(mixed + pltpu.roll(mixed, HEAD_SIZE, 1))
        k_total = jnp.where(lower, k_sums[0], k_sums[1]) * SCORE_SCALE
        v_total = jnp.where(lower, v_sums[0], v_sums[1])
        k_here = pl.ds(pl.multiple_of(q_width + j * LANES, LANES), LANES)
        v_here = pl.ds(pl.multiple_of(q_width + kv_width + j * LANES, LANES), LANES)
        qkv_grad_ref[:, k_here] = turn(k_total, cos_ref[...], -sin_ref[...]).astype(BF)
        qkv_grad_ref[:, v_here] = v_total.astype(BF)
        return carry

    lax.fori_loop(0, KEY_VALUE_HEADS // 2, pair_body, 0)

    x = x_ref[...].astype(F32)
    scale = lax.rsqrt(jnp.mean(x * x, axis=1, keepdims=True) + EPS)
    normed_ref[...] = (x * scale * gain_one_ref[...]).astype(BF)

    def norm_body(j, carry):
        here = tile_ds(j, step)
        grad = mm_nt(qkv_grad_ref[...], w_ref[here, :start])
        put(here, slice(0, start), mm_tn(normed_ref[:, here], qkv_grad_ref[...]))
        wide_ref[:, here] = grad
        return carry

    lax.fori_loop(0, width // step, norm_body, 0)
    normed_grad = wide_ref[...]
    gain_one_grad = jnp.sum(normed_grad * x * scale, axis=0, keepdims=True)
    u = normed_grad * gain_one_ref[...]
    inner = jnp.sum(u * x, axis=1, keepdims=True) * (1.0 / width)
    in_grad_ref[0] = in_grad_ref[0] + scale * u - x * (scale * scale * scale * inner)
    lanes = lane_iota((width, LANES))
    one = jnp.broadcast_to(gain_one_grad, (LANES, width)).T
    two = jnp.broadcast_to(gain_two_grad, (LANES, width)).T
    last = jnp.where(lanes == experts, one, last)
    last = jnp.where(lanes == experts + 1, two, last)
    put(slice(0, width), slice(start + width, start + width + LANES), last)


def attention_backward(
    index, micro, x, pack, gain_one, gain_two, ids, tables, grad, saved, terms, prior, made, q_width, kv_width,
    experts,
):
    rows, width = x.shape
    operands = [x, pack, gain_one, gain_two, ids[None, :], ids[:, None], *tables, grad, *saved, *terms]
    whole = pl.BlockSpec(memory_space=pltpu.VMEM)
    in_specs = [whole] * len(operands)
    aliases = {}
    if prior is not None:
        operands += [prior, *made]
        in_specs += [whole] + [pl.BlockSpec(memory_space=pl.ANY)] * 2
        aliases = {len(operands) - 2: 0, len(operands) - 1: 1}
    row_spec = pl.BlockSpec((1, rows, width), lambda i: (index, 0, 0))
    flops = 4 * rows * width * (q_width + 2 * kv_width + width) + 20 * QUERY_HEADS * rows * rows * 128
    return pl.pallas_call(
        functools.partial(
            attention_backward_kernel, terms=len(terms) // 2, q_width=q_width, kv_width=kv_width,
            experts=experts, carried=prior is not None,
        ),
        out_shape=(
            jax.ShapeDtypeStruct((micro, rows, width), BF),
            jax.ShapeDtypeStruct((micro, rows, width), F32),
            jax.ShapeDtypeStruct(pack.shape, BF),
        ),
        grid=(1,),
        in_specs=in_specs,
        out_specs=(row_spec, row_spec, whole),
        input_output_aliases=aliases,
        scratch_shapes=[
            pltpu.VMEM((rows, rows), F32),
            pltpu.VMEM((rows, width), F32),
            pltpu.VMEM((rows, q_width), BF),
            pltpu.VMEM((rows, q_width + 2 * kv_width), BF),
            pltpu.VMEM((rows, width), BF),
            pltpu.VMEM((rows, width), BF),
        ],
        compiler_params=pltpu.CompilerParams(vmem_limit_bytes=VMEM_LIMIT),
        cost_estimate=hint(
            flops=flops, transcendentals=QUERY_HEADS * rows * rows, bytes_accessed=40 << 20, share=1
        ),
        name="attention_backward",
    )(*operands)


def peer_chip(chip, distance):
    total = 0
    for bit in (1, 2, 4):
        total = total + bit * ((chip // bit + (distance // bit) % 2) % 2)
    return total


def where_am_i():
    f, d = lax.axis_index("fsdp"), lax.axis_index("dp")
    return f // 2, f % 2, d


def meet(peers):
    barrier = pltpu.get_barrier_semaphore()
    for peer in peers:
        pl.semaphore_signal(
            barrier, inc=1, device_id=peer, device_id_type=pl.DeviceIdType.MESH
        )
    pl.semaphore_wait(barrier, len(peers))


def push(src, dst, send, receive, peer):
    copy = pltpu.make_async_remote_copy(
        src_ref=src, dst_ref=dst, send_sem=send, recv_sem=receive, device_id=peer,
        device_id_type=pl.DeviceIdType.MESH,
    )
    copy.start()
    return copy


def gather_layer_kernel(
    w_ref, out_ref, own_sem, z_send, z_receive, x_send, x_receive, s_send, s_receive, *, chips, depth
):
    chip, core, d = where_am_i()
    rows = w_ref.shape[0]
    others = [peer_chip(chip, r) for r in range(1, chips)]
    f, sibling = chip * 2 + core, chip * 2 + 1 - core

    def block(owner, layer):
        first = pl.multiple_of((owner * depth + layer) * rows, rows)
        return out_ref.at[pl.ds(first, rows), :]

    peers = [(f, (d + i) % depth) for i in range(1, depth)]
    peers += [(c * 2 + core, d) for c in others] + [(sibling, d)]
    meet(peers)
    own = pltpu.make_async_copy(w_ref, block(f, d), own_sem)
    own.start()
    z_copies = [
        push(w_ref, block(f, d), z_send.at[i - 1], z_receive.at[i - 1], (f, (d + i) % depth))
        for i in range(1, depth)
    ]
    x_copies, s_copies = [], []
    layers = [(d + depth - i) % depth for i in range(depth)]
    for i, layer in enumerate(layers):
        if i:
            z_copies[i - 1].wait_recv()
        src = block(f, layer) if i else w_ref
        for r, c in enumerate(others):
            x_copies.append(
                push(src, block(f, layer), x_send.at[i, r], x_receive.at[i, r], (c * 2 + core, d))
            )
        s_copies.append(
            push(src, block(f, layer), s_send.at[i, 0], s_receive.at[i, 0], (sibling, d))
        )
    for i, layer in enumerate(layers):
        for r, c in enumerate(others):
            x_copies[i * (chips - 1) + r].wait_recv()
            there = block(c * 2 + core, layer)
            s_copies.append(
                push(there, there, s_send.at[i, r + 1], s_receive.at[i, r + 1], (sibling, d))
            )
    own.wait()
    for copy in z_copies + x_copies:
        copy.wait_send()
    for copy in s_copies:
        copy.wait()


def gather_layer(pack, chips, depth):
    dma = pltpu.SemaphoreType.DMA
    rows, width = pack.shape
    return pl.pallas_call(
        functools.partial(gather_layer_kernel, chips=chips, depth=depth),
        out_shape=jax.ShapeDtypeStruct((rows * 2 * chips * depth, width), pack.dtype),
        in_specs=[pl.BlockSpec(memory_space=pl.ANY)],
        out_specs=pl.BlockSpec(memory_space=pl.ANY),
        scratch_shapes=[
            dma(()), dma((depth - 1,)), dma((depth - 1,)), dma((depth, chips - 1)),
            dma((depth, chips - 1)), dma((depth, chips)), dma((depth, chips)),
        ],
        compiler_params=pltpu.CompilerParams(collective_id=1, has_side_effects=True),
        name="gather_layer",
    )(pack)


def reduce_layer_kernel(
    pack_ref, out_ref, s_buf, s_sum, x_buf, x_sum, z_buf,
    s_send, s_receive, x_send, x_receive, z_send, z_receive,
    *, chips, depth, parts,
):
    chip, core, d = where_am_i()
    total, width = pack_ref.shape
    rows = total // (2 * chips * depth)
    span = rows * depth
    step = width // parts
    distances = list(range(1, chips))
    others = [peer_chip(chip, r) for r in distances]
    f, sibling = chip * 2 + core, chip * 2 + 1 - core
    peers = [(f, (d + i) % depth) for i in range(1, depth)]
    peers += [(c * 2 + core, d) for c in others] + [(sibling, d)]
    meet(peers)

    def band(p):
        return slice(p * step, (p + 1) * step)

    def mine(c, k):
        return pl.ds(pl.multiple_of((c * 2 + k) * span, span), span)

    order = [(r, c) for r, c in zip(distances, others)][::-1] + [(0, chip)]
    s_copies = {}
    for p in range(parts):
        for r, c in order:
            s_copies[p, r] = push(
                pack_ref.at[mine(c, 1 - core), band(p)], s_buf.at[r, :, band(p)],
                s_send.at[p, r], s_receive.at[p, r], (sibling, d),
            )
    x_copies, z_copies = {}, {}

    def sum_chip(p):
        for r, c in order:
            s_copies[p, r].wait_recv()
            value = pack_ref[mine(c, core), band(p)].astype(F32) + s_buf[r, :, band(p)].astype(F32)
            s_sum[r, :, band(p)] = value.astype(s_sum.dtype)

    def send_chip(p):
        for r, c in order[:-1]:
            x_copies[p, r] = push(
                s_sum.at[r, :, band(p)], x_buf.at[r - 1, :, band(p)], x_send.at[p, r - 1],
                x_receive.at[p, r - 1], (c * 2 + core, d),
            )

    def sum_plane(p):
        value = s_sum[0, :, band(p)].astype(F32)
        for r in distances:
            x_copies[p, r].wait_recv()
            value = value + x_buf[r - 1, :, band(p)].astype(F32)
        x_sum[:, :, band(p)] = value.reshape(depth, rows, step).astype(x_sum.dtype)

    def send_plane(p):
        for i in range(1, depth):
            to = (d + i) % depth
            z_copies[p, i] = push(
                x_sum.at[to, :, band(p)], z_buf.at[i - 1, :, band(p)], z_send.at[p, i - 1],
                z_receive.at[p, i - 1], (f, to),
            )

    def finish(p):
        value = x_sum[d, :, band(p)].astype(F32)
        for i in range(1, depth):
            z_copies[p, i].wait_recv()
            value = value + z_buf[i - 1, :, band(p)].astype(F32)
        out_ref[:, band(p)] = value

    for p in range(parts + 1):
        if p < parts:
            sum_chip(p)
        if p > 0:
            send_chip(p - 1)
    for p in range(parts + 1):
        if p < parts:
            sum_plane(p)
        if p > 0:
            send_plane(p - 1)
    for p in range(parts):
        finish(p)
    for copy in [*s_copies.values(), *x_copies.values(), *z_copies.values()]:
        copy.wait_send()


def reduce_layer(pack, chips, depth, parts):
    dma = pltpu.SemaphoreType.DMA
    total, width = pack.shape
    rows = total // (2 * chips * depth)
    kind = BF if rows % 16 == 0 else F32
    return pl.pallas_call(
        functools.partial(reduce_layer_kernel, chips=chips, depth=depth, parts=parts),
        out_shape=jax.ShapeDtypeStruct((rows, width), F32),
        in_specs=[pl.BlockSpec(memory_space=pltpu.VMEM)],
        out_specs=pl.BlockSpec(memory_space=pltpu.VMEM),
        scratch_shapes=[
            pltpu.VMEM((chips, rows * depth, width), BF),
            pltpu.VMEM((chips, rows * depth, width), BF),
            pltpu.VMEM((chips - 1, rows * depth, width), BF),
            pltpu.VMEM((depth, rows, width), kind),
            pltpu.VMEM((depth - 1, rows, width), kind),
            dma((parts, chips)), dma((parts, chips)), dma((parts, chips - 1)), dma((parts, chips - 1)),
            dma((parts, depth - 1)), dma((parts, depth - 1)),
        ],
        compiler_params=pltpu.CompilerParams(
            collective_id=2, has_side_effects=True, vmem_limit_bytes=VMEM_LIMIT
        ),
        cost_estimate=pl.CostEstimate(flops=0, transcendentals=0, bytes_accessed=1 << 30),
        name="reduce_layer",
    )(pack)


def swap(value, distance, size):
    return lax.ppermute(value, "fsdp", [(i, i ^ distance) for i in range(size)])


def after(value, *earlier):
    return lax.optimization_barrier((value, *earlier))[0] if earlier else value


def send_near(value, size):
    return swap(value, 2, size), swap(value, 4, size)


def gather_chips(value, near, size):
    chips = size // 2
    if near is None:
        return [value] + [swap(value, 2 * r, size) for r in range(1, chips)]
    half = value.shape[0] // 2
    one, two = near
    return [value, one, two, swap(one[:half], 4, size), swap(two[half:], 2, size)]


def both_cores(pieces, size, *earlier):
    if earlier:
        pieces = [pieces[0]] + [after(p, *earlier) for p in pieces[1:]]
    chips = size // 2
    last = pieces[chips - 1 :]
    mine = jnp.stack(pieces[: chips - 1] + [jnp.concatenate(last) if last[1:] else last[0]])
    return mine, swap(mine, 1, size)


def scatter_near(kept, size, *earlier):
    chips = size // 2
    if chips != 4:
        return [swap(kept[2 * r + h], 2 * r, size) for r in range(1, chips) for h in range(2)]
    return [swap(after(kept[6], *earlier), 2, size), swap(after(kept[7], *earlier), 4, size)]


def scatter_far(kept, near, size, *earlier, rest=()):
    if size != 8:
        return (), ()
    add = lambda a, b: (a.astype(F32) + b.astype(F32)).astype(BF)
    by_one, by_two = after(near[0], *earlier), after(near[1], *earlier, *rest[:1])
    one_sum, two_sum = add(kept[3], by_two), add(kept[4], by_one)
    return (one_sum, two_sum), (swap(one_sum, 2, size), swap(two_sum, 4, size))


def scatter_rest(kept, size, *earlier):
    if size != 8:
        return ()
    return swap(after(kept[2], *earlier), 2, size), swap(after(kept[5], *earlier), 4, size)


def scattered(kept, near, far, rest):
    if not far:
        return [kept[0], kept[1]] + near
    return [kept[0], kept[1], rest[0], far[0], far[1], rest[1]]


def local(
    inputs, block_ids, routes, out_grad, norm_gain, w_query, key_weight, value_weight, w_output,
    moe_gain, w_router, w_gate, w_up, w_down,
):
    micro, _, rows, width = inputs.shape
    experts = w_router.shape[1]
    held, in_rows, hidden = w_gate.shape
    down_rows = w_down.shape[1]
    q_width, kv_width = w_query.shape[1], key_weight.shape[1]
    owners = lax.axis_size("fsdp")
    depth = lax.axis_size("dp")
    chips = owners // 2
    tables = tuple(jnp.asarray(t) for t in rope_tables(rows))
    start = q_width + 2 * kv_width + width
    group = max(1, held // 2)
    cuts = width // hidden

    split_down = w_down.reshape(held, down_rows, cuts, hidden).transpose(0, 2, 1, 3)
    packed = jnp.concatenate(
        [w_gate, w_up, split_down.reshape(held, cuts * down_rows, hidden)], axis=1
    )
    weights = [
        lax.all_gather(packed[g : g + group], "dp", axis=0, tiled=False)
        for g in range(0, held, group)
    ]
    pieces = [
        w_query, key_weight, value_weight, w_output, w_router, norm_gain[:, None], moe_gain[:, None]
    ]
    filled = sum(p.shape[1] for p in pieces)
    pieces.append(jnp.zeros((w_query.shape[0], start + LANES - filled), BF))
    pack = gather_layer(jnp.concatenate(pieces, axis=1), chips, depth)
    gain_one = pack[:, start + experts].astype(F32)[None, :]
    gain_two = pack[:, start + experts + 1].astype(F32)[None, :]
    first = lax.axis_index("fsdp") * held
    places = jnp.arange(8)[:, None]
    sel = ((jnp.arange(experts)[None, :] == first + places) & (places < held)).astype(BF)
    square = chips == 4

    def forward(m, x):
        return attention_forward(
            x, pack, gain_one, gain_two, block_ids[m, 0], routes[m, 0], tables, q_width, kv_width, experts
        )

    def dispatched(pay, grad, carried):
        side = 0 if carried is None else 1
        return dispatch(sel, pay[side], grad[side], side, 2, held, carried)

    def flat(carried):
        return [c.reshape(held, 2 * chips * CAP, width) for c in carried]

    saved, arrived, pays, moved, done, terms = [], [], [], [], {}, []
    ready = (pack,)
    for m in range(micro):
        grad = after(out_grad[m, 0], *ready)
        grad_near = None
        if square and m:
            grad_near = tuple(after(near, first_half[0]) for near in send_near(grad, owners))
        found_grad = gather_chips(grad, grad_near, owners)
        if m == 0:
            saved.append(forward(0, inputs[0, 0]))
            for n in range(1, micro):
                saved.append(forward(n, after(inputs[n, 0], saved[n - 1][4], *found_grad[1:])))
        pay = after(saved[m][6], *ready, *(grad_near or ()))
        pay_near = None
        if square and m == 0:
            one, two = send_near(pay, owners)
            pay_near = after(one, saved[-1][4]), after(two, saved[-1][4])
        found_pay = gather_chips(pay, pay_near, owners)
        ready = tuple(found_pay[chips - 1 :])
        arrived.append((found_pay, found_grad, grad_near))
        if m == 0:
            first_grad = both_cores(found_grad, owners)
            pays.append(both_cores(found_pay, owners, first_grad[0]))
            first_half = dispatched(pays[0], first_grad, None)

    def expert_part(m, g, *earlier):
        prior = done[m - 1, g][3] if m else None
        rows_in, slot_grad = moved[m]
        if earlier:
            rows_in = after(rows_in, *earlier)
        done[m, g] = experts_step(g * group, weights[g], rows_in, slot_grad, prior)

    def returned(m, earlier):
        parts = [
            [done[m, g][i].reshape(group, 2 * chips, CAP, -1) for g in range(len(weights))]
            for i in range(3)
        ]
        kept, before = [], ()
        sent = {}
        span = chips // 2
        for first in (span, 0):
            (sent[first],) = combine(sel, after(pays[m][1], *before), *parts, 1, first, span, None)
            before = (sent[first], *earlier)
        for first in (span, 0):
            found = combine(
                sel, after(pays[m][0], *before), *parts, 0, first, span, swap(sent[first], 1, owners)
            )
            before = (found[0],)
            kept = list(found) + kept
        return kept

    def backward(m, found, made, prior):
        out, in_grad, prior = attention_backward(
            m, micro, inputs[m, 0], pack, gain_one, gain_two, block_ids[m, 0], tables, out_grad[m, 0],
            saved[m], found, prior, made, q_width, kv_width, experts,
        )
        return (out, in_grad), prior

    added, far, rest = (), (), ()
    for m in range(micro):
        if m == 0:
            moved.append(flat(dispatched(pays[0], first_grad, first_half)))
            hold = arrived[1][2] if micro > 1 and square else ()
            expert_part(0, 0, *hold)
        else:
            found_grad = both_cores(arrived[m][1], owners, done[m - 1, 0][2])
            pays.append(both_cores(arrived[m][0], owners, found_grad[0]))
            half = dispatched(pays[m], found_grad, None)
            for g in range(1, len(weights)):
                expert_part(m - 1, g, half[0])
            kept = returned(m - 1, (*far, *rest))
            other = after(pays[m][1], kept[0], kept[-1])
            moved.append(flat(dispatched((None, other), found_grad, half)))
            near = scatter_near(kept, owners)
            expert_part(m, 0, kept[0], kept[-1])
            added, far = scatter_far(kept, near, owners, done[m, 0][2])
            rest = scatter_rest(kept, owners, *near)
            terms.append(scattered(kept, near, far, rest))
    for g in range(1, len(weights)):
        expert_part(micro - 1, g, *added)
    kept = returned(micro - 1, (*far, *rest))
    near = scatter_near(kept, owners)
    last_rest = scatter_rest(kept, owners)
    made, prior, held_back = None, None, ()
    for m in range(micro - 1):
        made, prior = backward(m, [after(terms[m][0], kept[0], kept[-1])] + terms[m][1:], made, prior)
        held_back = (prior,)
    last_far = scatter_far(kept, near, owners, *held_back, rest=last_rest)[1]
    terms.append(scattered(kept, near, last_far, last_rest))
    made, prior = backward(micro - 1, terms[-1], made, prior)
    sums = []
    for g in range(len(weights)):
        summed = after(done[micro - 1, g][3], *((kept[0], kept[-1]) if g else added))
        sums.append(lax.psum_scatter(summed, "dp", scatter_dimension=0, tiled=True)[0])
    layer = reduce_layer(prior, chips, depth, 5)
    marks = np.cumsum([0, q_width, kv_width, kv_width, width, experts, 1, 1])
    cut = [layer[:, a:b] for a, b in zip(marks[:-1], marks[1:])]
    stacked = jnp.concatenate(sums, axis=0).astype(F32)
    grad_down = stacked[:, 2 * in_rows :].reshape(held, cuts, down_rows, hidden)
    grad_down = grad_down.transpose(0, 2, 1, 3).reshape(held, down_rows, width)
    return (
        made[0][:, None],
        made[1][:, None],
        cut[5][:, 0], cut[0], cut[1], cut[2], cut[3], cut[6][:, 0], cut[4],
        stacked[:, :in_rows], stacked[:, in_rows : 2 * in_rows], grad_down,
    )


def solution(mesh):
    rows = ("fsdp", "dp")
    split = lambda rank: P(None, rows, *([None] * (rank - 2)))
    flat = P(rows, None)
    expert_spec = P("fsdp", "dp", None)
    in_specs = (
        split(4), split(3), split(4), split(4), P(rows), flat, flat, flat, flat, P(rows), flat,
        expert_spec, expert_spec, expert_spec,
    )
    out_specs = (
        split(4), split(4), P(rows), flat, flat, flat, flat, P(rows), flat,
        expert_spec, expert_spec, expert_spec,
    )
    return jax.shard_map(local, mesh=mesh, in_specs=in_specs, out_specs=out_specs, check_vma=False)
```

```python
import functools

import jax
import jax.numpy as jnp
import numpy as np
from jax import lax
from jax.experimental import pallas as pl
from jax.experimental.pallas import tpu as pltpu
from jax.sharding import PartitionSpec as P

QUERY_HEADS = 16
KEY_VALUE_HEADS = 8
HEAD_SIZE = 64
CAP = 144
EPS = 1e-06
RESIDUAL_SCALE = 0.22
SCORE_SCALE = 0.015625
THETA = 10000.0
NEG_FILL = -1e30
LANES = 128

BF = jnp.bfloat16
F32 = jnp.float32
VMEM_LIMIT = 64 * 1024 * 1024 - 128 * 1024


def mm(a, b):
    return jnp.dot(a, b, preferred_element_type=F32)


def mm_nt(a, b):
    return lax.dot_general(a, b, (((1,), (1,)), ((), ())), preferred_element_type=F32)


def mm_tn(a, b):
    return lax.dot_general(a, b, (((0,), (0,)), ((), ())), preferred_element_type=F32)


def rope_tables(sequence_length):
    half = HEAD_SIZE // 2
    inverse = np.float32(THETA) ** (-(np.arange(half, dtype=np.float32) * 2.0) / HEAD_SIZE)
    angles = np.arange(sequence_length, dtype=np.float32)[:, None] * inverse.astype(np.float32)[None, :]
    cosine, sine = np.cos(angles), np.sin(angles)
    copies = LANES // HEAD_SIZE
    cosine = np.tile(np.concatenate([cosine, cosine], 1), (1, copies))
    sine = np.tile(np.concatenate([-sine, sine], 1), (1, copies))
    return cosine.astype(np.float32), sine.astype(np.float32)


def lane_iota(shape):
    return lax.broadcasted_iota(jnp.int32, shape, len(shape) - 1)


def turn(block, cosine, sine):
    half = HEAD_SIZE // 2
    lower = (lane_iota(block.shape) % HEAD_SIZE) < half
    partner = jnp.where(
        lower, pltpu.roll(block, LANES - half, 1), pltpu.roll(block, half, 1)
    )
    return block * cosine + partner * sine


def hint(flops, transcendentals, bytes_accessed, share=256):
    return pl.CostEstimate(
        flops=flops // share, transcendentals=transcendentals // share,
        bytes_accessed=bytes_accessed // share,
    )


def tile_ds(index, width):
    return pl.ds(pl.multiple_of(index * width, width), width)


def head_pair(block, place):
    lower = lane_iota(block.shape) < HEAD_SIZE
    moved = pltpu.roll(block, HEAD_SIZE, 1)
    zero = jnp.zeros_like(block)
    low, high = (block, moved) if place == 0 else (moved, block)
    return jnp.where(lower, low, zero), jnp.where(lower, zero, high)


def attention_forward_kernel(
    x_ref, w_ref, gain_one_ref, gain_two_ref, id_row_ref, id_col_ref, cos_ref, sin_ref, picks_ref,
    q_ref, k_ref, v_ref, att_ref, lse_ref, res_ref, pay_ref, gate_ref,
    normed_ref, bias_ref,
    *, q_width, kv_width, experts,
):
    rows, width = x_ref.shape
    x = x_ref[...].astype(F32)
    scale = lax.rsqrt(jnp.mean(x * x, axis=1, keepdims=True) + EPS)
    normed_ref[...] = (x * scale * gain_one_ref[...]).astype(BF)
    bias_ref[...] = jnp.where(id_col_ref[...] <= id_row_ref[...], 0.0, NEG_FILL)
    step = 256

    def project(out_ref, start, count, rotate):
        def body(j, carry):
            cols = pl.ds(pl.multiple_of(start + j * step, step), step)
            part = mm(normed_ref[...], w_ref[:, cols])
            if rotate:
                part = jnp.concatenate(
                    [
                        turn(part[:, i * LANES : (i + 1) * LANES], cos_ref[...], sin_ref[...])
                        for i in range(step // LANES)
                    ],
                    axis=1,
                )
            out_ref[:, tile_ds(j, step)] = part.astype(BF)
            return carry

        lax.fori_loop(0, count // step, body, 0)

    project(q_ref, 0, q_width, True)
    project(k_ref, q_width, kv_width, True)
    project(v_ref, q_width + kv_width, kv_width, False)

    def pair_body(j, carry):
        k_block = k_ref[:, tile_ds(j, LANES)].astype(F32)
        v_block = v_ref[:, tile_ds(j, LANES)].astype(F32)
        for place in range(2):
            keys = head_pair(k_block, place)
            vals = head_pair(v_block, place)
            group = 2 * j + place
            q_block = q_ref[:, tile_ds(group, LANES)]
            out = None
            for side in range(2):
                scores = mm_nt(keys[side].astype(BF), q_block) * SCORE_SCALE + bias_ref[...]
                highest = jnp.max(scores, axis=0, keepdims=True)
                lifted = jnp.exp(scores - highest)
                total = jnp.sum(lifted, axis=0, keepdims=True)
                low = (lifted * (1.0 / total)).astype(BF)
                lse_ref[pl.ds(2 * group + side, 1), :] = highest + jnp.log(total)
                part = mm_tn(vals[side].astype(BF), low)
                out = part if out is None else out + part
            att_ref[:, tile_ds(group, LANES)] = out.T.astype(BF)
        return carry

    lax.fori_loop(0, KEY_VALUE_HEADS // 2, pair_body, 0)

    start = q_width + 2 * kv_width

    def out_body(j, total):
        cols = pl.ds(pl.multiple_of(start + j * step, step), step)
        here = tile_ds(j, step)
        value = x_ref[:, here].astype(F32) + RESIDUAL_SCALE * mm(att_ref[...], w_ref[:, cols])
        res_ref[:, here] = value
        return total + jnp.sum(value * value, axis=1, keepdims=True)

    square = lax.fori_loop(0, width // step, out_body, jnp.zeros((rows, 1), F32))
    scale = lax.rsqrt(square * (1.0 / width) + EPS)
    pay_ref[:rows, :] = (res_ref[...] * scale * gain_two_ref[...]).astype(BF)
    logits = mm(pay_ref[:rows, :], w_ref[:, start + width :])
    lanes = lane_iota(logits.shape)
    chosen = lanes < 0
    for k in range(picks_ref.shape[1]):
        chosen = chosen | (picks_ref[:, k : k + 1] == lanes)
    masked = jnp.where(chosen, logits, NEG_FILL)
    lifted = jnp.where(chosen, jnp.exp(masked - jnp.max(masked, axis=1, keepdims=True)), 0.0)
    gates = lifted / jnp.sum(lifted, axis=1, keepdims=True)
    across = gates.T[:experts, :]
    gate_ref[...] = across
    high = across.astype(BF)
    pay_ref[rows:, :rows] = high
    pay_ref[rows:, rows:] = (across - high.astype(F32)).astype(BF)


def attention_forward(x, pack, gain_one, gain_two, ids, picks, tables, q_width, kv_width, experts):
    rows, width = x.shape
    out_shape = (
        jax.ShapeDtypeStruct((rows, q_width), BF),
        jax.ShapeDtypeStruct((rows, kv_width), BF),
        jax.ShapeDtypeStruct((rows, kv_width), BF),
        jax.ShapeDtypeStruct((rows, q_width), BF),
        jax.ShapeDtypeStruct((QUERY_HEADS, rows), F32),
        jax.ShapeDtypeStruct((rows, width), F32),
        jax.ShapeDtypeStruct((rows + experts, width), BF),
        jax.ShapeDtypeStruct((experts, rows), F32),
    )
    flops = 2 * rows * width * (q_width + 2 * kv_width + width) + 8 * QUERY_HEADS * rows * rows * 128
    return pl.pallas_call(
        functools.partial(
            attention_forward_kernel, q_width=q_width, kv_width=kv_width, experts=experts
        ),
        out_shape=out_shape,
        scratch_shapes=[pltpu.VMEM((rows, width), BF), pltpu.VMEM((rows, rows), F32)],
        compiler_params=pltpu.CompilerParams(vmem_limit_bytes=VMEM_LIMIT),
        cost_estimate=hint(
            flops=flops, transcendentals=QUERY_HEADS * rows * rows, bytes_accessed=64 << 20, share=1
        ),
        name="attention_forward",
    )(x, pack, gain_one, gain_two, ids[None, :], ids[:, None], *tables, picks)


def slot_marks(sel_ref, gate_rows, upper_ref, local):
    picked = mm(sel_ref[...], gate_rows)
    rows = picked.shape[1] // 2
    gates = picked[:, :rows] + picked[:, rows:]
    used = gates != 0.0
    rank = mm(used.astype(F32).astype(BF), upper_ref[...])
    slots = jnp.where(used, rank, -1.0)
    places = lax.broadcasted_iota(jnp.int32, (CAP, rows), 0).astype(F32)
    hits = [places == slots[e : e + 1, :] for e in range(local)]
    return gates, hits


def fill_upper(upper_ref):
    rows = upper_ref.shape[0]
    upper = lax.broadcasted_iota(jnp.int32, (rows, rows), 0) < lane_iota((rows, rows))
    upper_ref[...] = jnp.where(upper, 1.0, 0.0).astype(BF)


def dispatch_kernel(sel_ref, pay_ref, grad_ref, *refs, local):
    rows_ref, slot_ref, upper_ref = refs[-3:]

    @pl.when(pl.program_id(0) == 0)
    def _():
        fill_upper(upper_ref)

    rows = grad_ref.shape[1]
    gates, hits = slot_marks(sel_ref, pay_ref[0, rows:, :], upper_ref, local)
    marks = jnp.concatenate([jnp.where(h, 1.0, 0.0).astype(BF) for h in hits], axis=0)
    column = jnp.concatenate(
        [
            jnp.sum(jnp.where(h, gates[e : e + 1, :], 0.0), axis=1, keepdims=True)
            for e, h in enumerate(hits)
        ],
        axis=0,
    )
    moved = mm(marks, pay_ref[0, :rows, :]).astype(BF)
    grads = (column * (RESIDUAL_SCALE * mm(marks, grad_ref[0]))).astype(BF)
    for e in range(local):
        rows_ref[e, 0, 0] = moved[e * CAP : (e + 1) * CAP]
        slot_ref[e, 0, 0] = grads[e * CAP : (e + 1) * CAP]


def dispatch(sel, pays, grads, place, places, local, carried):
    count, rows, width = grads.shape
    shape = jax.ShapeDtypeStruct((local, places, count, CAP, width), BF)
    out_spec = pl.BlockSpec((local, 1, 1, CAP, width), lambda s: (0, place, s, 0, 0))
    in_specs = [
        pl.BlockSpec(sel.shape, lambda s: (0, 0)),
        pl.BlockSpec((1,) + pays.shape[1:], lambda s: (s, 0, 0)),
        pl.BlockSpec((1, rows, width), lambda s: (s, 0, 0)),
    ]
    operands = [sel, pays, grads]
    aliases = {}
    if carried is not None:
        operands += list(carried)
        in_specs += [pl.BlockSpec(memory_space=pl.ANY)] * 2
        aliases = {3: 0, 4: 1}
    return pl.pallas_call(
        functools.partial(dispatch_kernel, local=local),
        out_shape=(shape, shape),
        grid=(count,),
        in_specs=in_specs,
        out_specs=(out_spec, out_spec),
        scratch_shapes=[pltpu.VMEM((rows, rows), BF)],
        input_output_aliases=aliases,
        compiler_params=pltpu.CompilerParams(vmem_limit_bytes=VMEM_LIMIT),
        cost_estimate=hint(
            flops=4 * count * local * CAP * rows * width, transcendentals=0, bytes_accessed=20 << 20
        ),
        name="dispatch",
    )(*operands)


def expert_kernel(x_ref, s_ref, w_ref, *refs, chunk, tile, last, carried):
    if carried:
        prior_ref, refs = refs[0], refs[1:]
    (
        pr_ref, dg_ref, dot_ref, grad_ref,
        gate_ref, up_ref, down_ref, act_ref, both_ref, acc_in_ref, acc_down_ref,
    ) = refs
    rows, width = x_ref.shape[-2:]
    hidden = gate_ref.shape[-1]
    owners = grad_ref.shape[0]
    in_rows, down_rows = width // owners, hidden // owners
    step = pl.program_id(1)
    pieces = width // hidden

    @pl.when(step == 0)
    def _():
        for o in range(owners):
            gate_ref[o * in_rows : (o + 1) * in_rows, :] = w_ref[o, 0, :in_rows, :]
            up_ref[o * in_rows : (o + 1) * in_rows, :] = w_ref[o, 0, in_rows : 2 * in_rows, :]
            for c in range(pieces):
                first = 2 * in_rows + c * down_rows
                down_ref[o * down_rows : (o + 1) * down_rows, c * hidden : (c + 1) * hidden] = w_ref[
                    o, 0, first : first + down_rows, :
                ]

    def chunk_body(c, carry):
        here = tile_ds(c, chunk)
        x = x_ref[0, here, :]
        s = s_ref[0, here, :]
        pre_gate = mm(x, gate_ref[...])
        pre_up = mm(x, up_ref[...])
        act_grad = mm_nt(s, down_ref[...])
        logistic = jax.nn.sigmoid(pre_gate)
        swish = pre_gate * logistic
        act = (swish * pre_up).astype(BF)
        gate_in = (
            act_grad * pre_up * logistic * (1.0 + pre_gate * (1.0 - logistic))
        ).astype(BF)
        up_in = (act_grad * swish).astype(BF)
        dot_ref[0, here, :] = jnp.sum(act.astype(F32) * act_grad, axis=1, keepdims=True)
        act_ref[here, :] = act
        both_ref[here, :hidden] = gate_in
        both_ref[here, hidden:] = up_in
        pr_ref[0, here, :] = mm(act, down_ref[...]).astype(BF)
        dg_ref[0, here, :] = (mm_nt(gate_in, gate_ref[...]) + mm_nt(up_in, up_ref[...])).astype(BF)
        return carry

    lax.fori_loop(0, rows // chunk, chunk_body, 0)

    def put(owner, first, value):
        count = value.shape[0]
        if carried:
            value = value + prior_ref[owner, 0, first : first + count, :].astype(F32)
        grad_ref[owner, 0, first : first + count, :] = value.astype(BF)

    def accumulate(acc_ref, here, part, emit):
        if last == 0:
            emit(part)
            return

        @pl.when(step == 0)
        def _():
            acc_ref[here, :] = part

        if last > 1:

            @pl.when((step > 0) & (step < last))
            def _():
                acc_ref[here, :] = acc_ref[here, :] + part

        @pl.when(step == last)
        def _():
            emit(acc_ref[here, :] + part)

    def in_body(t, carry):
        here = tile_ds(t, tile)

        def emit(total):
            for i in range(tile // in_rows):
                piece = total[i * in_rows : (i + 1) * in_rows]
                owner = t * (tile // in_rows) + i
                put(owner, 0, piece[:, :hidden])
                put(owner, in_rows, piece[:, hidden:])

        accumulate(acc_in_ref, here, mm_tn(x_ref[0, :, here], both_ref[...]), emit)
        return carry

    lax.fori_loop(0, width // tile, in_body, 0)

    def down_body(t, carry):
        here = tile_ds(t, tile)

        def emit(total):
            for i in range(tile // down_rows):
                piece = total[i * down_rows : (i + 1) * down_rows]
                owner = t * (tile // down_rows) + i
                for c in range(pieces):
                    put(owner, 2 * in_rows + c * down_rows, piece[:, c * hidden : (c + 1) * hidden])

        accumulate(acc_down_ref, here, mm_tn(act_ref[:, here], s_ref[0]), emit)
        return carry

    lax.fori_loop(0, hidden // tile, down_body, 0)


def experts_step(first, weights, rows_in, slot_grad, prior):
    owners, count, packed, hidden = weights.shape
    _, total, width = rows_in.shape
    rows = 8 * CAP
    steps = total // rows
    out_shape = (
        jax.ShapeDtypeStruct((count, total, width), BF),
        jax.ShapeDtypeStruct((count, total, width), BF),
        jax.ShapeDtypeStruct((count, total, 1), F32),
        jax.ShapeDtypeStruct(weights.shape, BF),
    )
    in_spec = pl.BlockSpec((1, rows, width), lambda e, t: (first + e, t, 0))
    pack_spec = pl.BlockSpec((owners, 1, packed, hidden), lambda e, t: (0, e, 0, 0))
    row_spec = lambda last: pl.BlockSpec((1, rows, last), lambda e, t: (e, t, 0))
    operands = [rows_in, slot_grad, weights]
    in_specs = [in_spec, in_spec, pack_spec]
    if prior is not None:
        operands.append(prior)
        in_specs.append(pack_spec)
    kept = 0 if steps == 1 else 1
    return pl.pallas_call(
        functools.partial(
            expert_kernel, chunk=rows // 3, tile=256, last=steps - 1, carried=prior is not None
        ),
        out_shape=out_shape,
        grid=(count, steps),
        in_specs=in_specs,
        out_specs=(row_spec(width), row_spec(width), row_spec(1), pack_spec),
        scratch_shapes=[
            pltpu.VMEM((width, hidden), BF),
            pltpu.VMEM((width, hidden), BF),
            pltpu.VMEM((hidden, width), BF),
            pltpu.VMEM((rows, hidden), BF),
            pltpu.VMEM((rows, 2 * hidden), BF),
            pltpu.VMEM((width, 2 * hidden) if kept else (8, LANES), F32),
            pltpu.VMEM((hidden, width) if kept else (8, LANES), F32),
        ],
        compiler_params=pltpu.CompilerParams(vmem_limit_bytes=VMEM_LIMIT),
        cost_estimate=hint(
            flops=18 * count * total * width * hidden, transcendentals=count * total * hidden,
            bytes_accessed=30 << 20, share=256 if prior is None else 1,
        ),
        name="experts",
    )(*operands)


def combine_kernel(sel_ref, pay_ref, *refs, groups, local, received):
    produced, returned, dots = (refs[i * groups : (i + 1) * groups] for i in range(3))
    rest = refs[3 * groups :]
    if received:
        other_ref, rest = rest[0], rest[1:]
    out_refs, upper_ref = rest[:-1], rest[-1]
    each = local // groups

    @pl.when(pl.program_id(0) == 0)
    def _():
        fill_upper(upper_ref)

    rows = upper_ref.shape[0]
    gates, hits = slot_marks(sel_ref, pay_ref[0], upper_ref, local)
    weighted = jnp.concatenate(
        [jnp.where(h, gates[e : e + 1, :], 0.0).astype(BF) for e, h in enumerate(hits)], axis=0
    )
    plain = jnp.concatenate([jnp.where(h, 1.0, 0.0).astype(BF) for h in hits], axis=0)
    made = jnp.concatenate([r[e, 0] for r in produced for e in range(each)], axis=0)
    back = jnp.concatenate([r[e, 0] for r in returned for e in range(each)], axis=0)
    out = mm_tn(weighted, made)
    grads = mm_tn(plain, back)
    pad = jnp.zeros((8 - local, rows), F32)
    dot_rows = jnp.concatenate(
        [
            jnp.sum(jnp.where(h, dots[e // each][e % each, 0], 0.0), axis=0, keepdims=True)
            for e, h in enumerate(hits)
        ]
        + ([pad] if local < 8 else []),
        axis=0,
    )
    high = dot_rows.astype(BF)
    low = (dot_rows - high.astype(F32)).astype(BF)
    tail = jnp.concatenate([mm_tn(sel_ref[...], high), mm_tn(sel_ref[...], low)], axis=1)
    half = tail.shape[0] // 2
    first = jnp.concatenate([out, tail[:half]], axis=0)
    second = jnp.concatenate([tail[half:], grads], axis=0)
    if received:
        first = first + other_ref[0, : rows + half, :].astype(F32)
        second = second + other_ref[0, rows + half :, :].astype(F32)

        def put(index):
            out_refs[2 * index][...] = first.astype(BF)
            out_refs[2 * index + 1][...] = second.astype(BF)

        for index in range(len(out_refs) // 2):
            pl.when(pl.program_id(0) == index)(functools.partial(put, index))
    else:
        out_refs[0][0, : rows + half, :] = first.astype(BF)
        out_refs[0][0, rows + half :, :] = second.astype(BF)


def combine(sel, pays, produced, returned, dots, side, first, span, other):
    count, total_rows, width = pays.shape
    groups, each = len(produced), produced[0].shape[0]
    local = groups * each
    experts = sel.shape[1]
    rows = total_rows - experts
    pick = lambda last: pl.BlockSpec((each, 1, CAP, last), lambda s: (0, side * count + first + s, 0, 0))
    in_specs = [
        pl.BlockSpec(sel.shape, lambda s: (0, 0)),
        pl.BlockSpec((1, experts, width), lambda s: (first + s, rows // experts, 0)),
    ]
    in_specs += [pick(width)] * (2 * groups) + [pick(1)] * groups
    operands = [sel, pays, *produced, *returned, *dots]
    total = 2 * rows + experts
    out_spec = pl.BlockSpec((1, total, width), lambda s: (s, 0, 0))
    out_shape = (jax.ShapeDtypeStruct((span, total, width), BF),)
    out_specs = (out_spec,)
    if other is not None:
        operands.append(other)
        in_specs.append(out_spec)
        out_shape = (jax.ShapeDtypeStruct((total // 2, width), BF),) * (2 * span)
        out_specs = (pl.BlockSpec((total // 2, width), lambda s: (0, 0)),) * (2 * span)
    return pl.pallas_call(
        functools.partial(combine_kernel, groups=groups, local=local, received=other is not None),
        out_shape=out_shape,
        grid=(span,),
        in_specs=in_specs,
        out_specs=out_specs,
        scratch_shapes=[pltpu.VMEM((rows, rows), BF)],
        compiler_params=pltpu.CompilerParams(vmem_limit_bytes=VMEM_LIMIT),
        cost_estimate=hint(
            flops=4 * span * local * CAP * rows * width, transcendentals=0, bytes_accessed=20 << 20, share=1
        ),
        name="combine",
    )(*operands)


def attention_backward_kernel(
    *refs, terms, q_width, kv_width, experts, carried,
):
    (
        x_ref, w_ref, gain_one_ref, gain_two_ref, id_row_ref, id_col_ref, cos_ref, sin_ref,
        grad_ref, q_ref, k_ref, v_ref, att_ref, lse_ref, res_ref, pay_ref, gate_ref,
    ) = refs[:17]
    term_refs = refs[17 : 17 + 2 * terms]
    rest = refs[17 + 2 * terms :]
    if carried:
        prior_ref, rest = rest[0], rest[3:]
    out_ref, in_grad_ref, pack_ref, bias_ref, wide_ref, att_grad_ref, qkv_grad_ref, branch_ref, normed_ref = rest
    rows, width = x_ref.shape
    step = 256
    start = q_width + 2 * kv_width

    def put(row_slice, cols, value):
        if carried:
            value = value + prior_ref[row_slice, cols].astype(F32)
        pack_ref[row_slice, cols] = value.astype(BF)

    def gathered(which, low, high):
        total = term_refs[which][low:high, :].astype(F32)
        for ref in term_refs[2 + which :: 2]:
            total = total + ref[low:high, :].astype(F32)
        return total

    half = experts // 2
    residual = res_ref[...]
    out_ref[0] = (residual + RESIDUAL_SCALE * gathered(0, 0, rows)).astype(BF)
    tail = jnp.concatenate([gathered(0, rows, rows + half), gathered(1, 0, half)], axis=0)
    weighted = tail[:, :rows] + tail[:, rows:]
    chosen = weighted - gate_ref[...] * jnp.sum(weighted, axis=0, keepdims=True)
    chosen = jnp.concatenate([chosen, jnp.zeros((LANES - experts, rows), F32)], axis=0)
    logit_grad = chosen.T.astype(BF)
    moe_grad = gathered(1, half, half + rows) + mm_nt(logit_grad, w_ref[:, start + width :])
    last = mm_tn(pay_ref[:rows, :], logit_grad)
    scale = lax.rsqrt(jnp.mean(residual * residual, axis=1, keepdims=True) + EPS)
    gain_two_grad = jnp.sum(moe_grad * residual * scale, axis=0, keepdims=True)
    u = moe_grad * gain_two_ref[...]
    inner = jnp.sum(u * residual, axis=1, keepdims=True) * (1.0 / width)
    res_grad = grad_ref[...].astype(F32) + scale * u - residual * (scale * scale * scale * inner)
    in_grad_ref[0] = res_grad
    branch_ref[...] = (RESIDUAL_SCALE * res_grad).astype(BF)
    bias_ref[...] = jnp.where(id_col_ref[...] <= id_row_ref[...], 0.0, NEG_FILL)

    def branch_body(j, carry):
        here = tile_ds(j, step)
        att_grad_ref[:, here] = mm_nt(
            branch_ref[...], w_ref[here, start : start + width]
        ).astype(BF)
        part = mm_tn(att_ref[:, here], branch_ref[...])
        put(here, slice(start, start + width), part)
        return carry

    lax.fori_loop(0, q_width // step, branch_body, 0)

    lower = lane_iota((rows, LANES)) < HEAD_SIZE

    def pair_body(j, carry):
        k_block = k_ref[:, tile_ds(j, LANES)].astype(F32)
        v_block = v_ref[:, tile_ds(j, LANES)].astype(F32)
        k_sums, v_sums = [], []
        for place in range(2):
            keys = [h.astype(BF) for h in head_pair(k_block, place)]
            vals = [h.astype(BF) for h in head_pair(v_block, place)]
            group = 2 * j + place
            here = tile_ds(group, LANES)
            q_block = q_ref[:, here]
            g_block = att_grad_ref[:, here]
            q_out = None
            k_parts, v_parts = [], []
            for side in range(2):
                scores = mm_nt(keys[side], q_block) * SCORE_SCALE + bias_ref[...]
                probs = jnp.exp(scores - lse_ref[pl.ds(2 * group + side, 1), :])
                weight_grad = mm_nt(vals[side], g_block)
                v_parts.append(mm(probs.astype(BF), g_block))
                dots = jnp.sum(probs * weight_grad, axis=0, keepdims=True)
                score_grad = (probs * (weight_grad - dots)).astype(BF)
                k_parts.append(mm(score_grad, q_block))
                part = mm_tn(keys[side], score_grad)
                q_out = part if q_out is None else q_out + part
            q_turned = turn(q_out.T * SCORE_SCALE, cos_ref[...], -sin_ref[...])
            qkv_grad_ref[:, here] = q_turned.astype(BF)
            for parts, sums in ((k_parts, k_sums), (v_parts, v_sums)):
                mixed = jnp.where(lower, parts[0], parts[1])
                sums.append(mixed + pltpu.roll(mixed, HEAD_SIZE, 1))
        k_total = jnp.where(lower, k_sums[0], k_sums[1]) * SCORE_SCALE
        v_total = jnp.where(lower, v_sums[0], v_sums[1])
        k_here = pl.ds(pl.multiple_of(q_width + j * LANES, LANES), LANES)
        v_here = pl.ds(pl.multiple_of(q_width + kv_width + j * LANES, LANES), LANES)
        qkv_grad_ref[:, k_here] = turn(k_total, cos_ref[...], -sin_ref[...]).astype(BF)
        qkv_grad_ref[:, v_here] = v_total.astype(BF)
        return carry

    lax.fori_loop(0, KEY_VALUE_HEADS // 2, pair_body, 0)

    x = x_ref[...].astype(F32)
    scale = lax.rsqrt(jnp.mean(x * x, axis=1, keepdims=True) + EPS)
    normed_ref[...] = (x * scale * gain_one_ref[...]).astype(BF)

    def norm_body(j, carry):
        here = tile_ds(j, step)
        grad = mm_nt(qkv_grad_ref[...], w_ref[here, :start])
        put(here, slice(0, start), mm_tn(normed_ref[:, here], qkv_grad_ref[...]))
        wide_ref[:, here] = grad
        return carry

    lax.fori_loop(0, width // step, norm_body, 0)
    normed_grad = wide_ref[...]
    gain_one_grad = jnp.sum(normed_grad * x * scale, axis=0, keepdims=True)
    u = normed_grad * gain_one_ref[...]
    inner = jnp.sum(u * x, axis=1, keepdims=True) * (1.0 / width)
    in_grad_ref[0] = in_grad_ref[0] + scale * u - x * (scale * scale * scale * inner)
    lanes = lane_iota((width, LANES))
    one = jnp.broadcast_to(gain_one_grad, (LANES, width)).T
    two = jnp.broadcast_to(gain_two_grad, (LANES, width)).T
    last = jnp.where(lanes == experts, one, last)
    last = jnp.where(lanes == experts + 1, two, last)
    put(slice(0, width), slice(start + width, start + width + LANES), last)


def attention_backward(
    index, micro, x, pack, gain_one, gain_two, ids, tables, grad, saved, terms, prior, made, q_width, kv_width,
    experts,
):
    rows, width = x.shape
    operands = [x, pack, gain_one, gain_two, ids[None, :], ids[:, None], *tables, grad, *saved, *terms]
    whole = pl.BlockSpec(memory_space=pltpu.VMEM)
    in_specs = [whole] * len(operands)
    aliases = {}
    if prior is not None:
        operands += [prior, *made]
        in_specs += [whole] + [pl.BlockSpec(memory_space=pl.ANY)] * 2
        aliases = {len(operands) - 2: 0, len(operands) - 1: 1}
    row_spec = pl.BlockSpec((1, rows, width), lambda i: (index, 0, 0))
    flops = 4 * rows * width * (q_width + 2 * kv_width + width) + 20 * QUERY_HEADS * rows * rows * 128
    return pl.pallas_call(
        functools.partial(
            attention_backward_kernel, terms=len(terms) // 2, q_width=q_width, kv_width=kv_width,
            experts=experts, carried=prior is not None,
        ),
        out_shape=(
            jax.ShapeDtypeStruct((micro, rows, width), BF),
            jax.ShapeDtypeStruct((micro, rows, width), F32),
            jax.ShapeDtypeStruct(pack.shape, BF),
        ),
        grid=(1,),
        in_specs=in_specs,
        out_specs=(row_spec, row_spec, whole),
        input_output_aliases=aliases,
        scratch_shapes=[
            pltpu.VMEM((rows, rows), F32),
            pltpu.VMEM((rows, width), F32),
            pltpu.VMEM((rows, q_width), BF),
            pltpu.VMEM((rows, q_width + 2 * kv_width), BF),
            pltpu.VMEM((rows, width), BF),
            pltpu.VMEM((rows, width), BF),
        ],
        compiler_params=pltpu.CompilerParams(vmem_limit_bytes=VMEM_LIMIT),
        cost_estimate=hint(
            flops=flops, transcendentals=QUERY_HEADS * rows * rows, bytes_accessed=40 << 20, share=1
        ),
        name="attention_backward",
    )(*operands)


def peer_chip(chip, distance):
    total = 0
    for bit in (1, 2, 4):
        total = total + bit * ((chip // bit + (distance // bit) % 2) % 2)
    return total


def where_am_i():
    f, d = lax.axis_index("fsdp"), lax.axis_index("dp")
    return f // 2, f % 2, d


def meet(peers):
    barrier = pltpu.get_barrier_semaphore()
    for peer in peers:
        pl.semaphore_signal(
            barrier, inc=1, device_id=peer, device_id_type=pl.DeviceIdType.MESH
        )
    pl.semaphore_wait(barrier, len(peers))


def push(src, dst, send, receive, peer):
    copy = pltpu.make_async_remote_copy(
        src_ref=src, dst_ref=dst, send_sem=send, recv_sem=receive, device_id=peer,
        device_id_type=pl.DeviceIdType.MESH,
    )
    copy.start()
    return copy


def gather_layer_kernel(
    w_ref, out_ref, own_sem, z_send, z_receive, x_send, x_receive, s_send, s_receive, *, chips, depth
):
    chip, core, d = where_am_i()
    rows = w_ref.shape[0]
    others = [peer_chip(chip, r) for r in range(1, chips)]
    f, sibling = chip * 2 + core, chip * 2 + 1 - core

    def block(owner, layer):
        first = pl.multiple_of((owner * depth + layer) * rows, rows)
        return out_ref.at[pl.ds(first, rows), :]

    peers = [(f, (d + i) % depth) for i in range(1, depth)]
    peers += [(c * 2 + core, d) for c in others] + [(sibling, d)]
    meet(peers)
    own = pltpu.make_async_copy(w_ref, block(f, d), own_sem)
    own.start()
    z_copies = [
        push(w_ref, block(f, d), z_send.at[i - 1], z_receive.at[i - 1], (f, (d + i) % depth))
        for i in range(1, depth)
    ]
    x_copies, s_copies = [], []
    layers = [(d + depth - i) % depth for i in range(depth)]
    for i, layer in enumerate(layers):
        if i:
            z_copies[i - 1].wait_recv()
        src = block(f, layer) if i else w_ref
        for r, c in enumerate(others):
            x_copies.append(
                push(src, block(f, layer), x_send.at[i, r], x_receive.at[i, r], (c * 2 + core, d))
            )
        s_copies.append(
            push(src, block(f, layer), s_send.at[i, 0], s_receive.at[i, 0], (sibling, d))
        )
    for i, layer in enumerate(layers):
        for r, c in enumerate(others):
            x_copies[i * (chips - 1) + r].wait_recv()
            there = block(c * 2 + core, layer)
            s_copies.append(
                push(there, there, s_send.at[i, r + 1], s_receive.at[i, r + 1], (sibling, d))
            )
    own.wait()
    for copy in z_copies + x_copies:
        copy.wait_send()
    for copy in s_copies:
        copy.wait()


def gather_layer(pack, chips, depth):
    dma = pltpu.SemaphoreType.DMA
    rows, width = pack.shape
    return pl.pallas_call(
        functools.partial(gather_layer_kernel, chips=chips, depth=depth),
        out_shape=jax.ShapeDtypeStruct((rows * 2 * chips * depth, width), pack.dtype),
        in_specs=[pl.BlockSpec(memory_space=pl.ANY)],
        out_specs=pl.BlockSpec(memory_space=pl.ANY),
        scratch_shapes=[
            dma(()), dma((depth - 1,)), dma((depth - 1,)), dma((depth, chips - 1)),
            dma((depth, chips - 1)), dma((depth, chips)), dma((depth, chips)),
        ],
        compiler_params=pltpu.CompilerParams(collective_id=1, has_side_effects=True),
        name="gather_layer",
    )(pack)


def reduce_layer_kernel(
    pack_ref, out_ref, s_buf, s_sum, x_buf, x_sum, z_buf,
    s_send, s_receive, x_send, x_receive, z_send, z_receive,
    *, chips, depth, parts,
):
    chip, core, d = where_am_i()
    total, width = pack_ref.shape
    rows = total // (2 * chips * depth)
    span = rows * depth
    step = width // parts
    distances = list(range(1, chips))
    others = [peer_chip(chip, r) for r in distances]
    f, sibling = chip * 2 + core, chip * 2 + 1 - core
    peers = [(f, (d + i) % depth) for i in range(1, depth)]
    peers += [(c * 2 + core, d) for c in others] + [(sibling, d)]
    meet(peers)

    def band(p):
        return slice(p * step, (p + 1) * step)

    def mine(c, k):
        return pl.ds(pl.multiple_of((c * 2 + k) * span, span), span)

    order = [(r, c) for r, c in zip(distances, others)][::-1] + [(0, chip)]
    s_copies = {}
    for p in range(parts):
        for r, c in order:
            s_copies[p, r] = push(
                pack_ref.at[mine(c, 1 - core), band(p)], s_buf.at[r, :, band(p)],
                s_send.at[p, r], s_receive.at[p, r], (sibling, d),
            )
    x_copies, z_copies = {}, {}

    def sum_chip(p):
        for r, c in order:
            s_copies[p, r].wait_recv()
            value = pack_ref[mine(c, core), band(p)].astype(F32) + s_buf[r, :, band(p)].astype(F32)
            s_sum[r, :, band(p)] = value.astype(s_sum.dtype)

    def send_chip(p):
        for r, c in order[:-1]:
            x_copies[p, r] = push(
                s_sum.at[r, :, band(p)], x_buf.at[r - 1, :, band(p)], x_send.at[p, r - 1],
                x_receive.at[p, r - 1], (c * 2 + core, d),
            )

    def sum_plane(p):
        value = s_sum[0, :, band(p)].astype(F32)
        for r in distances:
            x_copies[p, r].wait_recv()
            value = value + x_buf[r - 1, :, band(p)].astype(F32)
        x_sum[:, :, band(p)] = value.reshape(depth, rows, step).astype(x_sum.dtype)

    def send_plane(p):
        for i in range(1, depth):
            to = (d + i) % depth
            z_copies[p, i] = push(
                x_sum.at[to, :, band(p)], z_buf.at[i - 1, :, band(p)], z_send.at[p, i - 1],
                z_receive.at[p, i - 1], (f, to),
            )

    def finish(p):
        value = x_sum[d, :, band(p)].astype(F32)
        for i in range(1, depth):
            z_copies[p, i].wait_recv()
            value = value + z_buf[i - 1, :, band(p)].astype(F32)
        out_ref[:, band(p)] = value

    for p in range(parts + 1):
        if p < parts:
            sum_chip(p)
        if p > 0:
            send_chip(p - 1)
    for p in range(parts + 1):
        if p < parts:
            sum_plane(p)
        if p > 0:
            send_plane(p - 1)
    for p in range(parts):
        finish(p)
    for copy in [*s_copies.values(), *x_copies.values(), *z_copies.values()]:
        copy.wait_send()


def reduce_layer(pack, chips, depth, parts):
    dma = pltpu.SemaphoreType.DMA
    total, width = pack.shape
    rows = total // (2 * chips * depth)
    kind = BF if rows % 16 == 0 else F32
    return pl.pallas_call(
        functools.partial(reduce_layer_kernel, chips=chips, depth=depth, parts=parts),
        out_shape=jax.ShapeDtypeStruct((rows, width), F32),
        in_specs=[pl.BlockSpec(memory_space=pltpu.VMEM)],
        out_specs=pl.BlockSpec(memory_space=pltpu.VMEM),
        scratch_shapes=[
            pltpu.VMEM((chips, rows * depth, width), BF),
            pltpu.VMEM((chips, rows * depth, width), BF),
            pltpu.VMEM((chips - 1, rows * depth, width), BF),
            pltpu.VMEM((depth, rows, width), kind),
            pltpu.VMEM((depth - 1, rows, width), kind),
            dma((parts, chips)), dma((parts, chips)), dma((parts, chips - 1)), dma((parts, chips - 1)),
            dma((parts, depth - 1)), dma((parts, depth - 1)),
        ],
        compiler_params=pltpu.CompilerParams(
            collective_id=2, has_side_effects=True, vmem_limit_bytes=VMEM_LIMIT
        ),
        cost_estimate=pl.CostEstimate(flops=0, transcendentals=0, bytes_accessed=1 << 30),
        name="reduce_layer",
    )(pack)


def swap(value, distance, size):
    return lax.ppermute(value, "fsdp", [(i, i ^ distance) for i in range(size)])


def after(value, *earlier):
    return lax.optimization_barrier((value, *earlier))[0] if earlier else value


def send_near(value, size):
    return swap(value, 2, size), swap(value, 4, size)


def gather_chips(value, near, size):
    chips = size // 2
    if near is None:
        return [value] + [swap(value, 2 * r, size) for r in range(1, chips)]
    half = value.shape[0] // 2
    one, two = near
    return [value, one, two, swap(one[:half], 4, size), swap(two[half:], 2, size)]


def both_cores(pieces, size, *earlier):
    if earlier:
        pieces = [pieces[0]] + [after(p, *earlier) for p in pieces[1:]]
    chips = size // 2
    last = pieces[chips - 1 :]
    mine = jnp.stack(pieces[: chips - 1] + [jnp.concatenate(last) if last[1:] else last[0]])
    return mine, swap(mine, 1, size)


def scatter_near(kept, size, *earlier):
    chips = size // 2
    if chips != 4:
        return [swap(kept[2 * r + h], 2 * r, size) for r in range(1, chips) for h in range(2)]
    return [swap(after(kept[6], *earlier), 2, size), swap(after(kept[7], *earlier), 4, size)]


def scatter_far(kept, near, size, *earlier, rest=()):
    if size != 8:
        return (), ()
    add = lambda a, b: (a.astype(F32) + b.astype(F32)).astype(BF)
    by_one, by_two = after(near[0], *earlier, *rest[1:]), after(near[1], *earlier, *rest[:1])
    one_sum, two_sum = add(kept[3], by_two), add(kept[4], by_one)
    return (one_sum, two_sum), (swap(one_sum, 2, size), swap(two_sum, 4, size))


def scatter_rest(kept, size, *earlier):
    if size != 8:
        return ()
    return swap(after(kept[2], *earlier), 2, size), swap(after(kept[5], *earlier), 4, size)


def scattered(kept, near, far, rest):
    if not far:
        return [kept[0], kept[1]] + near
    return [kept[0], kept[1], rest[0], far[0], far[1], rest[1]]


def local(
    inputs, block_ids, routes, out_grad, norm_gain, w_query, key_weight, value_weight, w_output,
    moe_gain, w_router, w_gate, w_up, w_down,
):
    micro, _, rows, width = inputs.shape
    experts = w_router.shape[1]
    held, in_rows, hidden = w_gate.shape
    down_rows = w_down.shape[1]
    q_width, kv_width = w_query.shape[1], key_weight.shape[1]
    owners = lax.axis_size("fsdp")
    depth = lax.axis_size("dp")
    chips = owners // 2
    tables = tuple(jnp.asarray(t) for t in rope_tables(rows))
    start = q_width + 2 * kv_width + width
    group = max(1, held // 2)
    cuts = width // hidden

    split_down = w_down.reshape(held, down_rows, cuts, hidden).transpose(0, 2, 1, 3)
    packed = jnp.concatenate(
        [w_gate, w_up, split_down.reshape(held, cuts * down_rows, hidden)], axis=1
    )
    weights = [
        lax.all_gather(packed[g : g + group], "dp", axis=0, tiled=False)
        for g in range(0, held, group)
    ]
    pieces = [
        w_query, key_weight, value_weight, w_output, w_router, norm_gain[:, None], moe_gain[:, None]
    ]
    filled = sum(p.shape[1] for p in pieces)
    pieces.append(jnp.zeros((w_query.shape[0], start + LANES - filled), BF))
    pack = gather_layer(jnp.concatenate(pieces, axis=1), chips, depth)
    gain_one = pack[:, start + experts].astype(F32)[None, :]
    gain_two = pack[:, start + experts + 1].astype(F32)[None, :]
    first = lax.axis_index("fsdp") * held
    places = jnp.arange(8)[:, None]
    sel = ((jnp.arange(experts)[None, :] == first + places) & (places < held)).astype(BF)
    square = chips == 4

    def forward(m, x):
        return attention_forward(
            x, pack, gain_one, gain_two, block_ids[m, 0], routes[m, 0], tables, q_width, kv_width, experts
        )

    def dispatched(pay, grad, carried):
        side = 0 if carried is None else 1
        return dispatch(sel, pay[side], grad[side], side, 2, held, carried)

    def flat(carried):
        return [c.reshape(held, 2 * chips * CAP, width) for c in carried]

    saved, arrived, pays, moved, done, terms = [], [], [], [], {}, []
    ready = (pack,)
    for m in range(micro):
        grad = after(out_grad[m, 0], *ready)
        grad_near = None
        if square and m:
            grad_near = tuple(after(near, first_half[0]) for near in send_near(grad, owners))
        found_grad = gather_chips(grad, grad_near, owners)
        if m == 0:
            saved.append(forward(0, inputs[0, 0]))
            for n in range(1, micro):
                saved.append(forward(n, after(inputs[n, 0], saved[n - 1][4], *found_grad[1:])))
        pay = after(saved[m][6], *ready, *(grad_near or ()))
        pay_near = None
        if square and m == 0:
            one, two = send_near(pay, owners)
            pay_near = after(one, saved[-1][4]), after(two, saved[-1][4])
        found_pay = gather_chips(pay, pay_near, owners)
        ready = tuple(found_pay[chips - 1 :])
        arrived.append((found_pay, found_grad, grad_near))
        if m == 0:
            first_grad = both_cores(found_grad, owners)
            pays.append(both_cores(found_pay, owners, first_grad[0]))
            first_half = dispatched(pays[0], first_grad, None)

    def expert_part(m, g, *earlier):
        prior = done[m - 1, g][3] if m else None
        rows_in, slot_grad = moved[m]
        if earlier:
            rows_in = after(rows_in, *earlier)
        done[m, g] = experts_step(g * group, weights[g], rows_in, slot_grad, prior)

    def returned(m, earlier):
        parts = [
            [done[m, g][i].reshape(group, 2 * chips, CAP, -1) for g in range(len(weights))]
            for i in range(3)
        ]
        kept, before = [], ()
        sent = {}
        span = chips // 2
        for first in (span, 0):
            (sent[first],) = combine(sel, after(pays[m][1], *before), *parts, 1, first, span, None)
            before = (sent[first], *earlier)
        for first in (span, 0):
            found = combine(
                sel, after(pays[m][0], *before), *parts, 0, first, span, swap(sent[first], 1, owners)
            )
            before = (found[0],)
            kept = list(found) + kept
        return kept

    def backward(m, found, made, prior):
        out, in_grad, prior = attention_backward(
            m, micro, inputs[m, 0], pack, gain_one, gain_two, block_ids[m, 0], tables, out_grad[m, 0],
            saved[m], found, prior, made, q_width, kv_width, experts,
        )
        return (out, in_grad), prior

    added, far, rest = (), (), ()
    for m in range(micro):
        if m == 0:
            moved.append(flat(dispatched(pays[0], first_grad, first_half)))
            hold = arrived[1][2] if micro > 1 and square else ()
            expert_part(0, 0, *hold)
        else:
            found_grad = both_cores(arrived[m][1], owners, done[m - 1, 0][2])
            pays.append(both_cores(arrived[m][0], owners, found_grad[0]))
            half = dispatched(pays[m], found_grad, None)
            for g in range(1, len(weights)):
                expert_part(m - 1, g, half[0])
            kept = returned(m - 1, (*far, *rest))
            other = after(pays[m][1], kept[0], kept[-1])
            moved.append(flat(dispatched((None, other), found_grad, half)))
            near = scatter_near(kept, owners)
            expert_part(m, 0, kept[0], kept[-1])
            added, far = scatter_far(kept, near, owners, done[m, 0][2])
            rest = scatter_rest(kept, owners, *near)
            terms.append(scattered(kept, near, far, rest))
    for g in range(1, len(weights)):
        expert_part(micro - 1, g, *added)
    kept = returned(micro - 1, (*far, *rest))
    near = scatter_near(kept, owners)
    last_rest = scatter_rest(kept, owners)
    made, prior, held_back = None, None, ()
    for m in range(micro - 1):
        made, prior = backward(m, [after(terms[m][0], kept[0], kept[-1])] + terms[m][1:], made, prior)
        held_back = (prior,)
    last_added, last_far = scatter_far(kept, near, owners, *held_back, rest=last_rest)
    terms.append(scattered(kept, near, last_far, last_rest))
    made, prior = backward(micro - 1, terms[-1], made, prior)
    sums = []
    for g in range(len(weights)):
        summed = after(done[micro - 1, g][3], *(last_added if g else added))
        sums.append(lax.psum_scatter(summed, "dp", scatter_dimension=0, tiled=True)[0])
    layer = reduce_layer(prior, chips, depth, 5)
    marks = np.cumsum([0, q_width, kv_width, kv_width, width, experts, 1, 1])
    cut = [layer[:, a:b] for a, b in zip(marks[:-1], marks[1:])]
    stacked = jnp.concatenate(sums, axis=0).astype(F32)
    grad_down = stacked[:, 2 * in_rows :].reshape(held, cuts, down_rows, hidden)
    grad_down = grad_down.transpose(0, 2, 1, 3).reshape(held, down_rows, width)
    return (
        made[0][:, None],
        made[1][:, None],
        cut[5][:, 0], cut[0], cut[1], cut[2], cut[3], cut[6][:, 0], cut[4],
        stacked[:, :in_rows], stacked[:, in_rows : 2 * in_rows], grad_down,
    )


def solution(mesh):
    rows = ("fsdp", "dp")
    split = lambda rank: P(None, rows, *([None] * (rank - 2)))
    flat = P(rows, None)
    expert_spec = P("fsdp", "dp", None)
    in_specs = (
        split(4), split(3), split(4), split(4), P(rows), flat, flat, flat, flat, P(rows), flat,
        expert_spec, expert_spec, expert_spec,
    )
    out_specs = (
        split(4), split(4), P(rows), flat, flat, flat, flat, P(rows), flat,
        expert_spec, expert_spec, expert_spec,
    )
    return jax.shard_map(local, mesh=mesh, in_specs=in_specs, out_specs=out_specs, check_vma=False)
```
